32 devices in a mesh: seq: 16 (over z, y, x), tp: 2 (over core).
Axes of the slice: x: 2, y: 2, z: 4, core: 2. Of those that a mesh axis runs over, the one named last changes fastest.
Arguments:
- inputs: bfloat16 [2, 2048, 2048], P(None, ('seq', 'tp')), may hold values from -6 to 6
- cotangent: bfloat16 [2, 2048, 2048], P(None, ('seq', 'tp')), may hold values from -6 to 6
- attn_gain: bfloat16 [2048], replicated, may hold values from 0.5 to 1.5
- query_matrix: bfloat16 [2048, 2048], P('seq', 'tp'), may hold values from -0.125 to 0.125
- key_matrix: bfloat16 [2048, 512], P('seq', 'tp'), may hold values from -0.125 to 0.125
- value_matrix: bfloat16 [2048, 512], P('seq', 'tp'), may hold values from -0.125 to 0.125
- output_matrix: bfloat16 [2048, 2048], P('seq', 'tp'), may hold values from -0.75 to 0.75
- query_first_factor: bfloat16 [2048, 8], replicated, may hold values from -0.125 to 0.125
- query_second_factor: bfloat16 [8, 2048], P(None, 'tp'), may hold values from -0.75 to 0.75
- key_first_factor: bfloat16 [2048, 8], replicated, may hold values from -0.125 to 0.125
- key_second_factor: bfloat16 [8, 512], P(None, 'tp'), may hold values from -0.75 to 0.75
- value_first_factor: bfloat16 [2048, 8], replicated, may hold values from -0.125 to 0.125
- value_second_factor: bfloat16 [8, 512], P(None, 'tp'), may hold values from -0.75 to 0.75
- output_first_factor: bfloat16 [2048, 8], P('tp'), may hold values from -0.75 to 0.75
- output_second_factor: bfloat16 [8, 2048], replicated, may hold values from -0.75 to 0.75
- query_feature: bfloat16 [32, 64, 64], P('tp'), may hold values from -1 to 1
- key_feature_layer: bfloat16 [8, 64, 64], P('tp'), may hold values from -1 to 1
- mlp_gain: bfloat16 [2048], replicated, may hold values from 0.5 to 1.5
- gate_weight: bfloat16 [2048, 8192], P('seq', 'tp'), may hold values from -0.125 to 0.125
- up_weight: bfloat16 [2048, 8192], P('seq', 'tp'), may hold values from -0.125 to 0.125
- down_weight: bfloat16 [2048, 8192], P('seq', 'tp'), may hold values from -0.0625 to 0.0625
Outputs:
- outputs: bfloat16 [2, 2048, 2048], P(None, ('seq', 'tp'))
- input_gradient: float32 [2, 2048, 2048], P(None, ('seq', 'tp'))
- attn_gain_gradient: float32 [2048], replicated
- query_weight_gradient: float32 [2048, 2048], P('seq', 'tp')
- key_weight_gradient: float32 [2048, 512], P('seq', 'tp')
- value_weight_gradient: float32 [2048, 512], P('seq', 'tp')
- out_weight_gradient: float32 [2048, 2048], P('seq', 'tp')
- query_shrink_gradient: float32 [2048, 8], replicated
- query_expand_gradient: float32 [8, 2048], replicated
- key_shrink_gradient: float32 [2048, 8], replicated
- key_expand_gradient: float32 [8, 512], replicated
- value_shrink_gradient: float32 [2048, 8], replicated
- value_expand_gradient: float32 [8, 512], replicated
- out_shrink_gradient: float32 [2048, 8], replicated
- out_expand_gradient: float32 [8, 2048], replicated
- query_feature_gradient: float32 [32, 64, 64], replicated
- key_feature_gradient: float32 [8, 64, 64], replicated
- mlp_gain_gradient: float32 [2048], replicated
- gate_weight_gradient: float32 [2048, 8192], P('seq', 'tp')
- up_weight_gradient: float32 [2048, 8192], P('seq', 'tp')
- down_weight_gradient: float32 [2048, 8192], P('seq', 'tp')
The draws below stay inside these ranges and needn't reach their ends.
All inputs are finite; a program needn't handle non-finite values.
Results may differ from the reference program's by a relative error of at most 0.015.
Values may be sent and summed in bfloat16 or wider, within the bound.
No kernel may reach another device: no remote copies, remote signals or barrier semaphores. Data moves between devices by JAX's collectives and lax.ppermute only.
A program may use at most 384 MiB of HBM per device.

```python
import math
import jax
import jax.numpy as jnp
from jax import lax

MODEL_WIDTH = 2048
QUERY_HEADS = 32
KEY_VALUE_HEADS = 8
HEAD_SIZE = 64
FF = 8192
FEATURE_COUNT = 128
ADAPTER_RANK = 8
WIN = 64
TOKEN_POSITIONS = 128
MB = 2
LMB = 2048


def level_of(key, extent, cuts, least, top_value):
    level = 1.0
    for dim, blocks in cuts:
        heights = jax.random.uniform(jax.random.fold_in(jax.random.fold_in(key, 6), dim), (blocks,), jnp.float32, least / len(cuts), top_value / len(cuts))
        level = level * jnp.repeat(jnp.exp(heights), extent[dim] // blocks).reshape((-1,) + (1,) * (len(extent) - 1 - dim))
    return level


def noise(rng, shape, scale, bound, cuts=(), kind=jnp.bfloat16):
    values = scale * jax.random.normal(rng, shape, jnp.float32)
    if cuts:
        values = values * level_of(rng, shape, cuts, -0.22, 0.18)
    return jnp.clip(values, -bound, bound).astype(kind)


def setup_inputs(seed: int = 0) -> dict:
    arg_keys = jax.random.split(jax.random.key(seed), 22)
    inputs = noise(arg_keys[0], (MB, LMB, MODEL_WIDTH), 1.0, 6.0, ((1, 32),))
    cotangent = noise(arg_keys[1], (MB, LMB, MODEL_WIDTH), 1.0, 6.0, ((1, 32),))
    attn_gain = jnp.clip(1.0 + 0.1 * jax.random.normal(arg_keys[2], (MODEL_WIDTH,), jnp.float32), 0.5, 1.5).astype(jnp.bfloat16)
    query_matrix = noise(arg_keys[3], (MODEL_WIDTH, QUERY_HEADS * HEAD_SIZE), MODEL_WIDTH ** -0.5, 0.125, ((0, 16), (1, 2)))
    key_matrix = noise(arg_keys[4], (MODEL_WIDTH, KEY_VALUE_HEADS * HEAD_SIZE), MODEL_WIDTH ** -0.5, 0.125, ((0, 16), (1, 2)))
    value_matrix = noise(arg_keys[5], (MODEL_WIDTH, KEY_VALUE_HEADS * HEAD_SIZE), MODEL_WIDTH ** -0.5, 0.125, ((0, 16), (1, 2)))
    output_matrix = noise(arg_keys[6], (MODEL_WIDTH, QUERY_HEADS * HEAD_SIZE), HEAD_SIZE ** -0.5, 0.75, ((0, 16), (1, 2)))
    query_first_factor = noise(arg_keys[7], (MODEL_WIDTH, ADAPTER_RANK), MODEL_WIDTH ** -0.5, 0.125)
    query_second_factor = noise(arg_keys[8], (ADAPTER_RANK, QUERY_HEADS * HEAD_SIZE), (8 * ADAPTER_RANK) ** -0.5, 0.75, ((1, 2),))
    key_first_factor = noise(arg_keys[9], (MODEL_WIDTH, ADAPTER_RANK), MODEL_WIDTH ** -0.5, 0.125)
    key_second_factor = noise(arg_keys[10], (ADAPTER_RANK, KEY_VALUE_HEADS * HEAD_SIZE), (8 * ADAPTER_RANK) ** -0.5, 0.75, ((1, 2),))
    value_first_factor = noise(arg_keys[11], (MODEL_WIDTH, ADAPTER_RANK), MODEL_WIDTH ** -0.5, 0.125)
    value_second_factor = noise(arg_keys[12], (ADAPTER_RANK, KEY_VALUE_HEADS * HEAD_SIZE), (8 * ADAPTER_RANK) ** -0.5, 0.75, ((1, 2),))
    output_first_factor = noise(arg_keys[13], (QUERY_HEADS * HEAD_SIZE, ADAPTER_RANK), HEAD_SIZE ** -0.5, 0.75, ((0, 2),))
    output_second_factor = noise(arg_keys[14], (ADAPTER_RANK, MODEL_WIDTH), (8 * ADAPTER_RANK) ** -0.5, 0.75)
    query_feature = noise(arg_keys[15], (QUERY_HEADS, HEAD_SIZE, HEAD_SIZE), (HEAD_SIZE // 2) ** -0.5, 1.0, ((0, 2),))
    key_feature_layer = noise(arg_keys[16], (KEY_VALUE_HEADS, HEAD_SIZE, HEAD_SIZE), (HEAD_SIZE // 2) ** -0.5, 1.0, ((0, 2),))
    mlp_gain = jnp.clip(1.0 + 0.1 * jax.random.normal(arg_keys[17], (MODEL_WIDTH,), jnp.float32), 0.5, 1.5).astype(jnp.bfloat16)
    gate_weight = noise(arg_keys[18], (MODEL_WIDTH, FF), MODEL_WIDTH ** -0.5, 0.125, ((0, 16), (1, 2)))
    up_weight = noise(arg_keys[19], (MODEL_WIDTH, FF), MODEL_WIDTH ** -0.5, 0.125, ((0, 16), (1, 2)))
    down_weight = noise(arg_keys[20], (MODEL_WIDTH, FF), FF ** -0.5, 0.0625, ((0, 16), (1, 2)))
    return dict(inputs=inputs, cotangent=cotangent, attn_gain=attn_gain, query_matrix=query_matrix, key_matrix=key_matrix, value_matrix=value_matrix, output_matrix=output_matrix, query_first_factor=query_first_factor, query_second_factor=query_second_factor, key_first_factor=key_first_factor, key_second_factor=key_second_factor, value_first_factor=value_first_factor, value_second_factor=value_second_factor, output_first_factor=output_first_factor, output_second_factor=output_second_factor, query_feature=query_feature, key_feature_layer=key_feature_layer, mlp_gain=mlp_gain, gate_weight=gate_weight, up_weight=up_weight, down_weight=down_weight)


EPS = 1e-05
ADAPTER_SCALE = 2.0
ROPE_BASE = 500000.0
HIGH = lax.Precision.HIGHEST

@jax.custom_vjp
def low_rank(v):
    return lax.optimization_barrier(v.astype(jnp.bfloat16)).astype(jnp.float32)

@jax.custom_vjp
def low_rank_back(v):
    return v

def low_keep(v):
    return (low_rank(v), None)

def low_pass(kept, grad):
    return (grad,)

def back_keep(v):
    return (v, None)

def back_low(kept, grad):
    return (low_rank(grad),)
low_rank.defvjp(low_keep, low_pass)
low_rank_back.defvjp(back_keep, back_low)

def matrix_product(left, right):
    return jnp.dot(left, right, precision=HIGH, preferred_element_type=jnp.float32)

def product(form, left, right):
    return jnp.einsum(form, left, right, precision=HIGH, preferred_element_type=jnp.float32)

def root_norm(value_rows, gain):
    return value_rows * lax.rsqrt(lax.optimization_barrier(jnp.mean(value_rows * value_rows, axis=-1, keepdims=True)) + EPS) * gain

def rotary_tables(positions, width):
    half = width // 2
    inverse = ROPE_BASE ** (-(jnp.arange(half, dtype=jnp.float32) * (2.0 / width)))
    angles = positions.astype(jnp.float32)[:, None] * inverse[None, :]
    return (jnp.cos(angles), jnp.sin(angles))

def apply_rotation(value_rows, cosine_table, sine_table):
    half = value_rows.shape[-1] // 2
    first = value_rows[..., :half]
    second = value_rows[..., half:]
    cosine_table = cosine_table[:, None, :]
    sine_table = sine_table[:, None, :]
    return jnp.concatenate([first * cosine_table - second * sine_table, second * cosine_table + first * sine_table], axis=-1)

def hedgehog(logits):
    return jnp.concatenate([jax.nn.softmax(logits, axis=-1), jax.nn.softmax(-logits, axis=-1)], axis=-1)

def attention_masks(rows, tail_valid):
    query_pos = lax.broadcasted_iota(jnp.int32, (rows, rows + WIN), 0)
    key_pos = lax.broadcasted_iota(jnp.int32, (rows, rows + WIN), 1)
    usable = jnp.logical_or(key_pos >= WIN, tail_valid)
    linear_mask = jnp.logical_and(key_pos <= query_pos, usable)
    window_mask = jnp.logical_and(jnp.logical_and(key_pos > query_pos, key_pos <= query_pos + WIN), usable)
    return (linear_mask[:, None, None, :], window_mask[:, None, None, :])

def windows(value_rows, blocks):
    blocked = value_rows.reshape((blocks, TOKEN_POSITIONS) + value_rows.shape[1:])
    tails = jnp.concatenate([jnp.zeros_like(blocked[:1, TOKEN_POSITIONS - WIN:]), blocked[:-1, TOKEN_POSITIONS - WIN:]], axis=0)
    return jnp.concatenate([tails, blocked], axis=1)

def exclusive(value_rows):
    return jnp.concatenate([jnp.zeros_like(value_rows[:1]), jnp.cumsum(value_rows, axis=0)[:-1]], axis=0)

def layer(inputs, attn_gain, query_matrix, key_matrix, value_matrix, output_matrix, query_first_factor, query_second_factor, key_first_factor, key_second_factor, value_first_factor, value_second_factor, output_first_factor, output_second_factor, query_feature, key_feature_layer, mlp_gain, gate_weight, up_weight, down_weight):
    total_sum = inputs.shape[0]
    blocks = total_sum // TOKEN_POSITIONS
    group_size = QUERY_HEADS // KEY_VALUE_HEADS
    normed_input = low_rank(root_norm(inputs, attn_gain))
    cosine_table, sine_table = rotary_tables(jnp.arange(total_sum, dtype=jnp.int32), HEAD_SIZE)
    key_unrotated = matrix_product(normed_input, key_matrix) + ADAPTER_SCALE * matrix_product(matrix_product(normed_input, key_first_factor), key_second_factor)
    key_rows = low_rank(apply_rotation(low_rank_back(key_unrotated).reshape(total_sum, KEY_VALUE_HEADS, HEAD_SIZE), cosine_table, sine_table))
    value_projected = matrix_product(normed_input, value_matrix) + ADAPTER_SCALE * matrix_product(matrix_product(normed_input, value_first_factor), value_second_factor)
    value_rows = low_rank_back(low_rank(value_projected)).reshape(total_sum, KEY_VALUE_HEADS, HEAD_SIZE)
    key_logits = low_rank_back(product('thd,hde->the', key_rows, key_feature_layer))
    key_features = low_rank(hedgehog(key_logits))
    keys_window = windows(key_rows, blocks)
    values_window = windows(value_rows, blocks)
    features_window = windows(key_features, blocks)
    block_ids = jnp.arange(blocks, dtype=jnp.int32)
    usable = jnp.logical_or(jnp.arange(TOKEN_POSITIONS)[None, :] >= WIN, block_ids[:, None] > 0).astype(jnp.float32)
    live = features_window[:, :TOKEN_POSITIONS] * usable[:, :, None, None]
    states = product('nbgf,nbgd->ngfd', live, values_window[:, :TOKEN_POSITIONS])
    norms = lax.optimization_barrier(jnp.sum(live, axis=1))
    prior_states = exclusive(states)
    prior_norms = exclusive(norms)

    def block(pieces):
        rows_in, normalized_rows, keys_here, values_here, features_here, state_here, norm_here, index = pieces
        positions = index * TOKEN_POSITIONS + jnp.arange(TOKEN_POSITIONS, dtype=jnp.int32)
        cos_here, sin_here = rotary_tables(positions, HEAD_SIZE)
        query_unrotated = matrix_product(normalized_rows, query_matrix) + ADAPTER_SCALE * matrix_product(matrix_product(normalized_rows, query_first_factor), query_second_factor)
        query_rows = low_rank(apply_rotation(low_rank_back(query_unrotated).reshape(TOKEN_POSITIONS, QUERY_HEADS, HEAD_SIZE), cos_here, sin_here))
        query_logits = low_rank_back(product('thd,hde->the', query_rows, query_feature))
        query_feature_rows = low_rank(hedgehog(query_logits))
        grouped_rows = query_rows.reshape(TOKEN_POSITIONS, KEY_VALUE_HEADS, group_size, HEAD_SIZE)
        feature_groups = query_feature_rows.reshape(TOKEN_POSITIONS, KEY_VALUE_HEADS, group_size, FEATURE_COUNT)
        scores = low_rank_back(product('tgjd,bgd->tgjb', grouped_rows, keys_here) * (1.0 / math.sqrt(HEAD_SIZE)))
        similar = low_rank_back(product('tgjf,bgf->tgjb', feature_groups, features_here))
        linear_mask, window_mask = attention_masks(TOKEN_POSITIONS, index > 0)
        weights_all = jnp.where(window_mask, jnp.exp(scores), 0.0) + jnp.where(linear_mask, similar, 0.0)
        divisor = lax.optimization_barrier(jnp.sum(weights_all, axis=-1)) + product('tgjf,gf->tgj', feature_groups, norm_here)
        shares = low_rank(weights_all / divisor[..., None])
        mixed_heads = product('tgjb,bgd->tgjd', shares, values_here) + product('tgjf,gfd->tgjd', feature_groups, state_here) / divisor[..., None]
        mixed_heads = low_rank_back(low_rank(mixed_heads)).reshape(TOKEN_POSITIONS, QUERY_HEADS * HEAD_SIZE)
        adapter_branch = low_rank_back(matrix_product(mixed_heads, output_matrix.T) + ADAPTER_SCALE * matrix_product(matrix_product(mixed_heads, output_first_factor), output_second_factor))
        middle = rows_in + adapter_branch
        normed_mid = low_rank(root_norm(middle, mlp_gain))
        gate = low_rank_back(matrix_product(normed_mid, gate_weight))
        upper = low_rank_back(matrix_product(normed_mid, up_weight))
        active = low_rank(jax.nn.silu(gate) * upper)
        return middle + matrix_product(active, down_weight.T)
    outputs = lax.map(jax.checkpoint(block), (inputs.reshape(blocks, TOKEN_POSITIONS, MODEL_WIDTH), normed_input.reshape(blocks, TOKEN_POSITIONS, MODEL_WIDTH), keys_window, values_window, features_window, prior_states, prior_norms, block_ids))
    return outputs.reshape(total_sum, MODEL_WIDTH)

def reference(inputs, cotangent, attn_gain, query_matrix, key_matrix, value_matrix, output_matrix, query_first_factor, query_second_factor, key_first_factor, key_second_factor, value_first_factor, value_second_factor, output_first_factor, output_second_factor, query_feature, key_feature_layer, mlp_gain, gate_weight, up_weight, down_weight):
    shape = inputs.shape
    total_sum = shape[0] * shape[1]
    result, pullback = jax.vjp(layer, inputs.reshape(total_sum, MODEL_WIDTH).astype(jnp.float32), attn_gain.astype(jnp.float32), query_matrix.astype(jnp.float32), key_matrix.astype(jnp.float32), value_matrix.astype(jnp.float32), output_matrix.astype(jnp.float32), query_first_factor.astype(jnp.float32), query_second_factor.astype(jnp.float32), key_first_factor.astype(jnp.float32), key_second_factor.astype(jnp.float32), value_first_factor.astype(jnp.float32), value_second_factor.astype(jnp.float32), output_first_factor.astype(jnp.float32), output_second_factor.astype(jnp.float32), query_feature.astype(jnp.float32), key_feature_layer.astype(jnp.float32), mlp_gain.astype(jnp.float32), gate_weight.astype(jnp.float32), up_weight.astype(jnp.float32), down_weight.astype(jnp.float32))
    grads = pullback(cotangent.reshape(total_sum, MODEL_WIDTH).astype(jnp.float32))
    return (result.reshape(shape).astype(jnp.bfloat16), grads[0].reshape(shape), grads[1], grads[2], grads[3], grads[4], grads[5], grads[6], grads[7], grads[8], grads[9], grads[10], grads[11], grads[12], grads[13], grads[14], grads[15], grads[16], grads[17], grads[18], grads[19])
```

```python
import math

import jax
import jax.numpy as jnp
from jax import lax
from jax.sharding import PartitionSpec as P

WIN = 64


EPS = 1e-05
ADAPTER_SCALE = 2.0
ROPE_BASE = 500000.0
HIGH = lax.Precision.HIGHEST


def dense_product(form, left, right):
    return jnp.einsum(form, left, right, preferred_element_type=jnp.float32)


def exact_result(form, left, right):
    return jnp.einsum(form, left, right, precision=HIGH, preferred_element_type=jnp.float32)


def root_scale(value_rows):
    return lax.rsqrt(jnp.mean(value_rows * value_rows, axis=-1, keepdims=True) + EPS)


def norm_back(grad_normed, value_rows, scale, gain):
    gained = grad_normed * gain
    inner = jnp.mean(gained * value_rows, axis=-1, keepdims=True)
    return scale * gained - value_rows * (scale * scale * scale) * inner


def rotary_tables(positions, width):
    half = width // 2
    inverse = ROPE_BASE ** (-(jnp.arange(half, dtype=jnp.float32) * (2.0 / width)))
    angles = positions.astype(jnp.float32)[:, None] * inverse[None, :]
    return (jnp.cos(angles), jnp.sin(angles))


def apply_rotation(value_rows, cosine_table, sine_table):
    half = value_rows.shape[-1] // 2
    first = value_rows[..., :half]
    second = value_rows[..., half:]
    cosine_table = cosine_table[..., None, :]
    sine_table = sine_table[..., None, :]
    return jnp.concatenate(
        [first * cosine_table - second * sine_table, second * cosine_table + first * sine_table],
        axis=-1,
    )


def hedgehog(logits):
    return jnp.concatenate(
        [jax.nn.softmax(logits, axis=-1), jax.nn.softmax(-logits, axis=-1)], axis=-1
    )


def hedgehog_back(logits, grads):
    return jax.vjp(hedgehog, logits)[1](grads)[0]


def attention_masks(rows, tail_valid):
    query_pos = lax.broadcasted_iota(jnp.int32, (rows, rows + WIN), 0)
    key_pos = lax.broadcasted_iota(jnp.int32, (rows, rows + WIN), 1)
    usable = jnp.logical_or(key_pos[None] >= WIN, tail_valid[:, None, None])
    linear_mask = jnp.logical_and((key_pos <= query_pos)[None], usable)
    window_mask = jnp.logical_and(
        jnp.logical_and(key_pos > query_pos, key_pos <= query_pos + WIN)[None], usable
    )
    return (linear_mask[:, :, None, None, :], window_mask[:, :, None, None, :])


def mix_weights(grouped_queries, feature_groups, keys_window, features_window, tail_valid):
    scale = 1.0 / math.sqrt(grouped_queries.shape[-1])
    scores = dense_product("mtgjd,mbgd->mtgjb", grouped_queries, keys_window) * scale
    similar = dense_product("mtgjf,mbgf->mtgjb", feature_groups, features_window)
    linear_mask, window_mask = attention_masks(grouped_queries.shape[1], tail_valid)
    exponent = jnp.where(window_mask, jnp.exp(scores), 0.0)
    return (exponent, exponent + jnp.where(linear_mask, similar, 0.0), linear_mask, window_mask)


def exchange(value):
    return lax.all_to_all(value, "seq", 0, 0, tiled=True)


def sum_before(states, inclusive_after):
    micro, rows, lanes = states.shape
    chips = lax.axis_size("seq")
    padded = -rows % (8 * chips)
    pieces = jnp.pad(states, ((0, 0), (0, padded), (0, 0))).astype(jnp.bfloat16)
    pieces = pieces.reshape(micro, chips, -1, lanes).swapaxes(0, 1)
    share = exchange(pieces)
    blocks = chips * micro
    source = jnp.arange(blocks)
    order = (source % micro) * chips + source // micro
    if inclusive_after:
        chosen = order[None, :] > order[:, None]
    else:
        chosen = order[None, :] < order[:, None]
    summed = jnp.einsum(
        "ab,brl->arl",
        chosen.astype(jnp.bfloat16),
        share.reshape(blocks, -1, lanes),
        preferred_element_type=jnp.float32,
    )
    back = exchange(summed.reshape(chips, micro, -1, lanes))
    return back.swapaxes(0, 1).reshape(micro, rows + padded, lanes)[:, :rows]


def pack_state(state, norm):
    micro, groups, features, width = state.shape
    joined = jnp.concatenate([state.swapaxes(-1, -2), norm[:, :, None, :]], axis=2)
    return joined.reshape(micro, groups * (width + 1), features)


def unpack_state(packed, groups):
    micro, rows, features = packed.shape
    joined = packed.reshape(micro, groups, rows // groups, features)
    return (joined[:, :, :-1].swapaxes(-1, -2), joined[:, :, -1])


def neighbour_tail(value, by):
    size = lax.axis_size("seq")
    index = lax.axis_index("seq")
    arrived = lax.ppermute(value, "seq", [(i, (i + by) % size) for i in range(size)])
    blank = jnp.zeros_like(arrived[:1])
    if by == 1:
        wrapped = jnp.concatenate([blank, arrived[:-1]], axis=0)
        return jnp.where(index == 0, wrapped, arrived)
    wrapped = jnp.concatenate([arrived[1:], blank], axis=0)
    return jnp.where(index == size - 1, wrapped, arrived)


def gather_hidden(local):
    chips = lax.axis_size("seq")
    rows, hidden = local.shape
    pieces = local.reshape(rows, chips, hidden // chips).swapaxes(0, 1)
    mine = exchange(pieces).reshape(chips * rows, hidden // chips)
    return lax.all_gather(mine, "tp", axis=1, tiled=True)


def return_hidden(delta):
    chips = lax.axis_size("seq")
    mine = lax.psum_scatter(delta, "tp", scatter_dimension=1, tiled=True).astype(jnp.bfloat16)
    rows, hidden = mine.shape
    pieces = exchange(mine.reshape(chips, rows // chips, hidden))
    return pieces.swapaxes(0, 1).reshape(rows // chips, chips * hidden).astype(jnp.float32)


def gather_positions(rows):
    return lax.all_gather(rows, "seq", axis=0, tiled=True)


def sum_positions(partial):
    return lax.psum_scatter(
        partial.astype(jnp.bfloat16), "seq", scatter_dimension=0, tiled=True
    ).astype(jnp.float32)


def scatter_rows(delta):
    return lax.psum_scatter(
        delta.astype(jnp.bfloat16), "seq", scatter_dimension=0, tiled=True
    ).astype(jnp.float32)


def total_small(split, shared):
    chips = lax.axis_size("seq")
    cores = lax.axis_size("tp")
    unit = 128 * chips * 8
    flat_split = jnp.concatenate([part.reshape(-1) for part in split])
    flat_shared = jnp.concatenate([part.reshape(-1) for part in shared])
    flat_shared = jnp.pad(flat_shared, (0, -flat_shared.shape[0] % (cores * 128)))
    half = lax.psum_scatter(
        flat_shared.reshape(-1, 128), "tp", scatter_dimension=0, tiled=True
    ).reshape(-1)
    both = jnp.concatenate([flat_split, half])
    length = both.shape[0]
    both = jnp.pad(both, (0, -length % unit)).reshape(chips, -1, 128)
    mine = jnp.sum(exchange(both), axis=0)
    whole = lax.all_gather(lax.all_gather(mine, "seq", axis=0, tiled=True), "tp", axis=0)
    whole = whole.reshape(cores, -1)[:, :length]
    split_out = []
    start = 0
    for part in split:
        split_out.append(whole[:, start : start + part.size].reshape((cores,) + part.shape))
        start += part.size
    joined = whole[:, start:].reshape(-1)
    shared_out = []
    start = 0
    for part in shared:
        shared_out.append(joined[start : start + part.size].reshape(part.shape))
        start += part.size
    return (split_out, shared_out)


def beside(pair):
    return jnp.concatenate([pair[0], pair[1]], axis=-1)


def per_device(
    inputs,
    cotangent,
    attn_gain,
    query_matrix,
    key_matrix,
    value_matrix,
    output_matrix,
    query_first_factor,
    query_second_factor,
    key_first_factor,
    key_second_factor,
    value_first_factor,
    value_second_factor,
    output_first_factor,
    output_second_factor,
    query_feature,
    key_feature_layer,
    mlp_gain,
    gate_weight,
    up_weight,
    down_weight,
):
    micro, piece, width = inputs.shape
    core_count = lax.axis_size("tp")
    chain_count = lax.axis_size("seq")
    chain_index = lax.axis_index("seq")
    rows = piece * core_count
    span = rows * chain_count
    heads_here = query_feature.shape[0]
    head_width = query_feature.shape[1]
    groups_here = key_feature_layer.shape[0]
    group_size = heads_here // groups_here
    feature_width = 2 * head_width
    rank = query_first_factor.shape[1]
    scale = 1.0 / math.sqrt(head_width)
    query_width = heads_here * head_width
    key_width = groups_here * head_width
    own = micro * piece
    hidden = gate_weight.shape[1]
    shrink_all = jnp.concatenate([query_first_factor, key_first_factor, value_first_factor], axis=1)
    expand_all = jnp.zeros((3 * rank, query_width + 2 * key_width), jnp.bfloat16)
    expand_all = expand_all.at[:rank, :query_width].set(query_second_factor)
    expand_all = expand_all.at[rank : 2 * rank, query_width : query_width + key_width].set(
        key_second_factor
    )
    expand_all = expand_all.at[2 * rank :, query_width + key_width :].set(value_second_factor)
    gain_in = attn_gain.astype(jnp.float32)
    gain_mid = mlp_gain.astype(jnp.float32)

    project_full = lax.all_gather(
        jnp.concatenate([query_matrix, key_matrix, value_matrix], axis=1),
        "seq",
        axis=0,
        tiled=True,
    )
    output_full_weight = lax.all_gather(output_matrix, "seq", axis=0, tiled=True)
    gate_here = gather_hidden(gate_weight)
    up_here = gather_hidden(up_weight)
    down_here = gather_hidden(down_weight)
    cotangent_rows = cotangent.reshape(own, width)
    cotangent_all = gather_positions(cotangent_rows)

    rows_in = inputs.astype(jnp.float32)
    scale_in = root_scale(rows_in)
    normed_input = lax.all_gather(
        (rows_in * scale_in * gain_in).astype(jnp.bfloat16), "tp", axis=1, tiled=True
    )
    shrunk = dense_product("mtc,cr->mtr", normed_input, shrink_all)
    projected = dense_product(
        "mtc,ck->mtk", normed_input, project_full
    ) + ADAPTER_SCALE * exact_result("mtr,rk->mtk", shrunk, expand_all.astype(jnp.float32))
    positions = (
        jnp.arange(micro, dtype=jnp.int32)[:, None] * span
        + chain_index * rows
        + jnp.arange(rows, dtype=jnp.int32)[None, :]
    )
    cosine_table, sine_table = rotary_tables(positions.reshape(-1), head_width)
    cosine_table = cosine_table.reshape(micro, rows, -1)
    sine_table = sine_table.reshape(micro, rows, -1)
    query_rows = apply_rotation(
        projected[..., :query_width].reshape(micro, rows, heads_here, head_width),
        cosine_table,
        sine_table,
    ).astype(jnp.bfloat16)
    key_rows = apply_rotation(
        projected[..., query_width : query_width + key_width].reshape(
            micro, rows, groups_here, head_width
        ),
        cosine_table,
        sine_table,
    ).astype(jnp.bfloat16)
    value_rows = (
        projected[..., query_width + key_width :]
        .astype(jnp.bfloat16)
        .reshape(micro, rows, groups_here, head_width)
    )
    key_logits = dense_product("mthd,hde->mthe", key_rows, key_feature_layer)
    key_features = hedgehog(key_logits).astype(jnp.bfloat16)
    tail = neighbour_tail(
        jnp.concatenate(
            [
                key_rows[:, rows - WIN :],
                value_rows[:, rows - WIN :],
                key_features[:, rows - WIN :],
            ],
            axis=-1,
        ),
        1,
    )
    tail_valid = jnp.logical_or(chain_index > 0, jnp.arange(micro) > 0)
    keys_window = jnp.concatenate([tail[..., :head_width], key_rows], axis=1)
    values_window = jnp.concatenate([tail[..., head_width : 2 * head_width], value_rows], axis=1)
    features_window = jnp.concatenate([tail[..., 2 * head_width :], key_features], axis=1)
    usable = jnp.logical_or(jnp.arange(rows)[None] >= WIN, tail_valid[:, None])
    live = features_window[:, :rows] * usable.astype(jnp.bfloat16)[:, :, None, None]
    state_here = dense_product("mbgf,mbgd->mgfd", live, values_window[:, :rows])
    norm_here = jnp.sum(live.astype(jnp.float32), axis=1)
    prior_state, prior_norm = unpack_state(
        sum_before(pack_state(state_here, norm_here), False), groups_here
    )
    query_logits = dense_product("mthd,hde->mthe", query_rows, query_feature)
    query_feature_rows = hedgehog(query_logits).astype(jnp.bfloat16)
    grouped_queries = query_rows.reshape(micro, rows, groups_here, group_size, head_width)
    feature_groups = query_feature_rows.reshape(
        micro, rows, groups_here, group_size, feature_width
    )
    exponent, weights_all, linear_mask, window_mask = mix_weights(
        grouped_queries, feature_groups, keys_window, features_window, tail_valid
    )
    features_exact = feature_groups.astype(jnp.float32)
    divisor = jnp.sum(weights_all, axis=-1) + exact_result(
        "mtgjf,mgf->mtgj", features_exact, prior_norm
    )
    ratio = weights_all / divisor[..., None]
    shares = ratio.astype(jnp.bfloat16)
    prior_out = exact_result("mtgjf,mgfd->mtgjd", features_exact, prior_state) / divisor[..., None]
    mixed_heads = (
        (dense_product("mtgjb,mbgd->mtgjd", shares, values_window) + prior_out)
        .astype(jnp.bfloat16)
        .reshape(micro, rows, query_width)
    )
    output_low_rank = dense_product("mtc,cr->mtr", mixed_heads, output_first_factor)
    adapter_branch = dense_product(
        "mta,wa->mtw", mixed_heads, output_full_weight
    ) + ADAPTER_SCALE * exact_result(
        "mtr,rd->mtd", output_low_rank, output_second_factor.astype(jnp.float32)
    )
    middle = (
        rows_in + lax.psum_scatter(adapter_branch, "tp", scatter_dimension=1, tiled=True)
    ).reshape(own, width)
    scale_mid = root_scale(middle)

    normed_mid = gather_positions((middle * scale_mid * gain_mid).astype(jnp.bfloat16))
    gate = dense_product("tc,cf->tf", normed_mid, gate_here)
    upper = dense_product("tc,cf->tf", normed_mid, up_here)
    logistic = jax.nn.sigmoid(gate)
    active = (gate * logistic * upper).astype(jnp.bfloat16)
    active_back = dense_product("td,df->tf", cotangent_all, down_here)
    gate_back = (active_back * upper * logistic * (1.0 + gate * (1.0 - logistic))).astype(
        jnp.bfloat16
    )
    upper_back = (active_back * gate * logistic).astype(jnp.bfloat16)
    mid_norm_back = sum_positions(
        dense_product("tf,cf->tc", gate_back, gate_here)
        + dense_product("tf,cf->tc", upper_back, up_here)
    )
    results = middle + sum_positions(dense_product("tf,df->td", active, down_here))
    gate_delta = return_hidden(dense_product("tc,tf->cf", normed_mid, gate_back))
    up_delta = return_hidden(dense_product("tc,tf->cf", normed_mid, upper_back))
    down_delta = return_hidden(dense_product("td,tf->df", cotangent_all, active))

    mlp_gain_delta = jnp.sum(mid_norm_back * middle * scale_mid, axis=0)
    middle_back = cotangent_rows.astype(jnp.float32) + norm_back(
        mid_norm_back, middle, scale_mid, gain_mid
    )
    branch_back = lax.all_gather(
        middle_back.astype(jnp.bfloat16).reshape(micro, piece, width), "tp", axis=1, tiled=True
    )
    output_lifted = ADAPTER_SCALE * dense_product(
        "mtv,wv->mtw", branch_back, output_second_factor
    )
    out_delta = scatter_rows(dense_product("mtd,mtc->dc", branch_back, mixed_heads))
    out_shrink_delta = exact_result("mtc,mtr->cr", mixed_heads.astype(jnp.float32), output_lifted)
    output_second_delta = ADAPTER_SCALE * exact_result(
        "mtc,mtg->cg", output_low_rank, branch_back.astype(jnp.float32)
    )
    mixed_back = dense_product("mtd,dc->mtc", branch_back, output_full_weight) + exact_result(
        "mtr,cr->mtc", output_lifted, output_first_factor.astype(jnp.float32)
    )
    heads_back = mixed_back.astype(jnp.bfloat16).reshape(
        micro, rows, groups_here, group_size, head_width
    )
    shares_back = dense_product("mtgjd,mbgd->mtgjb", heads_back, values_window)
    values_window_back = dense_product("mtgjb,mtgjd->mbgd", shares, heads_back)
    heads_exact = heads_back.astype(jnp.float32)
    scaled_back = heads_exact / divisor[..., None]
    state_back = exact_result("mtgjf,mtgjd->mgfd", features_exact, scaled_back)
    query_features_back = exact_result("mtgjd,mgfd->mtgjf", scaled_back, prior_state)
    divisor_back = (
        -(jnp.sum(shares_back * ratio, axis=-1) + jnp.sum(heads_exact * prior_out, axis=-1))
        / divisor
    )
    weights_back = shares_back / divisor[..., None] + divisor_back[..., None]
    query_features_back = (
        query_features_back + divisor_back[..., None] * prior_norm[:, None, :, None, :]
    )
    norm_state_back = jnp.sum(divisor_back[..., None] * features_exact, axis=(1, 3))
    later_state, later_norm = unpack_state(
        sum_before(pack_state(state_back, norm_state_back), True), groups_here
    )
    scores_back = jnp.where(window_mask, weights_back * exponent, 0.0).astype(jnp.bfloat16)
    similar_back = jnp.where(linear_mask, weights_back, 0.0).astype(jnp.bfloat16)
    query_features_back = query_features_back + dense_product(
        "mtgjb,mbgf->mtgjf", similar_back, features_window
    )
    features_window_back = dense_product("mtgjb,mtgjf->mbgf", similar_back, feature_groups)
    queries_back = dense_product("mtgjb,mbgd->mtgjd", scores_back, keys_window) * scale
    keys_window_back = dense_product("mtgjb,mtgjd->mbgd", scores_back, grouped_queries) * scale
    usable_lead = usable.astype(jnp.float32)[:, :, None, None]
    values_lead = values_window[:, :rows].astype(jnp.float32)
    features_lead = features_window[:, :rows].astype(jnp.float32)
    features_lead_back = usable_lead * (
        exact_result("mbgd,mgfd->mbgf", values_lead, later_state) + later_norm[:, None]
    )
    values_lead_back = usable_lead * exact_result("mbgf,mgfd->mbgd", features_lead, later_state)
    returning = jnp.concatenate(
        [
            keys_window_back[:, :WIN],
            values_window_back[:, :WIN] + values_lead_back[:, :WIN],
            features_window_back[:, :WIN] + features_lead_back[:, :WIN],
        ],
        axis=-1,
    )
    arriving = neighbour_tail(returning.astype(jnp.bfloat16), -1).astype(jnp.float32)

    def gathered_back(window_back, lead_back, arrived):
        late = window_back[:, rows:] + arrived
        early = window_back[:, WIN:rows]
        if lead_back is not None:
            early = early + lead_back[:, WIN:]
        return jnp.concatenate([early, late], axis=1)

    keys_back = gathered_back(keys_window_back, None, arriving[..., :head_width])
    values_back = gathered_back(
        values_window_back, values_lead_back, arriving[..., head_width : 2 * head_width]
    )
    key_features_back = gathered_back(
        features_window_back, features_lead_back, arriving[..., 2 * head_width :]
    )
    key_logits_back = hedgehog_back(key_logits, key_features_back).astype(jnp.bfloat16)
    query_logits_back = hedgehog_back(
        query_logits, query_features_back.reshape(micro, rows, heads_here, feature_width)
    ).astype(jnp.bfloat16)
    key_feature_delta = dense_product("mthd,mthe->hde", key_rows, key_logits_back)
    query_feature_delta = dense_product("mthd,mthe->hde", query_rows, query_logits_back)
    keys_back = keys_back + dense_product("mthe,hde->mthd", key_logits_back, key_feature_layer)
    queries_back = queries_back.reshape(micro, rows, heads_here, head_width) + dense_product(
        "mthe,hde->mthd", query_logits_back, query_feature
    )
    projected_back = jnp.concatenate(
        [
            apply_rotation(queries_back, cosine_table, -sine_table)
            .astype(jnp.bfloat16)
            .reshape(micro, rows, query_width),
            apply_rotation(keys_back, cosine_table, -sine_table)
            .astype(jnp.bfloat16)
            .reshape(micro, rows, key_width),
            values_back.astype(jnp.bfloat16).reshape(micro, rows, key_width),
        ],
        axis=-1,
    )
    lift_all = ADAPTER_SCALE * dense_product("mtk,rk->mtr", projected_back, expand_all)
    project_delta = scatter_rows(dense_product("mtc,mtk->ck", normed_input, projected_back))
    expand_delta = ADAPTER_SCALE * exact_result(
        "mtr,mtk->rk", shrunk, projected_back.astype(jnp.float32)
    )
    shrink_delta = exact_result("mtc,mtr->cr", normed_input.astype(jnp.float32), lift_all)
    normed_back = dense_product("mtk,ck->mtc", projected_back, project_full) + exact_result(
        "mtr,cr->mtc", lift_all, shrink_all.astype(jnp.float32)
    )
    in_norm_back = lax.psum_scatter(normed_back, "tp", scatter_dimension=1, tiled=True)
    attn_gain_delta = jnp.sum(in_norm_back * rows_in * scale_in, axis=(0, 1))
    inputs_back = middle_back.reshape(micro, piece, width) + norm_back(
        in_norm_back, rows_in, scale_in, gain_in
    )
    split, shared = total_small(
        (
            expand_delta[:rank, :query_width],
            expand_delta[rank : 2 * rank, query_width : query_width + key_width],
            expand_delta[2 * rank :, query_width + key_width :],
            out_shrink_delta,
            query_feature_delta,
            key_feature_delta,
        ),
        (attn_gain_delta, shrink_delta, output_second_delta, mlp_gain_delta),
    )
    return (
        results.astype(jnp.bfloat16).reshape(micro, piece, width),
        inputs_back,
        shared[0],
        project_delta[:, :query_width],
        project_delta[:, query_width : query_width + key_width],
        project_delta[:, query_width + key_width :],
        out_delta,
        shared[1][:, :rank],
        beside(split[0]),
        shared[1][:, rank : 2 * rank],
        beside(split[1]),
        shared[1][:, 2 * rank :],
        beside(split[2]),
        split[3].reshape(-1, rank),
        shared[2],
        split[4].reshape(-1, head_width, head_width),
        split[5].reshape(-1, head_width, head_width),
        shared[3],
        gate_delta,
        up_delta,
        down_delta,
    )


def solution(mesh):
    return jax.shard_map(
        per_device,
        mesh=mesh,
        in_specs=(
            P(None, ("seq", "tp"), None),
            P(None, ("seq", "tp"), None),
            P(),
            P("seq", "tp"),
            P("seq", "tp"),
            P("seq", "tp"),
            P("seq", "tp"),
            P(),
            P(None, "tp"),
            P(),
            P(None, "tp"),
            P(),
            P(None, "tp"),
            P("tp", None),
            P(),
            P("tp", None, None),
            P("tp", None, None),
            P(),
            P("seq", "tp"),
            P("seq", "tp"),
            P("seq", "tp"),
        ),
        out_specs=(
            P(None, ("seq", "tp"), None),
            P(None, ("seq", "tp"), None),
            P(),
            P("seq", "tp"),
            P("seq", "tp"),
            P("seq", "tp"),
            P("seq", "tp"),
            P(),
            P(),
            P(),
            P(),
            P(),
            P(),
            P(),
            P(),
            P(),
            P(),
            P(),
            P("seq", "tp"),
            P("seq", "tp"),
            P("seq", "tp"),
        ),
        check_vma=False,
    )
```

```python
import math

import jax
import jax.numpy as jnp
from jax import lax
from jax.sharding import PartitionSpec as P

WIN = 64


EPS = 1e-05
ADAPTER_SCALE = 2.0
ROPE_BASE = 500000.0
HIGH = lax.Precision.HIGHEST


def dense_product(form, left, right):
    return jnp.einsum(form, left, right, preferred_element_type=jnp.float32)


def exact_result(form, left, right):
    return jnp.einsum(form, left, right, precision=HIGH, preferred_element_type=jnp.float32)


def root_scale(value_rows):
    return lax.rsqrt(jnp.mean(value_rows * value_rows, axis=-1, keepdims=True) + EPS)


def norm_back(grad_normed, value_rows, scale, gain):
    gained = grad_normed * gain
    inner = jnp.mean(gained * value_rows, axis=-1, keepdims=True)
    return scale * gained - value_rows * (scale * scale * scale) * inner


def rotary_tables(positions, width):
    half = width // 2
    inverse = ROPE_BASE ** (-(jnp.arange(half, dtype=jnp.float32) * (2.0 / width)))
    angles = positions.astype(jnp.float32)[:, None] * inverse[None, :]
    return (jnp.cos(angles), jnp.sin(angles))


def apply_rotation(value_rows, cosine_table, sine_table):
    half = value_rows.shape[-1] // 2
    first = value_rows[..., :half]
    second = value_rows[..., half:]
    cosine_table = cosine_table[..., None, :]
    sine_table = sine_table[..., None, :]
    return jnp.concatenate(
        [first * cosine_table - second * sine_table, second * cosine_table + first * sine_table],
        axis=-1,
    )


def hedgehog(logits):
    return jnp.concatenate(
        [jax.nn.softmax(logits, axis=-1), jax.nn.softmax(-logits, axis=-1)], axis=-1
    )


def hedgehog_back(logits, grads):
    return jax.vjp(hedgehog, logits)[1](grads)[0]


def attention_masks(rows, tail_valid):
    query_pos = lax.broadcasted_iota(jnp.int32, (rows, rows + WIN), 0)
    key_pos = lax.broadcasted_iota(jnp.int32, (rows, rows + WIN), 1)
    usable = jnp.logical_or(key_pos[None] >= WIN, tail_valid[:, None, None])
    linear_mask = jnp.logical_and((key_pos <= query_pos)[None], usable)
    window_mask = jnp.logical_and(
        jnp.logical_and(key_pos > query_pos, key_pos <= query_pos + WIN)[None], usable
    )
    return (linear_mask[:, :, None, None, :], window_mask[:, :, None, None, :])


def mix_weights(grouped_queries, feature_groups, keys_window, features_window, tail_valid):
    scale = 1.0 / math.sqrt(grouped_queries.shape[-1])
    scores = dense_product("mtgjd,mbgd->mtgjb", grouped_queries, keys_window) * scale
    similar = dense_product("mtgjf,mbgf->mtgjb", feature_groups, features_window)
    linear_mask, window_mask = attention_masks(grouped_queries.shape[1], tail_valid)
    exponent = jnp.where(window_mask, jnp.exp(scores), 0.0)
    return (exponent, exponent + jnp.where(linear_mask, similar, 0.0), linear_mask, window_mask)


def after(value, *earlier):
    return lax.optimization_barrier((value,) + earlier)[0]


def swapped(value):
    return lax.ppermute(value, "tp", [(0, 1), (1, 0)])


def gather_cores(value, axis):
    other = swapped(value)
    first = lax.axis_index("tp") == 0
    return jnp.concatenate(
        [jnp.where(first, value, other), jnp.where(first, other, value)], axis=axis
    )


def sum_cores(partial, axis):
    half = partial.shape[axis] // 2
    core = lax.axis_index("tp")
    keep = lax.dynamic_slice_in_dim(partial, core * half, half, axis)
    send = lax.dynamic_slice_in_dim(partial, (1 - core) * half, half, axis)
    return keep + swapped(send)


def exchange(value):
    return lax.all_to_all(value, "seq", 0, 0, tiled=True)


def sum_before(states, inclusive_after):
    micro, rows, lanes = states.shape
    chips = lax.axis_size("seq")
    padded = -rows % (8 * chips)
    pieces = jnp.pad(states, ((0, 0), (0, padded), (0, 0))).astype(jnp.bfloat16)
    pieces = pieces.reshape(micro, chips, -1, lanes).swapaxes(0, 1)
    share = exchange(pieces)
    blocks = chips * micro
    source = jnp.arange(blocks)
    order = (source % micro) * chips + source // micro
    if inclusive_after:
        chosen = order[None, :] > order[:, None]
    else:
        chosen = order[None, :] < order[:, None]
    summed = jnp.einsum(
        "ab,brl->arl",
        chosen.astype(jnp.bfloat16),
        share.reshape(blocks, -1, lanes),
        preferred_element_type=jnp.float32,
    )
    back = exchange(summed.reshape(chips, micro, -1, lanes))
    return back.swapaxes(0, 1).reshape(micro, rows + padded, lanes)[:, :rows]


def pack_state(state, norm):
    micro, groups, features, width = state.shape
    joined = jnp.concatenate([state.swapaxes(-1, -2), norm[:, :, None, :]], axis=2)
    return joined.reshape(micro, groups * (width + 1), features)


def unpack_state(packed, groups):
    micro, rows, features = packed.shape
    joined = packed.reshape(micro, groups, rows // groups, features)
    return (joined[:, :, :-1].swapaxes(-1, -2), joined[:, :, -1])


def neighbour_tail(value, by):
    size = lax.axis_size("seq")
    index = lax.axis_index("seq")
    arrived = lax.ppermute(value, "seq", [(i, (i + by) % size) for i in range(size)])
    blank = jnp.zeros_like(arrived[:1])
    if by == 1:
        wrapped = jnp.concatenate([blank, arrived[:-1]], axis=0)
        return jnp.where(index == 0, wrapped, arrived)
    wrapped = jnp.concatenate([arrived[1:], blank], axis=0)
    return jnp.where(index == size - 1, wrapped, arrived)


def gather_hidden(local):
    chips = lax.axis_size("seq")
    rows, hidden = local.shape
    pieces = local.reshape(rows, chips, hidden // chips).swapaxes(0, 1)
    mine = exchange(pieces).reshape(chips * rows, hidden // chips)
    return gather_cores(mine, 1)


def return_hidden(delta):
    chips = lax.axis_size("seq")
    mine = sum_cores(delta, 1).astype(jnp.bfloat16)
    rows, hidden = mine.shape
    pieces = exchange(mine.reshape(chips, rows // chips, hidden))
    return pieces.swapaxes(0, 1).reshape(rows // chips, chips * hidden).astype(jnp.float32)


def gather_positions(rows):
    return lax.all_gather(rows, "seq", axis=0, tiled=True)


def sum_positions(partial):
    return lax.psum_scatter(
        partial.astype(jnp.bfloat16), "seq", scatter_dimension=0, tiled=True
    ).astype(jnp.float32)


def scatter_rows(delta):
    return lax.psum_scatter(
        delta.astype(jnp.bfloat16), "seq", scatter_dimension=0, tiled=True
    ).astype(jnp.float32)


def total_small(split, shared):
    chips = lax.axis_size("seq")
    cores = lax.axis_size("tp")
    unit = 128 * chips * 8
    flat_split = jnp.concatenate([part.reshape(-1) for part in split])
    flat_shared = jnp.concatenate([part.reshape(-1) for part in shared])
    flat_shared = jnp.pad(flat_shared, (0, -flat_shared.shape[0] % (cores * 128)))
    half = sum_cores(flat_shared, 0)
    both = jnp.concatenate([flat_split, half])
    length = both.shape[0]
    both = jnp.pad(both, (0, -length % unit)).reshape(chips, -1, 128)
    mine = jnp.sum(exchange(both), axis=0)
    whole = exchange(jnp.broadcast_to(mine[None], both.shape)).reshape(1, -1)
    whole = gather_cores(whole, 0)[:, :length]
    split_out = []
    start = 0
    for part in split:
        split_out.append(whole[:, start : start + part.size].reshape((cores,) + part.shape))
        start += part.size
    joined = whole[:, start:].reshape(-1)
    shared_out = []
    start = 0
    for part in shared:
        shared_out.append(joined[start : start + part.size].reshape(part.shape))
        start += part.size
    return (split_out, shared_out)


def beside(pair):
    return jnp.concatenate([pair[0], pair[1]], axis=-1)


def per_device(
    inputs,
    cotangent,
    attn_gain,
    query_matrix,
    key_matrix,
    value_matrix,
    output_matrix,
    query_first_factor,
    query_second_factor,
    key_first_factor,
    key_second_factor,
    value_first_factor,
    value_second_factor,
    output_first_factor,
    output_second_factor,
    query_feature,
    key_feature_layer,
    mlp_gain,
    gate_weight,
    up_weight,
    down_weight,
):
    micro, piece, width = inputs.shape
    core_count = lax.axis_size("tp")
    chain_count = lax.axis_size("seq")
    chain_index = lax.axis_index("seq")
    rows = piece * core_count
    span = rows * chain_count
    heads_here = query_feature.shape[0]
    head_width = query_feature.shape[1]
    groups_here = key_feature_layer.shape[0]
    group_size = heads_here // groups_here
    feature_width = 2 * head_width
    rank = query_first_factor.shape[1]
    scale = 1.0 / math.sqrt(head_width)
    query_width = heads_here * head_width
    key_width = groups_here * head_width
    own = micro * piece
    hidden = gate_weight.shape[1]
    shrink_all = jnp.concatenate([query_first_factor, key_first_factor, value_first_factor], axis=1)
    expand_all = jnp.zeros((3 * rank, query_width + 2 * key_width), jnp.bfloat16)
    expand_all = expand_all.at[:rank, :query_width].set(query_second_factor)
    expand_all = expand_all.at[rank : 2 * rank, query_width : query_width + key_width].set(
        key_second_factor
    )
    expand_all = expand_all.at[2 * rank :, query_width + key_width :].set(value_second_factor)
    gain_in = attn_gain.astype(jnp.float32)
    gain_mid = mlp_gain.astype(jnp.float32)

    project_full = lax.all_gather(
        jnp.concatenate([query_matrix, key_matrix, value_matrix], axis=1),
        "seq",
        axis=0,
        tiled=True,
    )
    project_full, gate_here, up_here, down_here = lax.optimization_barrier(
        (
            project_full,
            gather_hidden(gate_weight),
            gather_hidden(up_weight),
            gather_hidden(down_weight),
        )
    )
    output_full_weight = lax.all_gather(
        after(output_matrix, project_full), "seq", axis=0, tiled=True
    )
    cotangent_rows = cotangent.reshape(own, width)
    cotangent_all = gather_positions(after(cotangent_rows, project_full))

    rows_in = inputs.astype(jnp.float32)
    scale_in = root_scale(rows_in)
    normed_input = gather_cores((rows_in * scale_in * gain_in).astype(jnp.bfloat16), 1)
    shrunk = dense_product("mtc,cr->mtr", normed_input, shrink_all)
    projected = dense_product(
        "mtc,ck->mtk", normed_input, project_full
    ) + ADAPTER_SCALE * exact_result("mtr,rk->mtk", shrunk, expand_all.astype(jnp.float32))
    positions = (
        jnp.arange(micro, dtype=jnp.int32)[:, None] * span
        + chain_index * rows
        + jnp.arange(rows, dtype=jnp.int32)[None, :]
    )
    cosine_table, sine_table = rotary_tables(positions.reshape(-1), head_width)
    cosine_table = cosine_table.reshape(micro, rows, -1)
    sine_table = sine_table.reshape(micro, rows, -1)
    query_rows = apply_rotation(
        projected[..., :query_width].reshape(micro, rows, heads_here, head_width),
        cosine_table,
        sine_table,
    ).astype(jnp.bfloat16)
    key_rows = apply_rotation(
        projected[..., query_width : query_width + key_width].reshape(
            micro, rows, groups_here, head_width
        ),
        cosine_table,
        sine_table,
    ).astype(jnp.bfloat16)
    value_rows = (
        projected[..., query_width + key_width :]
        .astype(jnp.bfloat16)
        .reshape(micro, rows, groups_here, head_width)
    )
    key_logits = dense_product("mthd,hde->mthe", key_rows, key_feature_layer)
    key_features = hedgehog(key_logits).astype(jnp.bfloat16)
    tail = neighbour_tail(
        jnp.concatenate(
            [
                key_rows[:, rows - WIN :],
                value_rows[:, rows - WIN :],
                key_features[:, rows - WIN :],
            ],
            axis=-1,
        ),
        1,
    )
    tail_valid = jnp.logical_or(chain_index > 0, jnp.arange(micro) > 0)
    keys_window = jnp.concatenate([tail[..., :head_width], key_rows], axis=1)
    values_window = jnp.concatenate([tail[..., head_width : 2 * head_width], value_rows], axis=1)
    features_window = jnp.concatenate([tail[..., 2 * head_width :], key_features], axis=1)
    usable = jnp.logical_or(jnp.arange(rows)[None] >= WIN, tail_valid[:, None])
    live = features_window[:, :rows] * usable.astype(jnp.bfloat16)[:, :, None, None]
    state_here = dense_product("mbgf,mbgd->mgfd", live, values_window[:, :rows])
    norm_here = jnp.sum(live.astype(jnp.float32), axis=1)
    prior_state, prior_norm = unpack_state(
        sum_before(pack_state(state_here, norm_here), False), groups_here
    )
    query_logits = dense_product("mthd,hde->mthe", query_rows, query_feature)
    query_feature_rows = hedgehog(query_logits).astype(jnp.bfloat16)
    grouped_queries = query_rows.reshape(micro, rows, groups_here, group_size, head_width)
    feature_groups = query_feature_rows.reshape(
        micro, rows, groups_here, group_size, feature_width
    )
    exponent, weights_all, linear_mask, window_mask = mix_weights(
        grouped_queries, feature_groups, keys_window, features_window, tail_valid
    )
    features_exact = feature_groups.astype(jnp.float32)
    divisor = jnp.sum(weights_all, axis=-1) + exact_result(
        "mtgjf,mgf->mtgj", features_exact, prior_norm
    )
    ratio = weights_all / divisor[..., None]
    shares = ratio.astype(jnp.bfloat16)
    prior_out = exact_result("mtgjf,mgfd->mtgjd", features_exact, prior_state) / divisor[..., None]
    mixed_heads = (
        (dense_product("mtgjb,mbgd->mtgjd", shares, values_window) + prior_out)
        .astype(jnp.bfloat16)
        .reshape(micro, rows, query_width)
    )
    output_low_rank = dense_product("mtc,cr->mtr", mixed_heads, output_first_factor)
    adapter_branch = dense_product(
        "mta,wa->mtw", mixed_heads, output_full_weight
    ) + ADAPTER_SCALE * exact_result(
        "mtr,rd->mtd", output_low_rank, output_second_factor.astype(jnp.float32)
    )
    middle = (rows_in + sum_cores(adapter_branch, 1)).reshape(own, width)
    scale_mid = root_scale(middle)

    normed_mid = gather_positions((middle * scale_mid * gain_mid).astype(jnp.bfloat16))
    gate = dense_product("tc,cf->tf", normed_mid, gate_here)
    upper = dense_product("tc,cf->tf", normed_mid, up_here)
    logistic = jax.nn.sigmoid(gate)
    active = (gate * logistic * upper).astype(jnp.bfloat16)
    active_back = dense_product("td,df->tf", cotangent_all, down_here)
    gate_back = (active_back * upper * logistic * (1.0 + gate * (1.0 - logistic))).astype(
        jnp.bfloat16
    )
    upper_back = (active_back * gate * logistic).astype(jnp.bfloat16)
    mid_norm_back = sum_positions(
        dense_product("tf,cf->tc", gate_back, gate_here)
        + dense_product("tf,cf->tc", upper_back, up_here)
    )
    mid_norm_back, gate_delta, up_delta, down_delta = lax.optimization_barrier(
        (
            mid_norm_back,
            return_hidden(dense_product("tc,tf->cf", normed_mid, gate_back)),
            return_hidden(dense_product("tc,tf->cf", normed_mid, upper_back)),
            return_hidden(dense_product("td,tf->df", cotangent_all, active)),
        )
    )
    down_rows = sum_positions(
        after(dense_product("tf,df->td", active, down_here).astype(jnp.bfloat16), mid_norm_back)
    )

    mlp_gain_delta = jnp.sum(mid_norm_back * middle * scale_mid, axis=0)
    middle_back = cotangent_rows.astype(jnp.float32) + norm_back(
        mid_norm_back, middle, scale_mid, gain_mid
    )
    branch_back = gather_cores(
        middle_back.astype(jnp.bfloat16).reshape(micro, piece, width), 1
    )
    output_lifted = ADAPTER_SCALE * dense_product(
        "mtv,wv->mtw", branch_back, output_second_factor
    )
    out_delta = scatter_rows(dense_product("mtd,mtc->dc", branch_back, mixed_heads))
    out_shrink_delta = exact_result("mtc,mtr->cr", mixed_heads.astype(jnp.float32), output_lifted)
    output_second_delta = ADAPTER_SCALE * exact_result(
        "mtc,mtg->cg", output_low_rank, branch_back.astype(jnp.float32)
    )
    mixed_back = dense_product("mtd,dc->mtc", branch_back, output_full_weight) + exact_result(
        "mtr,cr->mtc", output_lifted, output_first_factor.astype(jnp.float32)
    )
    heads_back = mixed_back.astype(jnp.bfloat16).reshape(
        micro, rows, groups_here, group_size, head_width
    )
    shares_back = dense_product("mtgjd,mbgd->mtgjb", heads_back, values_window)
    values_window_back = dense_product("mtgjb,mtgjd->mbgd", shares, heads_back)
    heads_exact = heads_back.astype(jnp.float32)
    scaled_back = heads_exact / divisor[..., None]
    state_back = exact_result("mtgjf,mtgjd->mgfd", features_exact, scaled_back)
    query_features_back = exact_result("mtgjd,mgfd->mtgjf", scaled_back, prior_state)
    divisor_back = (
        -(jnp.sum(shares_back * ratio, axis=-1) + jnp.sum(heads_exact * prior_out, axis=-1))
        / divisor
    )
    weights_back = shares_back / divisor[..., None] + divisor_back[..., None]
    query_features_back = (
        query_features_back + divisor_back[..., None] * prior_norm[:, None, :, None, :]
    )
    norm_state_back = jnp.sum(divisor_back[..., None] * features_exact, axis=(1, 3))
    later_state, later_norm = unpack_state(
        sum_before(pack_state(state_back, norm_state_back), True), groups_here
    )
    scores_back = jnp.where(window_mask, weights_back * exponent, 0.0).astype(jnp.bfloat16)
    similar_back = jnp.where(linear_mask, weights_back, 0.0).astype(jnp.bfloat16)
    query_features_back = query_features_back + dense_product(
        "mtgjb,mbgf->mtgjf", similar_back, features_window
    )
    features_window_back = dense_product("mtgjb,mtgjf->mbgf", similar_back, feature_groups)
    queries_back = dense_product("mtgjb,mbgd->mtgjd", scores_back, keys_window) * scale
    keys_window_back = dense_product("mtgjb,mtgjd->mbgd", scores_back, grouped_queries) * scale
    usable_lead = usable.astype(jnp.float32)[:, :, None, None]
    values_lead = values_window[:, :rows].astype(jnp.float32)
    features_lead = features_window[:, :rows].astype(jnp.float32)
    features_lead_back = usable_lead * (
        exact_result("mbgd,mgfd->mbgf", values_lead, later_state) + later_norm[:, None]
    )
    values_lead_back = usable_lead * exact_result("mbgf,mgfd->mbgd", features_lead, later_state)
    returning = jnp.concatenate(
        [
            keys_window_back[:, :WIN],
            values_window_back[:, :WIN] + values_lead_back[:, :WIN],
            features_window_back[:, :WIN] + features_lead_back[:, :WIN],
        ],
        axis=-1,
    )
    arriving = neighbour_tail(returning.astype(jnp.bfloat16), -1).astype(jnp.float32)

    def gathered_back(window_back, lead_back, arrived):
        late = window_back[:, rows:] + arrived
        early = window_back[:, WIN:rows]
        if lead_back is not None:
            early = early + lead_back[:, WIN:]
        return jnp.concatenate([early, late], axis=1)

    keys_back = gathered_back(keys_window_back, None, arriving[..., :head_width])
    values_back = gathered_back(
        values_window_back, values_lead_back, arriving[..., head_width : 2 * head_width]
    )
    key_features_back = gathered_back(
        features_window_back, features_lead_back, arriving[..., 2 * head_width :]
    )
    key_logits_back = hedgehog_back(key_logits, key_features_back).astype(jnp.bfloat16)
    query_logits_back = hedgehog_back(
        query_logits, query_features_back.reshape(micro, rows, heads_here, feature_width)
    ).astype(jnp.bfloat16)
    key_feature_delta = dense_product("mthd,mthe->hde", key_rows, key_logits_back)
    query_feature_delta = dense_product("mthd,mthe->hde", query_rows, query_logits_back)
    keys_back = keys_back + dense_product("mthe,hde->mthd", key_logits_back, key_feature_layer)
    queries_back = queries_back.reshape(micro, rows, heads_here, head_width) + dense_product(
        "mthe,hde->mthd", query_logits_back, query_feature
    )
    projected_back = jnp.concatenate(
        [
            apply_rotation(queries_back, cosine_table, -sine_table)
            .astype(jnp.bfloat16)
            .reshape(micro, rows, query_width),
            apply_rotation(keys_back, cosine_table, -sine_table)
            .astype(jnp.bfloat16)
            .reshape(micro, rows, key_width),
            values_back.astype(jnp.bfloat16).reshape(micro, rows, key_width),
        ],
        axis=-1,
    )
    lift_all = ADAPTER_SCALE * dense_product("mtk,rk->mtr", projected_back, expand_all)
    project_delta = scatter_rows(dense_product("mtc,mtk->ck", normed_input, projected_back))
    expand_delta = ADAPTER_SCALE * exact_result(
        "mtr,mtk->rk", shrunk, projected_back.astype(jnp.float32)
    )
    shrink_delta = exact_result("mtc,mtr->cr", normed_input.astype(jnp.float32), lift_all)
    normed_back = dense_product("mtk,ck->mtc", projected_back, project_full) + exact_result(
        "mtr,cr->mtc", lift_all, shrink_all.astype(jnp.float32)
    )
    in_norm_back = sum_cores(normed_back, 1)
    down_rows, middle_late, in_norm_back = lax.optimization_barrier(
        (down_rows, middle, in_norm_back)
    )
    results = middle_late + down_rows
    attn_gain_delta = jnp.sum(in_norm_back * rows_in * scale_in, axis=(0, 1))
    inputs_back = middle_back.reshape(micro, piece, width) + norm_back(
        in_norm_back, rows_in, scale_in, gain_in
    )
    split, shared = total_small(
        (
            expand_delta[:rank, :query_width],
            expand_delta[rank : 2 * rank, query_width : query_width + key_width],
            expand_delta[2 * rank :, query_width + key_width :],
            out_shrink_delta,
            query_feature_delta,
            key_feature_delta,
        ),
        (attn_gain_delta, shrink_delta, output_second_delta, mlp_gain_delta),
    )
    return (
        results.astype(jnp.bfloat16).reshape(micro, piece, width),
        inputs_back,
        shared[0],
        project_delta[:, :query_width],
        project_delta[:, query_width : query_width + key_width],
        project_delta[:, query_width + key_width :],
        out_delta,
        shared[1][:, :rank],
        beside(split[0]),
        shared[1][:, rank : 2 * rank],
        beside(split[1]),
        shared[1][:, 2 * rank :],
        beside(split[2]),
        split[3].reshape(-1, rank),
        shared[2],
        split[4].reshape(-1, head_width, head_width),
        split[5].reshape(-1, head_width, head_width),
        shared[3],
        gate_delta,
        up_delta,
        down_delta,
    )


def solution(mesh):
    return jax.shard_map(
        per_device,
        mesh=mesh,
        in_specs=(
            P(None, ("seq", "tp"), None),
            P(None, ("seq", "tp"), None),
            P(),
            P("seq", "tp"),
            P("seq", "tp"),
            P("seq", "tp"),
            P("seq", "tp"),
            P(),
            P(None, "tp"),
            P(),
            P(None, "tp"),
            P(),
            P(None, "tp"),
            P("tp", None),
            P(),
            P("tp", None, None),
            P("tp", None, None),
            P(),
            P("seq", "tp"),
            P("seq", "tp"),
            P("seq", "tp"),
        ),
        out_specs=(
            P(None, ("seq", "tp"), None),
            P(None, ("seq", "tp"), None),
            P(),
            P("seq", "tp"),
            P("seq", "tp"),
            P("seq", "tp"),
            P("seq", "tp"),
            P(),
            P(),
            P(),
            P(),
            P(),
            P(),
            P(),
            P(),
            P(),
            P(),
            P(),
            P("seq", "tp"),
            P("seq", "tp"),
            P("seq", "tp"),
        ),
        check_vma=False,
    )
```

```python
import math

import jax
import jax.numpy as jnp
from jax import lax
from jax.sharding import PartitionSpec as P

WIN = 64


EPS = 1e-05
ADAPTER_SCALE = 2.0
ROPE_BASE = 500000.0

PLANE = 4
CHUNKS = 4


def dense_product(form, left, right):
    return jnp.einsum(form, left, right, preferred_element_type=jnp.float32)


def halves(value, axis=-1):
    high = lax.reduce_precision(value, 8, 7)
    return jnp.concatenate(
        [high.astype(jnp.bfloat16), (value - high).astype(jnp.bfloat16)], axis=axis
    )


def folded(value):
    size = value.shape[-1] // 2
    return value[..., :size] + value[..., size:]


def root_scale(value_rows):
    return lax.rsqrt(jnp.mean(value_rows * value_rows, axis=-1, keepdims=True) + EPS)


def norm_back(grad_normed, value_rows, scale, gain):
    gained = grad_normed * gain
    inner = jnp.mean(gained * value_rows, axis=-1, keepdims=True)
    return scale * gained - value_rows * (scale * scale * scale) * inner


def rotary_tables(positions, width):
    half = width // 2
    inverse = ROPE_BASE ** (-(jnp.arange(half, dtype=jnp.float32) * (2.0 / width)))
    angles = positions.astype(jnp.float32)[:, None] * inverse[None, :]
    return (jnp.cos(angles), jnp.sin(angles))


def apply_rotation(value_rows, cosine_table, sine_table):
    half = value_rows.shape[-1] // 2
    first = value_rows[..., :half]
    second = value_rows[..., half:]
    return jnp.concatenate(
        [first * cosine_table - second * sine_table, second * cosine_table + first * sine_table],
        axis=-1,
    )


def both_softmax(logits):
    return (jax.nn.softmax(logits, axis=-1), jax.nn.softmax(-logits, axis=-1))


def both_softmax_back(plus, minus, grads):
    width = plus.shape[-1]
    grad_plus = grads[..., :width]
    grad_minus = grads[..., width:]
    return plus * (grad_plus - jnp.sum(grad_plus * plus, axis=-1, keepdims=True)) - minus * (
        grad_minus - jnp.sum(grad_minus * minus, axis=-1, keepdims=True)
    )


def after(value, *earlier):
    return lax.optimization_barrier((value,) + earlier)[0]


def plane_count():
    return lax.axis_size("seq") // PLANE


def my_plane():
    return lax.axis_index("seq") // PLANE


def my_place():
    return lax.axis_index("seq") % PLANE


def swapped(value):
    return lax.ppermute(value, "tp", [(0, 1), (1, 0)])


def opposite(value, bit):
    return lax.ppermute(value, "seq", [(i, i ^ bit) for i in range(lax.axis_size("seq"))])


def from_plane_before(value, by):
    size = lax.axis_size("seq")
    return lax.ppermute(value, "seq", [(i, (i + by * PLANE) % size) for i in range(size)])


def in_order(mine, other, upper, axis):
    return jnp.stack([jnp.where(upper, other, mine), jnp.where(upper, mine, other)], axis=axis)


def split_half(value, upper, axis):
    index = upper.astype(jnp.int32)
    return (
        lax.dynamic_index_in_dim(value, index, axis, False),
        lax.dynamic_index_in_dim(value, 1 - index, axis, False),
    )


def upper_bit(bit):
    return (my_place() & bit) > 0


def upper_core():
    return lax.axis_index("tp") > 0


def gather_plane(own):
    micro, piece, width = own.shape
    parts = []
    for part in range(micro):
        value = own[part]
        if part % 2 == 0:
            value = in_order(value, opposite(value, 1), upper_bit(1), 0)
            value = in_order(value, opposite(value, 2), upper_bit(2), 0)
        else:
            value = in_order(value, opposite(value, 2), upper_bit(2), 0)
            value = in_order(value, opposite(value, 1), upper_bit(1), 1)
        parts.append(value.reshape(PLANE, piece, width))
    rows = jnp.stack(parts)
    rows = in_order(rows, swapped(rows), upper_core(), 2)
    return rows.reshape(micro, PLANE, 2 * piece, width)


def sum_plane(partial):
    micro, places, rows, width = partial.shape
    keep, send = split_half(
        partial.reshape(micro, places, 2, rows // 2, width), upper_core(), 2
    )
    summed = (keep + swapped(send)).reshape(micro, 2, 2, rows // 2, width)
    parts = []
    for part in range(micro):
        value = summed[part]
        for bit, axis in ((1, 1), (2, 0)) if part % 2 == 0 else ((2, 0), (1, 0)):
            keep, send = split_half(value, upper_bit(bit), axis)
            value = keep + opposite(send.astype(jnp.bfloat16), bit).astype(jnp.float32)
        parts.append(value)
    return jnp.stack(parts)


def place_groups():
    chips = lax.axis_size("seq")
    return [list(range(first, first + PLANE)) for first in range(0, chips, PLANE)]


def column_groups():
    chips = lax.axis_size("seq")
    return [list(range(place, chips, PLANE)) for place in range(PLANE)]


def exchange_plane(pieces):
    return lax.all_to_all(
        pieces, "seq", 0, 0, tiled=True, axis_index_groups=place_groups()
    )


def stack_planes(value):
    planes = plane_count()
    whole = jnp.zeros((planes,) + value.shape, value.dtype)
    whole = lax.dynamic_update_index_in_dim(whole, value, my_plane(), 0)
    for by in range(1, planes):
        whole = lax.dynamic_update_index_in_dim(
            whole, from_plane_before(value, by), (my_plane() - by) % planes, 0
        )
    return whole


def return_heads(delta):
    planes = plane_count()
    blocks = delta.astype(jnp.bfloat16).reshape(planes, -1, delta.shape[1])
    total = lax.dynamic_index_in_dim(blocks, my_plane(), 0, False).astype(jnp.float32)
    for by in range(1, planes):
        send = lax.dynamic_index_in_dim(blocks, (my_plane() - by) % planes, 0, False)
        total = total + from_plane_before(send, planes - by).astype(jnp.float32)
    pieces = exchange_plane(
        total.astype(jnp.bfloat16).reshape(PLANE, -1, delta.shape[1])
    )
    return pieces.swapaxes(0, 1).astype(jnp.float32)


def sums_around(states, later):
    micro = states.shape[0]
    planes = plane_count()
    total = jnp.sum(states, axis=1).astype(jnp.bfloat16)
    pieces = jnp.stack([total] + [from_plane_before(total, by) for by in range(1, planes)])
    source = (my_plane() - jnp.arange(planes)) % planes
    part = jnp.arange(micro)
    if later:
        beside = source[:, None, None] > my_plane()
        beyond = part[None, :, None] > part[None, None, :]
    else:
        beside = source[:, None, None] < my_plane()
        beyond = part[None, :, None] < part[None, None, :]
    same = part[None, :, None] == part[None, None, :]
    chosen = jnp.logical_or(beyond, jnp.logical_and(same, beside)).astype(jnp.bfloat16)
    outer = dense_product("kab,karl->brl", chosen, pieces)
    running = outer
    sums = [None] * PLANE
    for place in reversed(range(PLANE)) if later else range(PLANE):
        sums[place] = running
        running = running + states[:, place]
    return jnp.stack(sums, axis=1)


def windows(arrived, blocks):
    rows = blocks.shape[2]
    tails = jnp.concatenate([arrived[:, None], blocks[:, :-1, rows - WIN :]], axis=1)
    return jnp.concatenate([tails, blocks], axis=2)


def gather_relative(value, flip):
    blocks = jnp.stack(
        [value] + [from_plane_before(value, by) for by in range(1, plane_count())]
    )
    for bit in (1, 2) if flip else (2, 1):
        blocks = jnp.stack([blocks, opposite(blocks, bit)])
    return blocks.reshape((-1,) + value.shape)


def scatter_relative(partial, flip):
    planes = plane_count()
    value = partial.reshape((2, 2, planes) + partial.shape[1:])
    for bit in (2, 1) if flip else (1, 2):
        value = value[0].astype(jnp.float32) + opposite(
            value[1].astype(jnp.bfloat16), bit
        ).astype(jnp.float32)
    total = value[0]
    for by in range(1, planes):
        total = total + from_plane_before(
            value[by].astype(jnp.bfloat16), planes - by
        ).astype(jnp.float32)
    return total


def source_chips(flip):
    planes = plane_count()
    outer, inner = (2, 1) if flip else (1, 2)
    index = jnp.arange(4 * planes)
    plane = (my_plane() - index % planes) % planes
    place = my_place() ^ ((index // planes % 2) * inner) ^ ((index // (2 * planes)) * outer)
    return plane * PLANE + place


def relative_places(flip):
    planes = plane_count()
    outer, inner = (2, 1) if flip else (1, 2)
    chip = jnp.arange(4 * planes)
    back = (my_plane() - chip // PLANE) % planes
    apart = my_place() ^ (chip % PLANE)
    return (apart // outer % 2) * 2 * planes + (apart // inner % 2) * planes + back


def picked(blocks, places):
    return jnp.stack(
        [
            lax.dynamic_index_in_dim(blocks, places[index], 0, False)
            for index in range(blocks.shape[0])
        ]
    )


def exchange(value):
    return lax.all_to_all(value, "seq", 0, 0, tiled=True)


def gather_hidden(locals_):
    chips = lax.axis_size("seq")
    rows, hidden = locals_[0].shape
    pieces = jnp.stack(
        [local.reshape(rows, chips, hidden // chips).swapaxes(0, 1) for local in locals_], axis=1
    )
    mine = exchange(pieces)
    other = swapped(mine)
    upper = upper_core()
    return tuple(
        in_order(mine[:, index], other[:, index], upper, 2).reshape(
            chips * rows, 2 * (hidden // chips)
        )
        for index in range(len(locals_))
    )


def return_hidden(deltas):
    chips = lax.axis_size("seq")
    pieces = []
    for delta in deltas:
        rows, hidden = delta.shape
        core = lax.axis_index("tp")
        keep = lax.dynamic_slice_in_dim(delta, core * (hidden // 2), hidden // 2, 1)
        send = lax.dynamic_slice_in_dim(delta, (1 - core) * (hidden // 2), hidden // 2, 1)
        total = (keep + swapped(send)).astype(jnp.bfloat16)
        pieces.append(total.reshape(chips, rows // chips, hidden // 2))
    back = exchange(jnp.stack(pieces, axis=1))
    return tuple(
        back[:, index].swapaxes(0, 1).reshape(back.shape[2], -1).astype(jnp.float32)
        for index in range(len(deltas))
    )


def gather_positions(rows):
    return lax.all_gather(rows, "seq", axis=0, tiled=True)


def sum_positions(partial):
    return lax.psum_scatter(partial, "seq", scatter_dimension=0, tiled=True)


def total_small(split, shared):
    chips = lax.axis_size("seq")
    cores = lax.axis_size("tp")
    unit = 128 * chips * 8
    flat_split = jnp.concatenate([part.reshape(-1) for part in split])
    own = flat_split.shape[0]
    placed = lax.dynamic_update_index_in_dim(
        jnp.zeros((PLANE, own), jnp.float32), flat_split, my_place(), 0
    ).reshape(-1)
    flat_shared = jnp.concatenate([part.reshape(-1) for part in shared])
    flat_shared = jnp.pad(flat_shared, (0, -flat_shared.shape[0] % (cores * 128)))
    keep, send = split_half(flat_shared.reshape(cores, -1), upper_core(), 0)
    both = jnp.concatenate([placed, keep + swapped(send)])
    length = both.shape[0]
    both = jnp.pad(both, (0, -length % unit)).reshape(chips, -1, 128)
    mine = jnp.sum(exchange(both), axis=0)
    whole = exchange(jnp.broadcast_to(mine[None], both.shape)).reshape(-1)
    whole = in_order(whole, swapped(whole), upper_core(), 0)[:, :length]
    heads = whole[:, : PLANE * own].reshape(cores, PLANE, own)
    split_out = []
    start = 0
    for part in split:
        split_out.append(
            heads[:, :, start : start + part.size].reshape((cores, PLANE) + part.shape)
        )
        start += part.size
    joined = whole[:, PLANE * own :].reshape(-1)
    shared_out = []
    start = 0
    for part in shared:
        shared_out.append(joined[start : start + part.size].reshape(part.shape))
        start += part.size
    return (split_out, shared_out)


def along_columns(parts):
    return parts.transpose(2, 0, 1, 3).reshape(parts.shape[2], -1)


def my_columns(value, axis):
    size = value.shape[axis] // PLANE
    return lax.dynamic_slice_in_dim(value, my_place() * size, size, axis)


def by_place(value):
    return value.reshape(value.shape[0], PLANE, -1).swapaxes(0, 1)


def per_device(
    inputs,
    cotangent,
    attn_gain,
    query_matrix,
    key_matrix,
    value_matrix,
    output_matrix,
    query_first_factor,
    query_second_factor,
    key_first_factor,
    key_second_factor,
    value_first_factor,
    value_second_factor,
    output_first_factor,
    output_second_factor,
    query_feature,
    key_feature_layer,
    mlp_gain,
    gate_weight,
    up_weight,
    down_weight,
):
    micro, piece, width = inputs.shape
    chips = lax.axis_size("seq")
    rows = piece * lax.axis_size("tp")
    span = rows * chips
    head_width = query_feature.shape[1]
    group_size = query_feature.shape[0] // key_feature_layer.shape[0]
    rank = query_first_factor.shape[1]
    scale = 1.0 / math.sqrt(head_width)
    query_width = query_matrix.shape[1] // PLANE
    heads = query_width // head_width
    own = micro * piece
    blocks = micro * PLANE
    gain_in = attn_gain.astype(jnp.float32)
    gain_mid = mlp_gain.astype(jnp.float32)
    shrink_all = jnp.concatenate([query_first_factor, key_first_factor, value_first_factor], axis=1)
    expand_all = jnp.zeros((3 * rank, query_width + 2 * head_width), jnp.bfloat16)
    expand_all = expand_all.at[:rank, :query_width].set(my_columns(query_second_factor, 1))
    expand_all = expand_all.at[rank : 2 * rank, query_width : query_width + head_width].set(
        my_columns(key_second_factor, 1)
    )
    expand_all = expand_all.at[2 * rank :, query_width + head_width :].set(
        my_columns(value_second_factor, 1)
    )
    query_map = my_columns(query_feature, 0)
    key_map = my_columns(key_feature_layer, 0)[0]
    first_factor = my_columns(output_first_factor, 0)
    second_twice = output_second_factor * jnp.bfloat16(ADAPTER_SCALE)

    pieces = exchange_plane(
        jnp.concatenate(
            [
                by_place(query_matrix),
                by_place(key_matrix),
                by_place(value_matrix),
                by_place(output_matrix),
            ],
            axis=2,
        )
    )
    joined = query_width + 2 * head_width
    project_here = stack_planes(pieces[:, :, :joined].reshape(-1, joined)).reshape(width, joined)
    rows_in = inputs.astype(jnp.float32)
    scale_in = root_scale(rows_in)
    normed_input = gather_plane((rows_in * scale_in * gain_in).astype(jnp.bfloat16))
    project_here, normed_input = lax.optimization_barrier((project_here, normed_input))
    output_here = lax.all_gather(
        after(pieces[:, :, joined:].reshape(-1, query_width), project_here),
        "seq",
        axis=0,
        tiled=True,
        axis_index_groups=column_groups(),
    )
    cotangent_rows = cotangent.reshape(own, width)
    cotangent_all = gather_positions(after(cotangent_rows, project_here))
    gate_here, up_here, down_here = gather_hidden((gate_weight, up_weight, down_weight))

    normed_flat = normed_input.reshape(blocks * rows, width)
    extended = dense_product(
        "tc,ck->tk", normed_flat, jnp.concatenate([project_here, shrink_all], axis=1)
    )
    shrunk = extended[:, joined:]
    shrunk_parts = halves(shrunk)
    expand_twice = expand_all * jnp.bfloat16(ADAPTER_SCALE)
    projected = extended[:, :joined] + dense_product(
        "tr,rk->tk", shrunk_parts, jnp.concatenate([expand_twice, expand_twice], axis=0)
    )
    positions = (
        jnp.arange(micro, dtype=jnp.int32)[:, None] * span
        + my_plane() * (PLANE * rows)
        + jnp.arange(PLANE * rows, dtype=jnp.int32)[None, :]
    )
    cosine_table, sine_table = rotary_tables(positions.reshape(-1), head_width)
    cosine_table = cosine_table.reshape(blocks, rows, -1)
    sine_table = sine_table.reshape(blocks, rows, -1)
    projected = projected.reshape(blocks, rows, joined)
    query_rows = apply_rotation(
        projected[..., :query_width].reshape(blocks, rows, heads, head_width),
        cosine_table[:, :, None],
        sine_table[:, :, None],
    ).astype(jnp.bfloat16)
    key_rows = apply_rotation(
        projected[..., query_width : query_width + head_width], cosine_table, sine_table
    ).astype(jnp.bfloat16)
    value_rows = projected[..., query_width + head_width :].astype(jnp.bfloat16)
    key_plus, key_minus = both_softmax(dense_product("ntd,de->nte", key_rows, key_map))
    key_features = jnp.concatenate([key_plus, key_minus], axis=-1).astype(jnp.bfloat16)
    carried = jnp.concatenate([key_rows, value_rows, key_features], axis=-1).reshape(
        micro, PLANE, rows, -1
    )
    arrived = from_plane_before(carried[:, -1, rows - WIN :], 1)
    wrapped = jnp.concatenate([jnp.zeros_like(arrived[:1]), arrived[:-1]], axis=0)
    arrived = jnp.where(my_plane() == 0, wrapped, arrived)
    window = windows(arrived, carried).reshape(blocks, WIN + rows, -1)
    keys_window = window[..., :head_width]
    values_window = window[..., head_width : 2 * head_width]
    features_window = window[..., 2 * head_width :]
    usable = jnp.logical_or(jnp.arange(blocks) > 0, my_plane() > 0)
    usable_lead = jnp.logical_or(jnp.arange(rows)[None] >= WIN, usable[:, None])[..., None]
    live = jnp.where(usable_lead, features_window[:, :rows], jnp.bfloat16(0))
    ones = jnp.ones((blocks, rows, 1), jnp.bfloat16)
    values_one = jnp.concatenate([values_window[:, :rows], ones], axis=-1)
    states = dense_product("nbd,nbf->ndf", values_one, live)
    prior = sums_around(states.reshape((micro, PLANE) + states.shape[1:]), False)
    prior = halves(prior.reshape(states.shape), 1)
    query_plus, query_minus = both_softmax(
        dense_product("nthd,hde->nthe", query_rows, query_map)
    )
    query_features = jnp.concatenate([query_plus, query_minus], axis=-1).astype(jnp.bfloat16)
    query_pos = lax.broadcasted_iota(jnp.int32, (rows, rows + WIN), 0)
    key_pos = lax.broadcasted_iota(jnp.int32, (rows, rows + WIN), 1)
    open_keys = jnp.logical_or(key_pos[None] >= WIN, usable[:, None, None])
    linear_mask = jnp.logical_and((key_pos <= query_pos)[None], open_keys)[:, :, None]
    window_mask = jnp.logical_and(
        jnp.logical_and(key_pos > query_pos, key_pos <= query_pos + WIN)[None], open_keys
    )[:, :, None]
    scores = dense_product("nthd,nbd->nthb", query_rows, keys_window) * scale
    similar = dense_product("nthf,nbf->nthb", query_features, features_window)
    exponent = jnp.where(window_mask, jnp.exp(scores), 0.0)
    weights_all = exponent + jnp.where(linear_mask, similar, 0.0)
    prior_rows = dense_product("nthf,nkf->nthk", query_features, prior)
    prior_rows = folded(prior_rows)
    divisor = jnp.sum(weights_all, axis=-1, keepdims=True) + prior_rows[..., head_width:]
    inverse = 1.0 / divisor
    ratio = weights_all * inverse
    shares = ratio.astype(jnp.bfloat16)
    prior_out = prior_rows[..., :head_width] * inverse
    mixed = (
        (dense_product("nthb,nbd->nthd", shares, values_window) + prior_out)
        .astype(jnp.bfloat16)
        .reshape(blocks * rows, query_width)
    )
    low_rank = dense_product("tc,cr->tr", mixed, first_factor)
    low_parts = halves(low_rank)
    mixed_low = jnp.concatenate([mixed, low_parts], axis=1)
    branch = dense_product(
        "ta,wa->tw",
        mixed_low,
        jnp.concatenate([output_here, second_twice.T, second_twice.T], axis=1),
    )
    middle = (rows_in + sum_plane(branch.reshape(micro, PLANE, rows, width))).reshape(own, width)
    scale_mid = root_scale(middle)

    normed_own = (middle * scale_mid * gain_mid).astype(jnp.bfloat16)
    step = own // CHUNKS
    active_back = dense_product("td,df->tf", cotangent_all, down_here)
    active_back = active_back.reshape(chips, CHUNKS, step, -1)
    gathered, gates, uppers, actives, returned = [], [], [], [], []
    for chunk in range(CHUNKS):
        flip = chunk % 2 == 1
        mine = normed_own[chunk * step : (chunk + 1) * step]
        if chunk >= 2:
            mine = after(mine, gathered[chunk - 2])
        whole = gather_relative(mine, flip).reshape(chips * step, width)
        gathered.append(whole)
        gate = dense_product("tc,cf->tf", whole, gate_here)
        upper = dense_product("tc,cf->tf", whole, up_here)
        logistic = jax.nn.sigmoid(gate)
        active = (gate * logistic * upper).astype(jnp.bfloat16)
        back = picked(active_back[:, chunk], source_chips(flip))
        back = back.reshape(chips * step, -1)
        gate_back = (back * upper * logistic * (1.0 + gate * (1.0 - logistic))).astype(
            jnp.bfloat16
        )
        upper_back = (back * gate * logistic).astype(jnp.bfloat16)
        partial = (
            dense_product("tf,cf->tc", gate_back, gate_here)
            + dense_product("tf,cf->tc", upper_back, up_here)
        )
        returned.append(scatter_relative(partial.reshape(chips, step, width), flip))
        gates.append(gate_back)
        uppers.append(upper_back)
        actives.append(
            picked(active.reshape(chips, step, -1), relative_places(flip))
        )
    normed_all = jnp.concatenate(gathered)
    active_all = jnp.stack(actives, axis=1).reshape(chips * own, -1)
    mid_norm_back, gate_delta, up_delta, down_delta = lax.optimization_barrier(
        (
            jnp.concatenate(returned),
            dense_product("tc,tf->cf", normed_all, jnp.concatenate(gates)),
            dense_product("tc,tf->cf", normed_all, jnp.concatenate(uppers)),
            dense_product("td,tf->df", cotangent_all, active_all),
        )
    )
    down_rows = sum_positions(
        after(
            dense_product("tf,df->td", active_all, down_here).astype(jnp.bfloat16), mid_norm_back
        )
    )
    gate_delta, up_delta, down_delta = return_hidden((gate_delta, up_delta, down_delta))

    mlp_gain_delta = jnp.sum(mid_norm_back * middle * scale_mid, axis=0)
    middle_back = cotangent_rows.astype(jnp.float32) + norm_back(
        mid_norm_back, middle, scale_mid, gain_mid
    )
    branch_back = gather_plane(middle_back.astype(jnp.bfloat16).reshape(micro, piece, width))
    branch_back = branch_back.reshape(blocks * rows, width)
    extended_back = dense_product(
        "td,dk->tk", branch_back, jnp.concatenate([output_here, second_twice.T], axis=1)
    )
    lifted = extended_back[:, query_width:]
    lifted_parts = halves(lifted)
    first_pair = jnp.concatenate([first_factor, first_factor], axis=1)
    mixed_back = extended_back[:, :query_width] + dense_product(
        "tr,cr->tc", lifted_parts, first_pair
    )
    out_full = dense_product("td,tc->dc", branch_back, mixed_low)
    out_delta = return_heads(out_full[:, :query_width])
    output_second_delta = ADAPTER_SCALE * folded(out_full[:, query_width:]).T
    out_shrink_delta = folded(dense_product("tc,tr->cr", mixed, lifted_parts))
    heads_back = mixed_back.astype(jnp.bfloat16).reshape(blocks, rows, heads, head_width)
    shares_back = dense_product("nthd,nbd->nthb", heads_back, values_window)
    values_window_back = dense_product("nthb,nthd->nbd", shares, heads_back)
    heads_exact = heads_back.astype(jnp.float32)
    divisor_back = (
        -(
            jnp.sum(shares_back * ratio, axis=-1, keepdims=True)
            + jnp.sum(heads_exact * prior_out, axis=-1, keepdims=True)
        )
        * inverse
    )
    scaled_back = jnp.concatenate([heads_exact * inverse, divisor_back], axis=-1).astype(
        jnp.bfloat16
    )
    states_back = dense_product("nthk,nthf->nkf", scaled_back, query_features)
    later = sums_around(states_back.reshape((micro, PLANE) + states_back.shape[1:]), True)
    later = halves(later.reshape(states_back.shape), 1)
    weights_back = shares_back * inverse + divisor_back
    scores_back = jnp.where(window_mask, weights_back * exponent, 0.0).astype(jnp.bfloat16)
    similar_back = jnp.where(linear_mask, weights_back, 0.0).astype(jnp.bfloat16)
    size = head_width + 1
    prior_state = prior[:, :head_width]
    prior_rest = prior[:, size : size + head_width]
    prior_norm = prior[:, head_width].astype(jnp.float32) + prior[:, size + head_width].astype(
        jnp.float32
    )
    query_features_back = (
        (
            dense_product("nthd,ndf->nthf", heads_back, prior_state)
            + dense_product("nthd,ndf->nthf", heads_back, prior_rest)
        )
        * inverse
        + divisor_back * prior_norm[:, None, None, :]
        + dense_product("nthb,nbf->nthf", similar_back, features_window)
    )
    features_window_back = dense_product("nthb,nthf->nbf", similar_back, query_features)
    queries_back = dense_product("nthb,nbd->nthd", scores_back, keys_window) * scale
    keys_window_back = dense_product("nthb,nthd->nbd", scores_back, query_rows) * scale
    features_lead_back = jnp.where(
        usable_lead,
        dense_product(
            "nbk,nkf->nbf", jnp.concatenate([values_one, values_one], axis=-1), later
        ),
        0.0,
    )
    values_lead_back = dense_product("nbf,nkf->nbk", live, later)
    values_lead_back = folded(values_lead_back)[..., :head_width]
    window_back = jnp.concatenate(
        [keys_window_back, values_window_back, features_window_back], axis=-1
    )
    lead_back = jnp.concatenate(
        [jnp.zeros_like(keys_window_back[:, :rows]), values_lead_back, features_lead_back], axis=-1
    )
    window_back = jnp.concatenate(
        [window_back[:, :rows] + lead_back, window_back[:, rows:]], axis=1
    ).reshape(micro, PLANE, WIN + rows, -1)
    planes = plane_count()
    arriving = from_plane_before(
        window_back[:, 0, :WIN].astype(jnp.bfloat16), planes - 1
    ).astype(jnp.float32)
    wrapped = jnp.concatenate([arriving[1:], jnp.zeros_like(arriving[:1])], axis=0)
    arriving = jnp.where(my_plane() == planes - 1, wrapped, arriving)
    following = jnp.concatenate([window_back[:, 1:, :WIN], arriving[:, None]], axis=1)
    carried_back = jnp.concatenate(
        [window_back[:, :, WIN:rows], window_back[:, :, rows:] + following], axis=2
    ).reshape(blocks, rows, -1)
    keys_back = carried_back[..., :head_width]
    values_back = carried_back[..., head_width : 2 * head_width]
    key_logits_back = both_softmax_back(
        key_plus, key_minus, carried_back[..., 2 * head_width :]
    ).astype(jnp.bfloat16)
    query_logits_back = both_softmax_back(query_plus, query_minus, query_features_back).astype(
        jnp.bfloat16
    )
    key_feature_delta = dense_product("ntd,nte->de", key_rows, key_logits_back)
    query_feature_delta = dense_product("nthd,nthe->hde", query_rows, query_logits_back)
    keys_back = keys_back + dense_product("nte,de->ntd", key_logits_back, key_map)
    queries_back = queries_back + dense_product("nthe,hde->nthd", query_logits_back, query_map)
    projected_back = jnp.concatenate(
        [
            apply_rotation(queries_back, cosine_table[:, :, None], -sine_table[:, :, None])
            .astype(jnp.bfloat16)
            .reshape(blocks * rows, query_width),
            apply_rotation(keys_back, cosine_table, -sine_table)
            .astype(jnp.bfloat16)
            .reshape(blocks * rows, head_width),
            values_back.astype(jnp.bfloat16).reshape(blocks * rows, head_width),
        ],
        axis=-1,
    )
    lift_all = dense_product("tk,rk->tr", projected_back, expand_twice)
    back_low = jnp.concatenate([projected_back, halves(lift_all)], axis=1)
    project_full = dense_product("tc,tk->ck", normed_flat, back_low)
    project_delta = return_heads(project_full[:, :joined])
    shrink_delta = folded(project_full[:, joined:])
    expand_delta = dense_product("tr,tk->rk", shrunk_parts, projected_back)
    expand_delta = ADAPTER_SCALE * (expand_delta[: 3 * rank] + expand_delta[3 * rank :])
    normed_back = dense_product(
        "tk,ck->tc",
        back_low,
        jnp.concatenate([project_here, shrink_all, shrink_all], axis=1),
    )
    in_norm_back = sum_plane(normed_back.reshape(micro, PLANE, rows, width))
    down_rows, middle_late, in_norm_back = lax.optimization_barrier(
        (down_rows, middle, in_norm_back)
    )
    results = middle_late + down_rows.astype(jnp.float32)
    attn_gain_delta = jnp.sum(in_norm_back * rows_in * scale_in, axis=(0, 1))
    inputs_back = middle_back.reshape(micro, piece, width) + norm_back(
        in_norm_back, rows_in, scale_in, gain_in
    )
    split, shared = total_small(
        (
            expand_delta[:rank, :query_width],
            expand_delta[rank : 2 * rank, query_width : query_width + head_width],
            expand_delta[2 * rank :, query_width + head_width :],
            out_shrink_delta,
            query_feature_delta,
            key_feature_delta,
        ),
        (attn_gain_delta, shrink_delta, output_second_delta, mlp_gain_delta),
    )
    return (
        results.astype(jnp.bfloat16).reshape(micro, piece, width),
        inputs_back,
        shared[0],
        project_delta[:, :, :query_width].reshape(-1, PLANE * query_width),
        project_delta[:, :, query_width : query_width + head_width].reshape(
            -1, PLANE * head_width
        ),
        project_delta[:, :, query_width + head_width :].reshape(-1, PLANE * head_width),
        out_delta.reshape(-1, PLANE * query_width),
        shared[1][:, :rank],
        along_columns(split[0]),
        shared[1][:, rank : 2 * rank],
        along_columns(split[1]),
        shared[1][:, 2 * rank :],
        along_columns(split[2]),
        split[3].reshape(-1, rank),
        shared[2],
        split[4].reshape(-1, head_width, head_width),
        split[5].reshape(-1, head_width, head_width),
        shared[3],
        gate_delta,
        up_delta,
        down_delta,
    )


def solution(mesh):
    return jax.shard_map(
        per_device,
        mesh=mesh,
        in_specs=(
            P(None, ("seq", "tp"), None),
            P(None, ("seq", "tp"), None),
            P(),
            P("seq", "tp"),
            P("seq", "tp"),
            P("seq", "tp"),
            P("seq", "tp"),
            P(),
            P(None, "tp"),
            P(),
            P(None, "tp"),
            P(),
            P(None, "tp"),
            P("tp", None),
            P(),
            P("tp", None, None),
            P("tp", None, None),
            P(),
            P("seq", "tp"),
            P("seq", "tp"),
            P("seq", "tp"),
        ),
        out_specs=(
            P(None, ("seq", "tp"), None),
            P(None, ("seq", "tp"), None),
            P(),
            P("seq", "tp"),
            P("seq", "tp"),
            P("seq", "tp"),
            P("seq", "tp"),
            P(),
            P(),
            P(),
            P(),
            P(),
            P(),
            P(),
            P(),
            P(),
            P(),
            P(),
            P("seq", "tp"),
            P("seq", "tp"),
            P("seq", "tp"),
        ),
        check_vma=False,
    )
```

```python
import math

import jax
import jax.numpy as jnp
from jax import lax
from jax.sharding import PartitionSpec as P

WIN = 64


EPS = 1e-05
ADAPTER_SCALE = 2.0
ROPE_BASE = 500000.0

PLANE = 4
CHUNKS = 4


def dense_product(form, left, right):
    return jnp.einsum(form, left, right, preferred_element_type=jnp.float32)


def halves(value, axis=-1):
    high = lax.reduce_precision(value, 8, 7)
    return jnp.concatenate(
        [high.astype(jnp.bfloat16), (value - high).astype(jnp.bfloat16)], axis=axis
    )


def folded(value):
    size = value.shape[-1] // 2
    return value[..., :size] + value[..., size:]


def root_scale(value_rows):
    return lax.rsqrt(jnp.mean(value_rows * value_rows, axis=-1, keepdims=True) + EPS)


def norm_back(grad_normed, value_rows, scale, gain):
    gained = grad_normed * gain
    inner = jnp.mean(gained * value_rows, axis=-1, keepdims=True)
    return scale * gained - value_rows * (scale * scale * scale) * inner


def rotary_tables(positions, width):
    half = width // 2
    inverse = ROPE_BASE ** (-(jnp.arange(half, dtype=jnp.float32) * (2.0 / width)))
    angles = positions.astype(jnp.float32)[:, None] * inverse[None, :]
    return (jnp.cos(angles), jnp.sin(angles))


def apply_rotation(value_rows, cosine_table, sine_table):
    half = value_rows.shape[-1] // 2
    first = value_rows[..., :half]
    second = value_rows[..., half:]
    return jnp.concatenate(
        [first * cosine_table - second * sine_table, second * cosine_table + first * sine_table],
        axis=-1,
    )


def both_softmax(logits):
    return (jax.nn.softmax(logits, axis=-1), jax.nn.softmax(-logits, axis=-1))


def both_softmax_back(plus, minus, grads):
    width = plus.shape[-1]
    grad_plus = grads[..., :width]
    grad_minus = grads[..., width:]
    return plus * (grad_plus - jnp.sum(grad_plus * plus, axis=-1, keepdims=True)) - minus * (
        grad_minus - jnp.sum(grad_minus * minus, axis=-1, keepdims=True)
    )


def after(value, *earlier):
    return lax.optimization_barrier((value,) + earlier)[0]


def plane_count():
    return lax.axis_size("seq") // PLANE


def my_plane():
    return lax.div(lax.axis_index("seq"), jnp.int32(PLANE))


def my_place():
    return lax.rem(lax.axis_index("seq"), jnp.int32(PLANE))


def plane_before(by):
    planes = plane_count()
    return lax.rem(my_plane() + jnp.int32(planes - by), jnp.int32(planes))


def at_block(blocks, index):
    return lax.dynamic_index_in_dim(blocks, index, 0, False, allow_negative_indices=False)


def swapped(value):
    return lax.ppermute(value, "tp", [(0, 1), (1, 0)])


def opposite(value, bit):
    return lax.ppermute(value, "seq", [(i, i ^ bit) for i in range(lax.axis_size("seq"))])


def from_plane_before(value, by):
    size = lax.axis_size("seq")
    return lax.ppermute(value, "seq", [(i, (i + by * PLANE) % size) for i in range(size)])


def in_order(mine, other, upper, axis):
    return jnp.stack([jnp.where(upper, other, mine), jnp.where(upper, mine, other)], axis=axis)


def split_half(value, upper, axis):
    index = upper.astype(jnp.int32)
    return (
        lax.dynamic_index_in_dim(value, index, axis, False, allow_negative_indices=False),
        lax.dynamic_index_in_dim(value, 1 - index, axis, False, allow_negative_indices=False),
    )


def upper_bit(bit):
    return (my_place() & bit) > 0


def upper_core():
    return lax.axis_index("tp") > 0


def gather_plane(own):
    micro, piece, width = own.shape
    parts = []
    for part in range(micro):
        value = own[part]
        if part % 2 == 0:
            value = in_order(value, opposite(value, 1), upper_bit(1), 0)
            value = in_order(value, opposite(value, 2), upper_bit(2), 0)
        else:
            value = in_order(value, opposite(value, 2), upper_bit(2), 0)
            value = in_order(value, opposite(value, 1), upper_bit(1), 1)
        parts.append(value.reshape(PLANE, piece, width))
    rows = jnp.stack(parts)
    rows = in_order(rows, swapped(rows), upper_core(), 2)
    return rows.reshape(micro, PLANE, 2 * piece, width)


def sum_plane(partial):
    micro, places, rows, width = partial.shape
    keep, send = split_half(
        partial.reshape(micro, places, 2, rows // 2, width), upper_core(), 2
    )
    summed = (keep + swapped(send)).reshape(micro, 2, 2, rows // 2, width)
    parts = []
    for part in range(micro):
        value = summed[part]
        for bit, axis in ((1, 1), (2, 0)) if part % 2 == 0 else ((2, 0), (1, 0)):
            keep, send = split_half(value, upper_bit(bit), axis)
            value = keep + opposite(send.astype(jnp.bfloat16), bit).astype(jnp.float32)
        parts.append(value)
    return jnp.stack(parts)


def place_groups():
    chips = lax.axis_size("seq")
    return [list(range(first, first + PLANE)) for first in range(0, chips, PLANE)]


def exchange_plane(pieces):
    return lax.all_to_all(
        pieces, "seq", 0, 0, tiled=True, axis_index_groups=place_groups()
    )


def stack_planes(value):
    planes = plane_count()
    whole = jnp.zeros((planes,) + value.shape, value.dtype)
    for by in range(planes):
        piece = from_plane_before(value, by) if by else value
        whole = lax.dynamic_update_slice_in_dim(
            whole, piece[None], plane_before(by), 0, allow_negative_indices=False
        )
    return whole


def return_heads(delta):
    planes = plane_count()
    blocks = delta.astype(jnp.bfloat16).reshape(planes, -1, delta.shape[1])
    total = at_block(blocks, my_plane()).astype(jnp.float32)
    for by in range(1, planes):
        send = at_block(blocks, plane_before(by))
        total = total + from_plane_before(send, planes - by).astype(jnp.float32)
    pieces = exchange_plane(
        total.astype(jnp.bfloat16).reshape(PLANE, -1, delta.shape[1])
    )
    return pieces.swapaxes(0, 1).astype(jnp.float32)


def sums_around(states, later):
    micro = states.shape[0]
    planes = plane_count()
    total = jnp.sum(states, axis=1).astype(jnp.bfloat16)
    pieces = jnp.stack([total] + [from_plane_before(total, by) for by in range(1, planes)])
    source = lax.rem(my_plane() + planes - jnp.arange(planes), jnp.int32(planes))
    part = jnp.arange(micro)
    if later:
        beside = source[:, None, None] > my_plane()
        beyond = part[None, :, None] > part[None, None, :]
    else:
        beside = source[:, None, None] < my_plane()
        beyond = part[None, :, None] < part[None, None, :]
    same = part[None, :, None] == part[None, None, :]
    chosen = jnp.logical_or(beyond, jnp.logical_and(same, beside)).astype(jnp.bfloat16)
    outer = dense_product("kab,karl->brl", chosen, pieces)
    running = outer
    sums = [None] * PLANE
    for place in reversed(range(PLANE)) if later else range(PLANE):
        sums[place] = running
        running = running + states[:, place]
    return jnp.stack(sums, axis=1)


def windows(arrived, blocks):
    rows = blocks.shape[2]
    tails = jnp.concatenate([arrived[:, None], blocks[:, :-1, rows - WIN :]], axis=1)
    return jnp.concatenate([tails, blocks], axis=2)


def gather_chips(value, flip):
    blocks = stack_planes(value)
    if flip:
        blocks = in_order(blocks, opposite(blocks, 1), upper_bit(1), 1)
        blocks = in_order(blocks, opposite(blocks, 2), upper_bit(2), 1)
    else:
        blocks = in_order(blocks, opposite(blocks, 2), upper_bit(2), 1)
        blocks = in_order(blocks, opposite(blocks, 1), upper_bit(1), 2)
    return blocks.reshape((-1,) + value.shape)


def scatter_chips(partial, flip):
    planes = plane_count()
    value = partial.reshape((planes, 2, 2) + partial.shape[1:])
    for bit, axis in ((2, 1), (1, 1)) if flip else ((1, 2), (2, 1)):
        keep, send = split_half(value, upper_bit(bit), axis)
        value = keep.astype(jnp.float32) + opposite(send.astype(jnp.bfloat16), bit).astype(
            jnp.float32
        )
    total = at_block(value, my_plane())
    for by in range(1, planes):
        send = at_block(value, plane_before(by)).astype(jnp.bfloat16)
        total = total + from_plane_before(send, planes - by).astype(jnp.float32)
    return total


def exchange(value):
    return lax.all_to_all(value, "seq", 0, 0, tiled=True)


def gather_hidden(locals_):
    chips = lax.axis_size("seq")
    rows, hidden = locals_[0].shape
    pieces = jnp.stack(
        [local.reshape(rows, chips, hidden // chips).swapaxes(0, 1) for local in locals_], axis=1
    )
    mine = exchange(pieces)
    other = swapped(mine)
    upper = upper_core()
    return tuple(
        in_order(mine[:, index], other[:, index], upper, 2).reshape(
            chips * rows, 2 * (hidden // chips)
        )
        for index in range(len(locals_))
    )


def return_hidden(deltas):
    chips = lax.axis_size("seq")
    pieces = []
    for delta in deltas:
        rows, hidden = delta.shape
        core = lax.axis_index("tp")
        keep, send = (
            lax.dynamic_slice_in_dim(
                delta, start * (hidden // 2), hidden // 2, 1, allow_negative_indices=False
            )
            for start in (core, 1 - core)
        )
        total = (keep + swapped(send)).astype(jnp.bfloat16)
        pieces.append(total.reshape(chips, rows // chips, hidden // 2))
    back = exchange(jnp.stack(pieces, axis=1))
    return tuple(
        back[:, index].swapaxes(0, 1).reshape(back.shape[2], -1).astype(jnp.float32)
        for index in range(len(deltas))
    )


def gather_positions(rows):
    return lax.all_gather(rows, "seq", axis=0, tiled=True)


def sum_positions(partial):
    return lax.psum_scatter(partial, "seq", scatter_dimension=0, tiled=True)


def total_small(split, shared):
    chips = lax.axis_size("seq")
    cores = lax.axis_size("tp")
    unit = 128 * chips * 8
    flat_split = jnp.concatenate([part.reshape(-1) for part in split])
    own = flat_split.shape[0]
    placed = lax.dynamic_update_slice_in_dim(
        jnp.zeros((PLANE, own), jnp.float32),
        flat_split[None],
        my_place(),
        0,
        allow_negative_indices=False,
    ).reshape(-1)
    flat_shared = jnp.concatenate([part.reshape(-1) for part in shared])
    flat_shared = jnp.pad(flat_shared, (0, -flat_shared.shape[0] % (cores * 128)))
    keep, send = split_half(flat_shared.reshape(cores, -1), upper_core(), 0)
    both = jnp.concatenate([placed, keep + swapped(send)])
    length = both.shape[0]
    both = jnp.pad(both, (0, -length % unit)).reshape(chips, -1, 128)
    mine = jnp.sum(exchange(both), axis=0)
    whole = exchange(jnp.broadcast_to(mine[None], both.shape)).reshape(-1)
    whole = in_order(whole, swapped(whole), upper_core(), 0)[:, :length]
    heads = whole[:, : PLANE * own].reshape(cores, PLANE, own)
    split_out = []
    start = 0
    for part in split:
        split_out.append(
            heads[:, :, start : start + part.size].reshape((cores, PLANE) + part.shape)
        )
        start += part.size
    joined = whole[:, PLANE * own :].reshape(-1)
    shared_out = []
    start = 0
    for part in shared:
        shared_out.append(joined[start : start + part.size].reshape(part.shape))
        start += part.size
    return (split_out, shared_out)


def along_columns(parts):
    return parts.transpose(2, 0, 1, 3).reshape(parts.shape[2], -1)


def my_columns(value, axis):
    size = value.shape[axis] // PLANE
    return lax.dynamic_slice_in_dim(
        value, my_place() * size, size, axis, allow_negative_indices=False
    )


def by_place(value):
    return value.reshape(value.shape[0], PLANE, -1).swapaxes(0, 1)


def per_device(
    inputs,
    cotangent,
    attn_gain,
    query_matrix,
    key_matrix,
    value_matrix,
    output_matrix,
    query_first_factor,
    query_second_factor,
    key_first_factor,
    key_second_factor,
    value_first_factor,
    value_second_factor,
    output_first_factor,
    output_second_factor,
    query_feature,
    key_feature_layer,
    mlp_gain,
    gate_weight,
    up_weight,
    down_weight,
):
    micro, piece, width = inputs.shape
    chips = lax.axis_size("seq")
    rows = piece * lax.axis_size("tp")
    span = rows * chips
    head_width = query_feature.shape[1]
    group_size = query_feature.shape[0] // key_feature_layer.shape[0]
    rank = query_first_factor.shape[1]
    scale = 1.0 / math.sqrt(head_width)
    query_width = query_matrix.shape[1] // PLANE
    heads = query_width // head_width
    own = micro * piece
    blocks = micro * PLANE
    gain_in = attn_gain.astype(jnp.float32)
    gain_mid = mlp_gain.astype(jnp.float32)
    shrink_all = jnp.concatenate([query_first_factor, key_first_factor, value_first_factor], axis=1)
    expand_all = jnp.zeros((3 * rank, query_width + 2 * head_width), jnp.bfloat16)
    expand_all = expand_all.at[:rank, :query_width].set(my_columns(query_second_factor, 1))
    expand_all = expand_all.at[rank : 2 * rank, query_width : query_width + head_width].set(
        my_columns(key_second_factor, 1)
    )
    expand_all = expand_all.at[2 * rank :, query_width + head_width :].set(
        my_columns(value_second_factor, 1)
    )
    query_map = my_columns(query_feature, 0)
    key_map = my_columns(key_feature_layer, 0)[0]
    first_factor = my_columns(output_first_factor, 0)
    second_twice = output_second_factor * jnp.bfloat16(ADAPTER_SCALE)

    pieces = exchange_plane(
        jnp.concatenate(
            [
                by_place(query_matrix),
                by_place(key_matrix),
                by_place(value_matrix),
                by_place(output_matrix),
            ],
            axis=2,
        )
    )
    joined = query_width + 2 * head_width
    project_here = stack_planes(pieces[:, :, :joined].reshape(-1, joined)).reshape(width, joined)
    rows_in = inputs.astype(jnp.float32)
    scale_in = root_scale(rows_in)
    normed_input = gather_plane((rows_in * scale_in * gain_in).astype(jnp.bfloat16))
    project_here, normed_input = lax.optimization_barrier((project_here, normed_input))
    output_here = stack_planes(
        after(pieces[:, :, joined:].reshape(-1, query_width), project_here)
    ).reshape(width, query_width)
    cotangent_rows = cotangent.reshape(own, width)
    cotangent_all = gather_positions(after(cotangent_rows, project_here))
    gate_here, up_here, down_here = gather_hidden((gate_weight, up_weight, down_weight))

    normed_flat = normed_input.reshape(blocks * rows, width)
    extended = dense_product(
        "tc,ck->tk", normed_flat, jnp.concatenate([project_here, shrink_all], axis=1)
    )
    shrunk = extended[:, joined:]
    shrunk_parts = halves(shrunk)
    expand_twice = expand_all * jnp.bfloat16(ADAPTER_SCALE)
    projected = extended[:, :joined] + dense_product(
        "tr,rk->tk", shrunk_parts, jnp.concatenate([expand_twice, expand_twice], axis=0)
    )
    positions = (
        jnp.arange(micro, dtype=jnp.int32)[:, None] * span
        + my_plane() * (PLANE * rows)
        + jnp.arange(PLANE * rows, dtype=jnp.int32)[None, :]
    )
    cosine_table, sine_table = rotary_tables(positions.reshape(-1), head_width)
    cosine_table = cosine_table.reshape(blocks, rows, -1)
    sine_table = sine_table.reshape(blocks, rows, -1)
    projected = projected.reshape(blocks, rows, joined)
    query_rows = apply_rotation(
        projected[..., :query_width].reshape(blocks, rows, heads, head_width),
        cosine_table[:, :, None],
        sine_table[:, :, None],
    ).astype(jnp.bfloat16)
    key_rows = apply_rotation(
        projected[..., query_width : query_width + head_width], cosine_table, sine_table
    ).astype(jnp.bfloat16)
    value_rows = projected[..., query_width + head_width :].astype(jnp.bfloat16)
    key_plus, key_minus = both_softmax(dense_product("ntd,de->nte", key_rows, key_map))
    key_features = jnp.concatenate([key_plus, key_minus], axis=-1).astype(jnp.bfloat16)
    carried = jnp.concatenate([key_rows, value_rows, key_features], axis=-1).reshape(
        micro, PLANE, rows, -1
    )
    arrived = from_plane_before(carried[:, -1, rows - WIN :], 1)
    wrapped = jnp.concatenate([jnp.zeros_like(arrived[:1]), arrived[:-1]], axis=0)
    arrived = jnp.where(my_plane() == 0, wrapped, arrived)
    window = windows(arrived, carried).reshape(blocks, WIN + rows, -1)
    keys_window = window[..., :head_width]
    values_window = window[..., head_width : 2 * head_width]
    features_window = window[..., 2 * head_width :]
    usable = jnp.logical_or(jnp.arange(blocks) > 0, my_plane() > 0)
    usable_lead = jnp.logical_or(jnp.arange(rows)[None] >= WIN, usable[:, None])[..., None]
    live = jnp.where(usable_lead, features_window[:, :rows], jnp.bfloat16(0))
    ones = jnp.ones((blocks, rows, 1), jnp.bfloat16)
    values_one = jnp.concatenate([values_window[:, :rows], ones], axis=-1)
    states = dense_product("nbd,nbf->ndf", values_one, live)
    prior = sums_around(states.reshape((micro, PLANE) + states.shape[1:]), False)
    prior, gate_here, up_here, down_here = lax.optimization_barrier(
        (prior, gate_here, up_here, down_here)
    )
    prior = halves(prior.reshape(states.shape), 1)
    query_plus, query_minus = both_softmax(
        dense_product("nthd,hde->nthe", query_rows, query_map)
    )
    query_features = jnp.concatenate([query_plus, query_minus], axis=-1).astype(jnp.bfloat16)
    query_pos = lax.broadcasted_iota(jnp.int32, (rows, rows + WIN), 0)
    key_pos = lax.broadcasted_iota(jnp.int32, (rows, rows + WIN), 1)
    open_keys = jnp.logical_or(key_pos[None] >= WIN, usable[:, None, None])
    linear_mask = jnp.logical_and((key_pos <= query_pos)[None], open_keys)[:, :, None]
    window_mask = jnp.logical_and(
        jnp.logical_and(key_pos > query_pos, key_pos <= query_pos + WIN)[None], open_keys
    )[:, :, None]
    scores = dense_product("nthd,nbd->nthb", query_rows, keys_window) * scale
    similar = dense_product("nthf,nbf->nthb", query_features, features_window)
    exponent = jnp.where(window_mask, jnp.exp(scores), 0.0)
    weights_all = exponent + jnp.where(linear_mask, similar, 0.0)
    prior_rows = dense_product("nthf,nkf->nthk", query_features, prior)
    prior_rows = folded(prior_rows)
    divisor = jnp.sum(weights_all, axis=-1, keepdims=True) + prior_rows[..., head_width:]
    inverse = 1.0 / divisor
    ratio = weights_all * inverse
    shares = ratio.astype(jnp.bfloat16)
    prior_out = prior_rows[..., :head_width] * inverse
    mixed = (
        (dense_product("nthb,nbd->nthd", shares, values_window) + prior_out)
        .astype(jnp.bfloat16)
        .reshape(blocks * rows, query_width)
    )
    mixed, cotangent_all = lax.optimization_barrier((mixed, cotangent_all))
    low_rank = dense_product("tc,cr->tr", mixed, first_factor)
    low_parts = halves(low_rank)
    mixed_low = jnp.concatenate([mixed, low_parts], axis=1)
    branch = dense_product(
        "ta,wa->tw",
        mixed_low,
        jnp.concatenate([output_here, second_twice.T, second_twice.T], axis=1),
    )
    middle = (rows_in + sum_plane(branch.reshape(micro, PLANE, rows, width))).reshape(own, width)
    scale_mid = root_scale(middle)

    normed_own = (middle * scale_mid * gain_mid).astype(jnp.bfloat16)
    step = own // CHUNKS
    active_back = dense_product("td,df->tf", cotangent_all, down_here)
    active_back = active_back.reshape(chips, CHUNKS, step, -1)
    gathered, gates, uppers, actives, returned = [], [], [], [], []
    for chunk in range(CHUNKS):
        flip = chunk % 2 == 1
        mine = normed_own[chunk * step : (chunk + 1) * step]
        if chunk >= 2:
            mine = after(mine, gathered[chunk - 2])
        whole = gather_chips(mine, flip).reshape(chips * step, width)
        gathered.append(whole)
        gate = dense_product("tc,cf->tf", whole, gate_here)
        upper = dense_product("tc,cf->tf", whole, up_here)
        logistic = jax.nn.sigmoid(gate)
        active = (gate * logistic * upper).astype(jnp.bfloat16)
        back = active_back[:, chunk].reshape(chips * step, -1)
        gate_back = (back * upper * logistic * (1.0 + gate * (1.0 - logistic))).astype(
            jnp.bfloat16
        )
        upper_back = (back * gate * logistic).astype(jnp.bfloat16)
        partial = (
            dense_product("tf,cf->tc", gate_back, gate_here)
            + dense_product("tf,cf->tc", upper_back, up_here)
        )
        returned.append(scatter_chips(partial.reshape(chips, step, width), flip))
        gates.append(gate_back)
        uppers.append(upper_back)
        actives.append(active.reshape(chips, step, -1))
    normed_all = jnp.concatenate(gathered)
    active_all = jnp.stack(actives, axis=1).reshape(chips * own, -1)
    mid_norm_back, gate_delta, up_delta, down_delta = lax.optimization_barrier(
        (
            jnp.concatenate(returned),
            dense_product("tc,tf->cf", normed_all, jnp.concatenate(gates)),
            dense_product("tc,tf->cf", normed_all, jnp.concatenate(uppers)),
            dense_product("td,tf->df", cotangent_all, active_all),
        )
    )
    down_rows = sum_positions(
        after(
            dense_product("tf,df->td", active_all, down_here).astype(jnp.bfloat16), mid_norm_back
        )
    )
    gate_delta, up_delta, down_delta = return_hidden((gate_delta, up_delta, down_delta))

    mlp_gain_delta = jnp.sum(mid_norm_back * middle * scale_mid, axis=0)
    middle_back = cotangent_rows.astype(jnp.float32) + norm_back(
        mid_norm_back, middle, scale_mid, gain_mid
    )
    branch_back = gather_plane(middle_back.astype(jnp.bfloat16).reshape(micro, piece, width))
    branch_back = branch_back.reshape(blocks * rows, width)
    extended_back = dense_product(
        "td,dk->tk", branch_back, jnp.concatenate([output_here, second_twice.T], axis=1)
    )
    lifted = extended_back[:, query_width:]
    lifted_parts = halves(lifted)
    first_pair = jnp.concatenate([first_factor, first_factor], axis=1)
    mixed_back = extended_back[:, :query_width] + dense_product(
        "tr,cr->tc", lifted_parts, first_pair
    )
    out_full = dense_product("td,tc->dc", branch_back, mixed_low)
    out_delta = return_heads(out_full[:, :query_width])
    output_second_delta = ADAPTER_SCALE * folded(out_full[:, query_width:]).T
    out_shrink_delta = folded(dense_product("tc,tr->cr", mixed, lifted_parts))
    heads_back = mixed_back.astype(jnp.bfloat16).reshape(blocks, rows, heads, head_width)
    shares_back = dense_product("nthd,nbd->nthb", heads_back, values_window)
    values_window_back = dense_product("nthb,nthd->nbd", shares, heads_back)
    heads_exact = heads_back.astype(jnp.float32)
    divisor_back = (
        -(
            jnp.sum(shares_back * ratio, axis=-1, keepdims=True)
            + jnp.sum(heads_exact * prior_out, axis=-1, keepdims=True)
        )
        * inverse
    )
    scaled_back = jnp.concatenate([heads_exact * inverse, divisor_back], axis=-1).astype(
        jnp.bfloat16
    )
    states_back = dense_product("nthk,nthf->nkf", scaled_back, query_features)
    later = sums_around(states_back.reshape((micro, PLANE) + states_back.shape[1:]), True)
    later = halves(later.reshape(states_back.shape), 1)
    weights_back = shares_back * inverse + divisor_back
    scores_back = jnp.where(window_mask, weights_back * exponent, 0.0).astype(jnp.bfloat16)
    similar_back = jnp.where(linear_mask, weights_back, 0.0).astype(jnp.bfloat16)
    size = head_width + 1
    prior_state = prior[:, :head_width]
    prior_rest = prior[:, size : size + head_width]
    prior_norm = prior[:, head_width].astype(jnp.float32) + prior[:, size + head_width].astype(
        jnp.float32
    )
    query_features_back = (
        (
            dense_product("nthd,ndf->nthf", heads_back, prior_state)
            + dense_product("nthd,ndf->nthf", heads_back, prior_rest)
        )
        * inverse
        + divisor_back * prior_norm[:, None, None, :]
        + dense_product("nthb,nbf->nthf", similar_back, features_window)
    )
    features_window_back = dense_product("nthb,nthf->nbf", similar_back, query_features)
    queries_back = dense_product("nthb,nbd->nthd", scores_back, keys_window) * scale
    keys_window_back = dense_product("nthb,nthd->nbd", scores_back, query_rows) * scale
    features_lead_back = jnp.where(
        usable_lead,
        dense_product(
            "nbk,nkf->nbf", jnp.concatenate([values_one, values_one], axis=-1), later
        ),
        0.0,
    )
    values_lead_back = dense_product("nbf,nkf->nbk", live, later)
    values_lead_back = folded(values_lead_back)[..., :head_width]
    window_back = jnp.concatenate(
        [keys_window_back, values_window_back, features_window_back], axis=-1
    )
    lead_back = jnp.concatenate(
        [jnp.zeros_like(keys_window_back[:, :rows]), values_lead_back, features_lead_back], axis=-1
    )
    window_back = jnp.concatenate(
        [window_back[:, :rows] + lead_back, window_back[:, rows:]], axis=1
    ).reshape(micro, PLANE, WIN + rows, -1)
    planes = plane_count()
    arriving = from_plane_before(
        window_back[:, 0, :WIN].astype(jnp.bfloat16), planes - 1
    ).astype(jnp.float32)
    wrapped = jnp.concatenate([arriving[1:], jnp.zeros_like(arriving[:1])], axis=0)
    arriving = jnp.where(my_plane() == planes - 1, wrapped, arriving)
    following = jnp.concatenate([window_back[:, 1:, :WIN], arriving[:, None]], axis=1)
    carried_back = jnp.concatenate(
        [window_back[:, :, WIN:rows], window_back[:, :, rows:] + following], axis=2
    ).reshape(blocks, rows, -1)
    keys_back = carried_back[..., :head_width]
    values_back = carried_back[..., head_width : 2 * head_width]
    key_logits_back = both_softmax_back(
        key_plus, key_minus, carried_back[..., 2 * head_width :]
    ).astype(jnp.bfloat16)
    query_logits_back = both_softmax_back(query_plus, query_minus, query_features_back).astype(
        jnp.bfloat16
    )
    key_feature_delta = dense_product("ntd,nte->de", key_rows, key_logits_back)
    query_feature_delta = dense_product("nthd,nthe->hde", query_rows, query_logits_back)
    keys_back = keys_back + dense_product("nte,de->ntd", key_logits_back, key_map)
    queries_back = queries_back + dense_product("nthe,hde->nthd", query_logits_back, query_map)
    projected_back = jnp.concatenate(
        [
            apply_rotation(queries_back, cosine_table[:, :, None], -sine_table[:, :, None])
            .astype(jnp.bfloat16)
            .reshape(blocks * rows, query_width),
            apply_rotation(keys_back, cosine_table, -sine_table)
            .astype(jnp.bfloat16)
            .reshape(blocks * rows, head_width),
            values_back.astype(jnp.bfloat16).reshape(blocks * rows, head_width),
        ],
        axis=-1,
    )
    projected_back, gate_delta, up_delta, down_delta = lax.optimization_barrier(
        (projected_back, gate_delta, up_delta, down_delta)
    )
    lift_all = dense_product("tk,rk->tr", projected_back, expand_twice)
    back_low = jnp.concatenate([projected_back, halves(lift_all)], axis=1)
    project_full = dense_product("tc,tk->ck", normed_flat, back_low)
    project_delta = return_heads(project_full[:, :joined])
    shrink_delta = folded(project_full[:, joined:])
    expand_delta = dense_product("tr,tk->rk", shrunk_parts, projected_back)
    expand_delta = ADAPTER_SCALE * (expand_delta[: 3 * rank] + expand_delta[3 * rank :])
    normed_back = dense_product(
        "tk,ck->tc",
        back_low,
        jnp.concatenate([project_here, shrink_all, shrink_all], axis=1),
    )
    in_norm_back = sum_plane(normed_back.reshape(micro, PLANE, rows, width))
    down_rows, middle_late, in_norm_back = lax.optimization_barrier(
        (down_rows, middle, in_norm_back)
    )
    results = middle_late + down_rows.astype(jnp.float32)
    attn_gain_delta = jnp.sum(in_norm_back * rows_in * scale_in, axis=(0, 1))
    inputs_back = middle_back.reshape(micro, piece, width) + norm_back(
        in_norm_back, rows_in, scale_in, gain_in
    )
    split, shared = total_small(
        (
            expand_delta[:rank, :query_width],
            expand_delta[rank : 2 * rank, query_width : query_width + head_width],
            expand_delta[2 * rank :, query_width + head_width :],
            out_shrink_delta,
            query_feature_delta,
            key_feature_delta,
        ),
        (attn_gain_delta, shrink_delta, output_second_delta, mlp_gain_delta),
    )
    return (
        results.astype(jnp.bfloat16).reshape(micro, piece, width),
        inputs_back,
        shared[0],
        project_delta[:, :, :query_width].reshape(-1, PLANE * query_width),
        project_delta[:, :, query_width : query_width + head_width].reshape(
            -1, PLANE * head_width
        ),
        project_delta[:, :, query_width + head_width :].reshape(-1, PLANE * head_width),
        out_delta.reshape(-1, PLANE * query_width),
        shared[1][:, :rank],
        along_columns(split[0]),
        shared[1][:, rank : 2 * rank],
        along_columns(split[1]),
        shared[1][:, 2 * rank :],
        along_columns(split[2]),
        split[3].reshape(-1, rank),
        shared[2],
        split[4].reshape(-1, head_width, head_width),
        split[5].reshape(-1, head_width, head_width),
        shared[3],
        gate_delta,
        up_delta,
        down_delta,
    )


def solution(mesh):
    return jax.shard_map(
        per_device,
        mesh=mesh,
        in_specs=(
            P(None, ("seq", "tp"), None),
            P(None, ("seq", "tp"), None),
            P(),
            P("seq", "tp"),
            P("seq", "tp"),
            P("seq", "tp"),
            P("seq", "tp"),
            P(),
            P(None, "tp"),
            P(),
            P(None, "tp"),
            P(),
            P(None, "tp"),
            P("tp", None),
            P(),
            P("tp", None, None),
            P("tp", None, None),
            P(),
            P("seq", "tp"),
            P("seq", "tp"),
            P("seq", "tp"),
        ),
        out_specs=(
            P(None, ("seq", "tp"), None),
            P(None, ("seq", "tp"), None),
            P(),
            P("seq", "tp"),
            P("seq", "tp"),
            P("seq", "tp"),
            P("seq", "tp"),
            P(),
            P(),
            P(),
            P(),
            P(),
            P(),
            P(),
            P(),
            P(),
            P(),
            P(),
            P("seq", "tp"),
            P("seq", "tp"),
            P("seq", "tp"),
        ),
        check_vma=False,
    )
```

```python
import math

import jax
import jax.numpy as jnp
from jax import lax
from jax.sharding import PartitionSpec as P

WIN = 64


EPS = 1e-05
ADAPTER_SCALE = 2.0
ROPE_BASE = 500000.0

PLANE = 4
CHUNKS = 2
MEMBERS = 8


def dense_product(form, left, right):
    return jnp.einsum(form, left, right, preferred_element_type=jnp.float32)


def halves(value, axis=-1):
    high = lax.reduce_precision(value, 8, 7)
    return jnp.concatenate(
        [high.astype(jnp.bfloat16), (value - high).astype(jnp.bfloat16)], axis=axis
    )


def folded(value):
    size = value.shape[-1] // 2
    return value[..., :size] + value[..., size:]


def root_scale(value_rows):
    return lax.rsqrt(jnp.mean(value_rows * value_rows, axis=-1, keepdims=True) + EPS)


def norm_back(grad_normed, value_rows, scale, gain):
    gained = grad_normed * gain
    inner = jnp.mean(gained * value_rows, axis=-1, keepdims=True)
    return scale * gained - value_rows * (scale * scale * scale) * inner


def rotary_tables(positions, width):
    half = width // 2
    inverse = ROPE_BASE ** (-(jnp.arange(half, dtype=jnp.float32) * (2.0 / width)))
    angles = positions.astype(jnp.float32)[:, None] * inverse[None, :]
    return (jnp.cos(angles), jnp.sin(angles))


def apply_rotation(value_rows, cosine_table, sine_table):
    half = value_rows.shape[-1] // 2
    first = value_rows[..., :half]
    second = value_rows[..., half:]
    return jnp.concatenate(
        [first * cosine_table - second * sine_table, second * cosine_table + first * sine_table],
        axis=-1,
    )


def both_softmax(logits):
    return (jax.nn.softmax(logits, axis=-1), jax.nn.softmax(-logits, axis=-1))


def both_softmax_back(plus, minus, grads):
    width = plus.shape[-1]
    grad_plus = grads[..., :width]
    grad_minus = grads[..., width:]
    return plus * (grad_plus - jnp.sum(grad_plus * plus, axis=-1, keepdims=True)) - minus * (
        grad_minus - jnp.sum(grad_minus * minus, axis=-1, keepdims=True)
    )


def after(value, *earlier):
    return lax.optimization_barrier((value,) + earlier)[0]


def plane_count():
    return lax.axis_size("seq") // PLANE


def my_plane():
    return lax.div(lax.axis_index("seq"), jnp.int32(PLANE))


def my_place():
    return lax.rem(lax.axis_index("seq"), jnp.int32(PLANE))


def plane_before(by):
    planes = plane_count()
    return lax.rem(my_plane() + jnp.int32(planes - by), jnp.int32(planes))


def at_block(blocks, index):
    return lax.dynamic_index_in_dim(blocks, index, 0, False, allow_negative_indices=False)


def swapped(value):
    return lax.ppermute(value, "tp", [(0, 1), (1, 0)])


def opposite(value, bit):
    return lax.ppermute(value, "seq", [(i, i ^ bit) for i in range(lax.axis_size("seq"))])


def from_plane_before(value, by):
    size = lax.axis_size("seq")
    return lax.ppermute(value, "seq", [(i, (i + by * PLANE) % size) for i in range(size)])


def in_order(mine, other, upper, axis):
    return jnp.stack([jnp.where(upper, other, mine), jnp.where(upper, mine, other)], axis=axis)


def split_half(value, upper, axis):
    index = upper.astype(jnp.int32)
    return (
        lax.dynamic_index_in_dim(value, index, axis, False, allow_negative_indices=False),
        lax.dynamic_index_in_dim(value, 1 - index, axis, False, allow_negative_indices=False),
    )


def upper_bit(bit):
    return (my_place() & bit) > 0


def upper_core():
    return lax.axis_index("tp") > 0


def gather_plane(own):
    micro, piece, width = own.shape
    parts = []
    for part in range(micro):
        value = own[part]
        if part % 2 == 0:
            value = in_order(value, opposite(value, 1), upper_bit(1), 0)
            value = in_order(value, opposite(value, 2), upper_bit(2), 0)
        else:
            value = in_order(value, opposite(value, 2), upper_bit(2), 0)
            value = in_order(value, opposite(value, 1), upper_bit(1), 1)
        parts.append(value.reshape(PLANE, piece, width))
    rows = jnp.stack(parts)
    rows = in_order(rows, swapped(rows), upper_core(), 2)
    return rows.reshape(micro, PLANE, 2 * piece, width)


def sum_plane(partial):
    micro, places, rows, width = partial.shape
    keep, send = split_half(
        partial.reshape(micro, places, 2, rows // 2, width), upper_core(), 2
    )
    summed = (keep + swapped(send)).reshape(micro, 2, 2, rows // 2, width)
    parts = []
    for part in range(micro):
        value = summed[part]
        for bit, axis in ((1, 1), (2, 0)) if part % 2 == 0 else ((2, 0), (1, 0)):
            keep, send = split_half(value, upper_bit(bit), axis)
            value = keep + opposite(send.astype(jnp.bfloat16), bit).astype(jnp.float32)
        parts.append(value)
    return jnp.stack(parts)


def place_groups():
    chips = lax.axis_size("seq")
    return [list(range(first, first + PLANE)) for first in range(0, chips, PLANE)]


def exchange_plane(pieces):
    return lax.all_to_all(
        pieces, "seq", 0, 0, tiled=True, axis_index_groups=place_groups()
    )


def stack_planes(value):
    planes = plane_count()
    whole = jnp.zeros((planes,) + value.shape, value.dtype)
    for by in range(planes):
        piece = from_plane_before(value, by) if by else value
        whole = lax.dynamic_update_slice_in_dim(
            whole, piece[None], plane_before(by), 0, allow_negative_indices=False
        )
    return whole.reshape((-1,) + value.shape[1:])


def return_heads(delta, columns):
    planes = plane_count()
    blocks = delta.astype(jnp.bfloat16).reshape(planes, -1, delta.shape[1])
    total = at_block(blocks, my_plane()).astype(jnp.float32)
    for by in range(1, planes):
        send = at_block(blocks, plane_before(by))
        total = total + from_plane_before(send, planes - by).astype(jnp.float32)
    pieces = exchange_plane(
        total.astype(jnp.bfloat16).reshape(PLANE, -1, delta.shape[1])
    )
    pieces = pieces.astype(jnp.float32)
    return (pieces[:, :, :columns].swapaxes(0, 1), jnp.sum(pieces[:, :, columns:], axis=0).T)


def outer_sums(total, later):
    micro = total.shape[0]
    planes = plane_count()
    total = total.astype(jnp.bfloat16)
    pieces = jnp.stack([total] + [from_plane_before(total, by) for by in range(1, planes)])
    source = lax.rem(my_plane() + planes - jnp.arange(planes), jnp.int32(planes))
    part = jnp.arange(micro)
    if later:
        beside = source[:, None, None] > my_plane()
        beyond = part[None, :, None] > part[None, None, :]
    else:
        beside = source[:, None, None] < my_plane()
        beyond = part[None, :, None] < part[None, None, :]
    same = part[None, :, None] == part[None, None, :]
    chosen = jnp.logical_or(beyond, jnp.logical_and(same, beside)).astype(jnp.bfloat16)
    return dense_product("kab,karl->brl", chosen, pieces)


def from_block_before(last):
    arrived = from_plane_before(last, 1)
    wrapped = jnp.concatenate([jnp.zeros_like(arrived[:1]), arrived[:-1]], axis=0)
    return jnp.where(my_plane() == 0, wrapped, arrived)


def from_block_behind(first):
    planes = plane_count()
    arrived = from_plane_before(first, planes - 1)
    wrapped = jnp.concatenate([arrived[1:], jnp.zeros_like(arrived[:1])], axis=0)
    return jnp.where(my_plane() == planes - 1, wrapped, arrived)


def windows(arrived, blocks):
    rows = blocks.shape[2]
    tails = jnp.concatenate([arrived[:, None], blocks[:, :-1, rows - WIN :]], axis=1)
    return jnp.concatenate([tails, blocks], axis=2)


def upper_chip(bit):
    return (lax.axis_index("seq") & bit) > 0


def position_bits():
    chips = lax.axis_size("seq")
    return [bit for bit in (4, 16, 32, 64, 128, 256) if bit < chips]


def hidden_groups():
    groups = {}
    for chip in range(lax.axis_size("seq")):
        groups.setdefault(chip & ~11, []).append(chip)
    return list(groups.values())


def gather_chips(value, flip):
    blocks = in_order(value, opposite(value, 8), upper_chip(8), 0)
    if flip:
        blocks = in_order(blocks, opposite(blocks, 1), upper_chip(1), 1)
        blocks = in_order(blocks, opposite(blocks, 2), upper_chip(2), 1)
    else:
        blocks = in_order(blocks, opposite(blocks, 2), upper_chip(2), 1)
        blocks = in_order(blocks, opposite(blocks, 1), upper_chip(1), 2)
    return blocks.reshape((MEMBERS,) + value.shape)


def halved(value, bit, axis):
    keep, send = split_half(value, upper_chip(bit), axis)
    return keep.astype(jnp.float32) + opposite(send.astype(jnp.bfloat16), bit).astype(jnp.float32)


def scatter_chips(partial, flip):
    value = partial.reshape((2, 2, 2) + partial.shape[1:])
    bit, axis = (2, 1) if flip else (1, 2)
    keep, send = split_half(value, upper_chip(bit), axis)
    send = send.astype(jnp.bfloat16)
    value = keep.astype(jnp.float32) + opposite(send, bit).astype(jnp.float32)
    value = halved(value, 3 - bit, 1)
    return (halved(value, 8, 0), send)


def exchange(value):
    return lax.all_to_all(value, "seq", 0, 0, tiled=True)


def exchange_members(value):
    return lax.all_to_all(
        value, "seq", 0, 0, tiled=True, axis_index_groups=hidden_groups()
    )


def flipped(value):
    for axis, bit in enumerate(reversed(position_bits())):
        value = jnp.where(upper_chip(bit), jnp.flip(value, axis + 1), value)
    return value


def to_relative(value):
    rows, width = value.shape
    count = len(position_bits())
    value = value.reshape((rows,) + (2,) * (count + 1) + (-1,))
    return flipped(value.swapaxes(count, count + 1)).reshape(rows, width)


def from_relative(value):
    rows, width = value.shape
    count = len(position_bits())
    value = flipped(value.reshape((rows,) + (2,) * (count + 1) + (-1,)))
    return value.swapaxes(count, count + 1).reshape(rows, width)


def deal_hidden(local):
    rows, hidden = local.shape
    pieces = local.reshape(rows, MEMBERS, hidden // MEMBERS).swapaxes(0, 1)
    return exchange_members(pieces).reshape(MEMBERS * rows, -1)


def widened(value):
    for bit in position_bits():
        value = jnp.concatenate([value, opposite(value, bit)], axis=0)
    return value


def narrowed(value):
    for bit in reversed(position_bits()):
        half = value.shape[0] // 2
        arrived = opposite(value[half:].astype(jnp.bfloat16), bit)
        value = (value[:half].astype(jnp.float32) + arrived.astype(jnp.float32)).astype(
            jnp.bfloat16
        )
    return value


def deal_back(values, rows):
    back = exchange_members(
        jnp.stack([value.reshape(MEMBERS, rows, -1) for value in values], axis=1)
    )
    return tuple(
        back[:, index].swapaxes(0, 1).reshape(rows, -1).astype(jnp.float32)
        for index in range(len(values))
    )


def gather_positions(rows):
    return lax.all_gather(
        rows, "seq", axis=0, tiled=True, axis_index_groups=hidden_groups()
    )


def sum_positions(partial):
    return lax.psum_scatter(
        partial, "seq", scatter_dimension=0, tiled=True, axis_index_groups=hidden_groups()
    )


def lanes(value):
    return value.reshape(-1, 128)


def everywhere(value):
    chips = lax.axis_size("seq")
    whole = exchange(jnp.broadcast_to(value[None], (chips,) + value.shape))
    return in_order(whole, swapped(whole), upper_core(), 0)


def total_heads(split, shared, gain, earlier):
    planes = plane_count()
    flat = jnp.concatenate([lanes(part) for part in split], axis=0)
    count = -(-flat.shape[0] // planes)
    flat = jnp.pad(flat, ((0, count * planes - flat.shape[0]), (0, 0)))
    flat = flat.reshape(planes, count, 128)
    mine = at_block(flat, my_plane())
    for by in range(1, planes):
        mine = mine + from_plane_before(at_block(flat, plane_before(by)), planes - by)
    both = jnp.concatenate([lanes(part) for part in shared] + [lanes(gain)], axis=0)
    keep, send = split_half(both.reshape(2, -1, 128), upper_core(), 0)
    both = keep + swapped(send)
    half = both.shape[0]
    payload = jnp.concatenate([mine, both], axis=0)
    payload = jnp.pad(payload, ((0, -payload.shape[0] % 8), (0, 0)))
    payload, *earlier = lax.optimization_barrier((payload,) + earlier)
    whole = everywhere(payload)
    cores, chips = whole.shape[:2]
    heads = whole[:, :, :count].reshape(cores, planes, PLANE, count, 128)
    heads = heads.swapaxes(1, 2).reshape(cores, PLANE, planes * count, 128)
    split_out = []
    start = 0
    for part in split:
        size = part.size // 128
        split_out.append(
            heads[:, :, start : start + size].reshape((cores, PLANE) + part.shape)
        )
        start += size
    rest = whole[:, :, count : count + half].swapaxes(0, 1).reshape(chips, cores * half, 128)
    shared_out = []
    start = 0
    for part in shared:
        size = part.size // 128
        shared_out.append(rest[:, start : start + size].reshape((chips,) + part.shape))
        start += size
    return (split_out, shared_out, jnp.sum(rest[:, start:], axis=0).reshape(-1), earlier)


def along_columns(parts):
    return parts.transpose(2, 0, 1, 3).reshape(parts.shape[2], -1)


def my_columns(value, axis):
    size = value.shape[axis] // PLANE
    return lax.dynamic_slice_in_dim(
        value, my_place() * size, size, axis, allow_negative_indices=False
    )


def by_place(value):
    return value.reshape(value.shape[0], PLANE, -1).swapaxes(0, 1)


def per_device(
    inputs,
    cotangent,
    attn_gain,
    query_matrix,
    key_matrix,
    value_matrix,
    output_matrix,
    query_first_factor,
    query_second_factor,
    key_first_factor,
    key_second_factor,
    value_first_factor,
    value_second_factor,
    output_first_factor,
    output_second_factor,
    query_feature,
    key_feature_layer,
    mlp_gain,
    gate_weight,
    up_weight,
    down_weight,
):
    micro, piece, width = inputs.shape
    chips = lax.axis_size("seq")
    rows = piece * lax.axis_size("tp")
    span = rows * chips
    head_width = query_feature.shape[1]
    group_size = query_feature.shape[0] // key_feature_layer.shape[0]
    rank = query_first_factor.shape[1]
    scale = 1.0 / math.sqrt(head_width)
    query_width = query_matrix.shape[1] // PLANE
    heads = query_width // head_width
    own = micro * piece
    blocks = micro * PLANE
    gain_in = attn_gain.astype(jnp.float32)
    gain_mid = mlp_gain.astype(jnp.float32)
    shrink_all = jnp.concatenate([query_first_factor, key_first_factor, value_first_factor], axis=1)
    expand_all = jnp.zeros((3 * rank, query_width + 2 * head_width), jnp.bfloat16)
    expand_all = expand_all.at[:rank, :query_width].set(my_columns(query_second_factor, 1))
    expand_all = expand_all.at[rank : 2 * rank, query_width : query_width + head_width].set(
        my_columns(key_second_factor, 1)
    )
    expand_all = expand_all.at[2 * rank :, query_width + head_width :].set(
        my_columns(value_second_factor, 1)
    )
    query_map = my_columns(query_feature, 0)
    key_map = my_columns(key_feature_layer, 0)[0]
    first_factor = my_columns(output_first_factor, 0)
    second_twice = output_second_factor * jnp.bfloat16(ADAPTER_SCALE)

    pieces = exchange_plane(
        jnp.concatenate(
            [
                by_place(query_matrix),
                by_place(key_matrix),
                by_place(value_matrix),
                by_place(output_matrix),
            ],
            axis=2,
        )
    )
    joined = query_width + 2 * head_width
    project_here = stack_planes(pieces[:, :, :joined].reshape(-1, joined))
    rows_in = inputs.astype(jnp.float32)
    scale_in = root_scale(rows_in)
    normed_input = gather_plane(
        after((rows_in * scale_in * gain_in).astype(jnp.bfloat16), pieces)
    )
    project_here, normed_input = lax.optimization_barrier((project_here, normed_input))
    cotangent_rows = cotangent.reshape(own, width)
    cotangent_all = gather_positions(after(to_relative(cotangent_rows), normed_input))
    gate_dealt = deal_hidden(after(gate_weight, project_here))
    up_dealt = deal_hidden(after(up_weight, gate_dealt))
    down_dealt = deal_hidden(after(down_weight, up_dealt))

    normed_flat = normed_input.reshape(blocks * rows, width)
    extended = dense_product(
        "tc,ck->tk", normed_flat, jnp.concatenate([project_here, shrink_all], axis=1)
    )
    shrunk = extended[:, joined:]
    shrunk_parts = halves(shrunk)
    expand_twice = expand_all * jnp.bfloat16(ADAPTER_SCALE)
    projected = extended[:, :joined] + dense_product(
        "tr,rk->tk", shrunk_parts, jnp.concatenate([expand_twice, expand_twice], axis=0)
    )
    positions = (
        jnp.arange(micro, dtype=jnp.int32)[:, None] * span
        + my_plane() * (PLANE * rows)
        + jnp.arange(PLANE * rows, dtype=jnp.int32)[None, :]
    )
    cosine_table, sine_table = rotary_tables(positions.reshape(-1), head_width)
    cosine_table = cosine_table.reshape(blocks, rows, -1)
    sine_table = sine_table.reshape(blocks, rows, -1)
    projected = projected.reshape(blocks, rows, joined)
    query_rows = apply_rotation(
        projected[..., :query_width].reshape(blocks, rows, heads, head_width),
        cosine_table[:, :, None],
        sine_table[:, :, None],
    ).astype(jnp.bfloat16)
    key_rows = apply_rotation(
        projected[..., query_width : query_width + head_width], cosine_table, sine_table
    ).astype(jnp.bfloat16)
    value_rows = projected[..., query_width + head_width :].astype(jnp.bfloat16)
    key_plus, key_minus = both_softmax(dense_product("ntd,de->nte", key_rows, key_map))
    key_features = jnp.concatenate([key_plus, key_minus], axis=-1).astype(jnp.bfloat16)
    carried = jnp.concatenate([key_rows, value_rows, key_features], axis=-1).reshape(
        micro, PLANE, rows, -1
    )
    arrived = from_block_before(carried[:, -1, rows - WIN :])
    window = windows(arrived, carried).reshape(blocks, WIN + rows, -1)
    keys_window = window[..., :head_width]
    values_window = window[..., head_width : 2 * head_width]
    features_window = window[..., 2 * head_width :]
    usable = jnp.logical_or(jnp.arange(blocks) > 0, my_plane() > 0)
    ones = jnp.ones((blocks, rows, 1), jnp.bfloat16)
    values_one = jnp.concatenate([value_rows, ones], axis=-1)
    states = dense_product("nbd,nbf->ndf", values_one, key_features)
    states = states.reshape((micro, PLANE) + states.shape[1:])
    outer = outer_sums(jnp.sum(states, axis=1), False)
    tails = window.reshape(micro, PLANE, WIN + rows, -1)[:, :, :WIN]
    tails_one = jnp.concatenate(
        [tails[..., head_width : 2 * head_width], jnp.ones((micro, PLANE, WIN, 1), jnp.bfloat16)],
        axis=-1,
    )
    prior = -dense_product("mpbd,mpbf->mpdf", tails_one, tails[..., 2 * head_width :])
    running = outer
    sums = []
    for place in range(PLANE):
        sums.append(running)
        running = running + states[:, place]
    prior = prior + jnp.stack(sums, axis=1)
    prior, gate_dealt, up_dealt = lax.optimization_barrier((prior, gate_dealt, up_dealt))
    prior = halves(prior.reshape((blocks,) + prior.shape[2:]), 1)
    output_here = stack_planes(
        after(pieces[:, :, joined:].reshape(-1, query_width), prior)
    )
    gate_mine = widened(after(gate_dealt, prior))
    query_plus, query_minus = both_softmax(
        dense_product("nthd,hde->nthe", query_rows, query_map)
    )
    query_features = jnp.concatenate([query_plus, query_minus], axis=-1).astype(jnp.bfloat16)
    query_pos = lax.broadcasted_iota(jnp.int32, (rows, rows + WIN), 0)
    key_pos = lax.broadcasted_iota(jnp.int32, (rows, rows + WIN), 1)
    open_keys = jnp.logical_or(key_pos[None] >= WIN, usable[:, None, None])
    linear_mask = jnp.logical_and((key_pos <= query_pos)[None], open_keys)[:, :, None]
    window_mask = jnp.logical_and(
        jnp.logical_and(key_pos > query_pos, key_pos <= query_pos + WIN)[None], open_keys
    )[:, :, None]
    scores = dense_product("nthd,nbd->nthb", query_rows, keys_window) * scale
    similar = dense_product("nthf,nbf->nthb", query_features, features_window)
    exponent = jnp.where(window_mask, jnp.exp(scores), 0.0)
    weights_all = exponent + jnp.where(linear_mask, similar, 0.0)
    prior_rows = dense_product("nthf,nkf->nthk", query_features, prior)
    prior_rows = folded(prior_rows)
    divisor = jnp.sum(weights_all, axis=-1, keepdims=True) + prior_rows[..., head_width:]
    inverse = 1.0 / divisor
    ratio = weights_all * inverse
    shares = ratio.astype(jnp.bfloat16)
    prior_out = prior_rows[..., :head_width] * inverse
    mixed = (
        (dense_product("nthb,nbd->nthd", shares, values_window) + prior_out)
        .astype(jnp.bfloat16)
        .reshape(blocks * rows, query_width)
    )
    mixed, gate_mine, down_dealt, cotangent_all = lax.optimization_barrier(
        (mixed, gate_mine, down_dealt, cotangent_all)
    )
    up_mine = widened(after(up_dealt, gate_mine))
    low_rank = dense_product("tc,cr->tr", mixed, first_factor)
    low_parts = halves(low_rank)
    mixed_low = jnp.concatenate([mixed, low_parts], axis=1)
    branch = dense_product(
        "ta,wa->tw",
        mixed_low,
        jnp.concatenate([output_here, second_twice.T, second_twice.T], axis=1),
    )
    middle = (rows_in + sum_plane(branch.reshape(micro, PLANE, rows, width))).reshape(own, width)
    scale_mid = root_scale(middle)
    middle, up_mine = lax.optimization_barrier((middle, up_mine))
    down_mine = widened(after(down_dealt, up_mine))
    project_ff = jnp.concatenate(
        [gate_mine, up_mine, swapped(gate_mine), swapped(up_mine)], axis=1
    )
    part = gate_mine.shape[1]

    normed_own = to_relative((middle * scale_mid * gain_mid).astype(jnp.bfloat16))
    step = own // CHUNKS
    down_here = jnp.concatenate([down_mine, swapped(down_mine)], axis=1)
    active_back = dense_product("td,df->tf", cotangent_all, down_here)
    active_back = active_back.reshape(MEMBERS, CHUNKS, step, -1)
    gathered, backs, actives, returned, firsts = [], [], [], [], []
    for chunk in range(CHUNKS):
        flip = chunk % 2 == 1
        mine = normed_own[chunk * step : (chunk + 1) * step]
        if chunk >= 2:
            mine = after(mine, gathered[chunk - 2])
        whole = gather_chips(mine, flip).reshape(MEMBERS * step, width)
        gathered.append(whole)
        both = dense_product("tc,cf->tf", whole, project_ff)
        gate = jnp.concatenate([both[:, :part], both[:, 2 * part : 3 * part]], axis=1)
        upper = jnp.concatenate([both[:, part : 2 * part], both[:, 3 * part :]], axis=1)
        logistic = jax.nn.sigmoid(gate)
        active = (gate * logistic * upper).astype(jnp.bfloat16)
        back = active_back[:, chunk].reshape(MEMBERS * step, -1)
        gate_back = (back * upper * logistic * (1.0 + gate * (1.0 - logistic))).astype(
            jnp.bfloat16
        )
        upper_back = (back * gate * logistic).astype(jnp.bfloat16)
        both_back = jnp.concatenate(
            [gate_back[:, :part], upper_back[:, :part], gate_back[:, part:], upper_back[:, part:]],
            axis=1,
        )
        partial = dense_product("tf,cf->tc", both_back, project_ff)
        summed, first = scatter_chips(partial.reshape(MEMBERS, step, width), flip)
        returned.append(summed)
        firsts.append(first)
        backs.append(both_back)
        actives.append(active.reshape(MEMBERS, step, -1))
    normed_all = jnp.concatenate(gathered)
    early = [after(item, firsts[-1]) for item in backs]
    active_all = jnp.stack(actives, axis=1).reshape(MEMBERS * own, -1)
    backs_all = jnp.concatenate(early)
    sends = (
        dense_product("tc,tf->cf", normed_all, backs_all[:, 2 * part :]).astype(jnp.bfloat16),
        dense_product("td,tf->df", cotangent_all, active_all[:, part:]).astype(jnp.bfloat16),
    )
    keeps = (
        dense_product("tc,tf->cf", normed_all, backs_all[:, : 2 * part]),
        dense_product("td,tf->df", cotangent_all, active_all[:, :part]),
    )
    sums = [
        (keep + swapped(send).astype(jnp.float32)).astype(jnp.bfloat16)
        for keep, send in zip(keeps, sends)
    ]
    mid_norm_back, both_sum, down_sum = lax.optimization_barrier(
        (jnp.concatenate(returned), sums[0], sums[1])
    )
    gate_part = narrowed(both_sum[:, :part])
    mid_norm_back = from_relative(mid_norm_back)
    mlp_gain_delta = jnp.sum(mid_norm_back * middle * scale_mid, axis=0)
    middle_back = cotangent_rows.astype(jnp.float32) + norm_back(
        mid_norm_back, middle, scale_mid, gain_mid
    )
    branch_back = gather_plane(middle_back.astype(jnp.bfloat16).reshape(micro, piece, width))
    branch_back = branch_back.reshape(blocks * rows, width)
    down_rows = sum_positions(
        after(
            dense_product("tf,df->td", active_all, down_here).astype(jnp.bfloat16), branch_back
        )
    )
    extended_back = dense_product(
        "td,dk->tk", branch_back, jnp.concatenate([output_here, second_twice.T], axis=1)
    )
    lifted = extended_back[:, query_width:]
    lifted_parts = halves(lifted)
    first_pair = jnp.concatenate([first_factor, first_factor], axis=1)
    mixed_back = extended_back[:, :query_width] + dense_product(
        "tr,cr->tc", lifted_parts, first_pair
    )
    out_full = dense_product("td,tc->dc", branch_back, mixed_low)
    out_delta, output_second_delta = return_heads(
        jnp.concatenate(
            [out_full[:, :query_width], ADAPTER_SCALE * folded(out_full[:, query_width:])], axis=1
        ),
        query_width,
    )
    out_shrink_delta = folded(dense_product("tc,tr->cr", mixed, lifted_parts))
    heads_back = mixed_back.astype(jnp.bfloat16).reshape(blocks, rows, heads, head_width)
    shares_back = dense_product("nthd,nbd->nthb", heads_back, values_window)
    values_window_back = dense_product("nthb,nthd->nbd", shares, heads_back)
    heads_exact = heads_back.astype(jnp.float32)
    divisor_back = (
        -(
            jnp.sum(shares_back * ratio, axis=-1, keepdims=True)
            + jnp.sum(heads_exact * prior_out, axis=-1, keepdims=True)
        )
        * inverse
    )
    scaled_back = jnp.concatenate([heads_exact * inverse, divisor_back], axis=-1).astype(
        jnp.bfloat16
    )
    states_back = dense_product("nthk,nthf->nkf", scaled_back, query_features)
    states_back = states_back.reshape((micro, PLANE) + states_back.shape[1:])
    outer = outer_sums(jnp.sum(states_back, axis=1), True)
    next_first = from_block_behind(states_back[:, 0].astype(jnp.bfloat16)).astype(jnp.float32)
    running = outer
    sums = [None] * PLANE
    for place in reversed(range(PLANE)):
        behind = states_back[:, place + 1] if place + 1 < PLANE else next_first
        sums[place] = jnp.stack([running, running - behind], axis=1)
        running = running + states_back[:, place]
    later = jnp.stack(sums, axis=1)
    later = halves(later.reshape((2 * blocks,) + later.shape[3:]), 1)
    later, gate_part = lax.optimization_barrier((later, gate_part))
    up_part = narrowed(after(both_sum[:, part:], gate_part))
    weights_back = shares_back * inverse + divisor_back
    scores_back = jnp.where(window_mask, weights_back * exponent, 0.0).astype(jnp.bfloat16)
    similar_back = jnp.where(linear_mask, weights_back, 0.0).astype(jnp.bfloat16)
    size = head_width + 1
    prior_state = prior[:, :head_width]
    prior_rest = prior[:, size : size + head_width]
    prior_norm = prior[:, head_width].astype(jnp.float32) + prior[:, size + head_width].astype(
        jnp.float32
    )
    query_features_back = (
        (
            dense_product("nthd,ndf->nthf", heads_back, prior_state)
            + dense_product("nthd,ndf->nthf", heads_back, prior_rest)
        )
        * inverse
        + divisor_back * prior_norm[:, None, None, :]
        + dense_product("nthb,nbf->nthf", similar_back, features_window)
    )
    features_window_back = dense_product("nthb,nthf->nbf", similar_back, query_features)
    queries_back = dense_product("nthb,nbd->nthd", scores_back, keys_window) * scale
    keys_window_back = dense_product("nthb,nthd->nbd", scores_back, query_rows) * scale
    halved_one = values_one.reshape(2 * blocks, rows // 2, head_width + 1)
    features_lead_back = dense_product(
        "nbk,nkf->nbf", jnp.concatenate([halved_one, halved_one], axis=-1), later
    ).reshape(blocks, rows, -1)
    values_lead_back = dense_product(
        "nbf,nkf->nbk", key_features.reshape(2 * blocks, rows // 2, -1), later
    )
    values_lead_back = folded(values_lead_back)[..., :head_width].reshape(blocks, rows, -1)
    window_back = jnp.concatenate(
        [keys_window_back, values_window_back, features_window_back], axis=-1
    ).reshape(micro, PLANE, WIN + rows, -1)
    arriving = from_block_behind(window_back[:, 0, :WIN].astype(jnp.bfloat16))
    following = jnp.concatenate(
        [window_back[:, 1:, :WIN], arriving[:, None].astype(jnp.float32)], axis=1
    )
    carried_back = jnp.concatenate(
        [window_back[:, :, WIN:rows], window_back[:, :, rows:] + following], axis=2
    ).reshape(blocks, rows, -1)
    keys_back = carried_back[..., :head_width]
    values_back = carried_back[..., head_width : 2 * head_width] + values_lead_back
    carried_back, up_part, out_delta = lax.optimization_barrier(
        (carried_back, up_part, out_delta)
    )
    down_part = narrowed(after(down_sum, up_part))
    key_logits_back = both_softmax_back(
        key_plus, key_minus, carried_back[..., 2 * head_width :] + features_lead_back
    ).astype(jnp.bfloat16)
    query_logits_back = both_softmax_back(query_plus, query_minus, query_features_back).astype(
        jnp.bfloat16
    )
    key_feature_delta = dense_product("ntd,nte->de", key_rows, key_logits_back)
    query_feature_delta = dense_product("nthd,nthe->hde", query_rows, query_logits_back)
    keys_back = keys_back + dense_product("nte,de->ntd", key_logits_back, key_map)
    queries_back = queries_back + dense_product("nthe,hde->nthd", query_logits_back, query_map)
    projected_back = jnp.concatenate(
        [
            apply_rotation(queries_back, cosine_table[:, :, None], -sine_table[:, :, None])
            .astype(jnp.bfloat16)
            .reshape(blocks * rows, query_width),
            apply_rotation(keys_back, cosine_table, -sine_table)
            .astype(jnp.bfloat16)
            .reshape(blocks * rows, head_width),
            values_back.astype(jnp.bfloat16).reshape(blocks * rows, head_width),
        ],
        axis=-1,
    )
    projected_back, down_rows, down_part = lax.optimization_barrier(
        (projected_back, down_rows, down_part)
    )
    gate_delta, up_delta, down_delta = deal_back((gate_part, up_part, down_part), width // chips)
    lift_all = dense_product("tk,rk->tr", projected_back, expand_twice)
    back_low = jnp.concatenate([projected_back, halves(lift_all)], axis=1)
    project_full = dense_product("tc,tk->ck", normed_flat, back_low)
    project_delta, shrink_delta = return_heads(
        jnp.concatenate([project_full[:, :joined], folded(project_full[:, joined:])], axis=1),
        joined,
    )
    expand_delta = dense_product("tr,tk->rk", shrunk_parts, projected_back)
    expand_delta = ADAPTER_SCALE * (expand_delta[: 3 * rank] + expand_delta[3 * rank :])
    normed_back = dense_product(
        "tk,ck->tc",
        back_low,
        jnp.concatenate([project_here, shrink_all, shrink_all], axis=1),
    )
    in_norm_back = sum_plane(normed_back.reshape(micro, PLANE, rows, width))
    down_rows, middle_late, in_norm_back = lax.optimization_barrier(
        (down_rows, middle, in_norm_back)
    )
    results = middle_late + from_relative(down_rows).astype(jnp.float32)
    attn_gain_delta = jnp.sum(in_norm_back * rows_in * scale_in, axis=(0, 1))
    inputs_back = middle_back.reshape(micro, piece, width) + norm_back(
        in_norm_back, rows_in, scale_in, gain_in
    )
    split, shared, gain_totals, (gate_delta, up_delta, down_delta) = total_heads(
        (
            expand_delta[:rank, :query_width],
            expand_delta[rank : 2 * rank, query_width : query_width + head_width],
            expand_delta[2 * rank :, query_width + head_width :],
            out_shrink_delta,
            query_feature_delta,
            key_feature_delta,
        ),
        (shrink_delta, output_second_delta),
        jnp.concatenate([attn_gain_delta, mlp_gain_delta]),
        (gate_delta, up_delta, down_delta),
    )
    shrink_total = shared[0].swapaxes(1, 2).reshape(width, 3 * rank)
    return (
        results.astype(jnp.bfloat16).reshape(micro, piece, width),
        inputs_back,
        gain_totals[:width],
        project_delta[:, :, :query_width].reshape(-1, PLANE * query_width),
        project_delta[:, :, query_width : query_width + head_width].reshape(
            -1, PLANE * head_width
        ),
        project_delta[:, :, query_width + head_width :].reshape(-1, PLANE * head_width),
        out_delta.reshape(-1, PLANE * query_width),
        shrink_total[:, :rank],
        along_columns(split[0]),
        shrink_total[:, rank : 2 * rank],
        along_columns(split[1]),
        shrink_total[:, 2 * rank :],
        along_columns(split[2]),
        split[3].reshape(-1, rank),
        shared[1].swapaxes(0, 1).reshape(rank, width),
        split[4].reshape(-1, head_width, head_width),
        split[5].reshape(-1, head_width, head_width),
        gain_totals[width:],
        gate_delta,
        up_delta,
        down_delta,
    )


def solution(mesh):
    return jax.shard_map(
        per_device,
        mesh=mesh,
        in_specs=(
            P(None, ("seq", "tp"), None),
            P(None, ("seq", "tp"), None),
            P(),
            P("seq", "tp"),
            P("seq", "tp"),
            P("seq", "tp"),
            P("seq", "tp"),
            P(),
            P(None, "tp"),
            P(),
            P(None, "tp"),
            P(),
            P(None, "tp"),
            P("tp", None),
            P(),
            P("tp", None, None),
            P("tp", None, None),
            P(),
            P("seq", "tp"),
            P("seq", "tp"),
            P("seq", "tp"),
        ),
        out_specs=(
            P(None, ("seq", "tp"), None),
            P(None, ("seq", "tp"), None),
            P(),
            P("seq", "tp"),
            P("seq", "tp"),
            P("seq", "tp"),
            P("seq", "tp"),
            P(),
            P(),
            P(),
            P(),
            P(),
            P(),
            P(),
            P(),
            P(),
            P(),
            P(),
            P("seq", "tp"),
            P("seq", "tp"),
            P("seq", "tp"),
        ),
        check_vma=False,
    )
```

```python
import math

import jax
import jax.numpy as jnp
from jax import lax
from jax.sharding import PartitionSpec as P

WIN = 64


EPS = 1e-05
ADAPTER_SCALE = 2.0
ROPE_BASE = 500000.0

PLANE = 4
CHUNKS = 2
MEMBERS = 8


def dense_product(form, left, right):
    return jnp.einsum(form, left, right, preferred_element_type=jnp.float32)


def halves(value, axis=-1):
    high = lax.reduce_precision(value, 8, 7)
    return jnp.concatenate(
        [high.astype(jnp.bfloat16), (value - high).astype(jnp.bfloat16)], axis=axis
    )


def folded(value):
    size = value.shape[-1] // 2
    return value[..., :size] + value[..., size:]


def root_scale(value_rows):
    return lax.rsqrt(jnp.mean(value_rows * value_rows, axis=-1, keepdims=True) + EPS)


def norm_back(grad_normed, value_rows, scale, gain):
    gained = grad_normed * gain
    inner = jnp.mean(gained * value_rows, axis=-1, keepdims=True)
    return scale * gained - value_rows * (scale * scale * scale) * inner


def rotary_tables(positions, width):
    half = width // 2
    inverse = ROPE_BASE ** (-(jnp.arange(half, dtype=jnp.float32) * (2.0 / width)))
    angles = positions.astype(jnp.float32)[:, None] * inverse[None, :]
    return (jnp.cos(angles), jnp.sin(angles))


def apply_rotation(value_rows, cosine_table, sine_table):
    half = value_rows.shape[-1] // 2
    first = value_rows[..., :half]
    second = value_rows[..., half:]
    return jnp.concatenate(
        [first * cosine_table - second * sine_table, second * cosine_table + first * sine_table],
        axis=-1,
    )


def both_softmax(logits):
    return (jax.nn.softmax(logits, axis=-1), jax.nn.softmax(-logits, axis=-1))


def both_softmax_back(plus, minus, grads):
    width = plus.shape[-1]
    grad_plus = grads[..., :width]
    grad_minus = grads[..., width:]
    return plus * (grad_plus - jnp.sum(grad_plus * plus, axis=-1, keepdims=True)) - minus * (
        grad_minus - jnp.sum(grad_minus * minus, axis=-1, keepdims=True)
    )


def after(value, *earlier):
    return lax.optimization_barrier((value,) + earlier)[0]


def plane_count():
    return lax.axis_size("seq") // PLANE


def my_plane():
    return lax.div(lax.axis_index("seq"), jnp.int32(PLANE))


def my_place():
    return lax.rem(lax.axis_index("seq"), jnp.int32(PLANE))


def plane_before(by):
    planes = plane_count()
    return lax.rem(my_plane() + jnp.int32(planes - by), jnp.int32(planes))


def at_block(blocks, index):
    return lax.dynamic_index_in_dim(blocks, index, 0, False, allow_negative_indices=False)


def swapped(value):
    return lax.ppermute(value, "tp", [(0, 1), (1, 0)])


def opposite(value, bit):
    return lax.ppermute(value, "seq", [(i, i ^ bit) for i in range(lax.axis_size("seq"))])


def from_plane_before(value, by):
    size = lax.axis_size("seq")
    return lax.ppermute(value, "seq", [(i, (i + by * PLANE) % size) for i in range(size)])


def in_order(mine, other, upper, axis):
    return jnp.stack([jnp.where(upper, other, mine), jnp.where(upper, mine, other)], axis=axis)


def split_half(value, upper, axis):
    index = upper.astype(jnp.int32)
    return (
        lax.dynamic_index_in_dim(value, index, axis, False, allow_negative_indices=False),
        lax.dynamic_index_in_dim(value, 1 - index, axis, False, allow_negative_indices=False),
    )


def upper_bit(bit):
    return (my_place() & bit) > 0


def upper_core():
    return lax.axis_index("tp") > 0


def gather_plane(own, *others):
    micro, piece, width = own.shape
    parts = []
    for part in range(micro):
        value = own[part]
        if part % 2 == 0:
            value = in_order(value, opposite(value, 1), upper_bit(1), 0)
            value = in_order(value, opposite(value, 2), upper_bit(2), 0)
        else:
            value = in_order(value, opposite(value, 2), upper_bit(2), 0)
            value = in_order(value, opposite(value, 1), upper_bit(1), 1)
        parts.append(value.reshape(PLANE, piece, width))
    rows, *others = lax.optimization_barrier((jnp.stack(parts),) + others)
    rows = in_order(rows, swapped(rows), upper_core(), 2)
    return (rows.reshape(micro, PLANE, 2 * piece, width), *others)


def sum_cores(partial):
    micro, places, rows, width = partial.shape
    keep, send = split_half(
        partial.reshape(micro, places, 2, rows // 2, width), upper_core(), 2
    )
    return keep + swapped(send)


def sum_plane(summed):
    micro, places, rows, width = summed.shape
    summed = summed.reshape(micro, 2, 2, rows, width)
    parts = []
    for part in range(micro):
        value = summed[part]
        for bit, axis in ((1, 1), (2, 0)) if part % 2 == 0 else ((2, 0), (1, 0)):
            keep, send = split_half(value, upper_bit(bit), axis)
            value = keep + opposite(send.astype(jnp.bfloat16), bit).astype(jnp.float32)
        parts.append(value)
    return jnp.stack(parts)


def place_groups():
    chips = lax.axis_size("seq")
    return [list(range(first, first + PLANE)) for first in range(0, chips, PLANE)]


def exchange_plane(pieces):
    return lax.all_to_all(
        pieces, "seq", 0, 0, tiled=True, axis_index_groups=place_groups()
    )


def stack_planes(value):
    planes = plane_count()
    whole = jnp.zeros((planes,) + value.shape, value.dtype)
    for by in range(planes):
        piece = from_plane_before(value, by) if by else value
        whole = lax.dynamic_update_slice_in_dim(
            whole, piece[None], plane_before(by), 0, allow_negative_indices=False
        )
    return whole.reshape((-1,) + value.shape[1:])


def return_heads(delta, columns):
    planes = plane_count()
    blocks = delta.astype(jnp.bfloat16).reshape(planes, -1, delta.shape[1])
    total = at_block(blocks, my_plane()).astype(jnp.float32)
    for by in range(1, planes):
        send = at_block(blocks, plane_before(by))
        total = total + from_plane_before(send, planes - by).astype(jnp.float32)
    pieces = exchange_plane(
        total.astype(jnp.bfloat16).reshape(PLANE, -1, delta.shape[1])
    )
    pieces = pieces.astype(jnp.float32)
    return (pieces[:, :, :columns].swapaxes(0, 1), jnp.sum(pieces[:, :, columns:], axis=0).T)


def outer_sums(total, later):
    micro = total.shape[0]
    planes = plane_count()
    total = total.astype(jnp.bfloat16)
    pieces = jnp.stack([total] + [from_plane_before(total, by) for by in range(1, planes)])
    source = lax.rem(my_plane() + planes - jnp.arange(planes), jnp.int32(planes))
    part = jnp.arange(micro)
    if later:
        beside = source[:, None, None] > my_plane()
        beyond = part[None, :, None] > part[None, None, :]
    else:
        beside = source[:, None, None] < my_plane()
        beyond = part[None, :, None] < part[None, None, :]
    same = part[None, :, None] == part[None, None, :]
    chosen = jnp.logical_or(beyond, jnp.logical_and(same, beside)).astype(jnp.bfloat16)
    return dense_product("kab,karl->brl", chosen, pieces)


def from_block_before(last):
    arrived = from_plane_before(last, 1)
    wrapped = jnp.concatenate([jnp.zeros_like(arrived[:1]), arrived[:-1]], axis=0)
    return jnp.where(my_plane() == 0, wrapped, arrived)


def from_block_behind(first):
    planes = plane_count()
    arrived = from_plane_before(first, planes - 1)
    wrapped = jnp.concatenate([arrived[1:], jnp.zeros_like(arrived[:1])], axis=0)
    return jnp.where(my_plane() == planes - 1, wrapped, arrived)


def windows(arrived, blocks):
    rows = blocks.shape[2]
    tails = jnp.concatenate([arrived[:, None], blocks[:, :-1, rows - WIN :]], axis=1)
    return jnp.concatenate([tails, blocks], axis=2)


def upper_chip(bit):
    return (lax.axis_index("seq") & bit) > 0


def position_bits():
    chips = lax.axis_size("seq")
    return [bit for bit in (4, 16, 32, 64, 128, 256) if bit < chips]


def hidden_groups():
    groups = {}
    for chip in range(lax.axis_size("seq")):
        groups.setdefault(chip & ~11, []).append(chip)
    return list(groups.values())


def gather_chips(value, flip):
    blocks = in_order(value, opposite(value, 8), upper_chip(8), 0)
    if flip:
        blocks = in_order(blocks, opposite(blocks, 1), upper_chip(1), 1)
        blocks = in_order(blocks, opposite(blocks, 2), upper_chip(2), 1)
    else:
        blocks = in_order(blocks, opposite(blocks, 2), upper_chip(2), 1)
        blocks = in_order(blocks, opposite(blocks, 1), upper_chip(1), 2)
    return blocks.reshape((MEMBERS,) + value.shape)


def halved(value, bit, axis):
    keep, send = split_half(value, upper_chip(bit), axis)
    return keep.astype(jnp.float32) + opposite(send.astype(jnp.bfloat16), bit).astype(jnp.float32)


def scatter_chips(partial, flip):
    value = partial.reshape((2, 2, 2) + partial.shape[1:])
    bit, axis = (2, 1) if flip else (1, 2)
    keep, send = split_half(value, upper_chip(bit), axis)
    send = send.astype(jnp.bfloat16)
    value = keep.astype(jnp.float32) + opposite(send, bit).astype(jnp.float32)
    value = halved(value, 3 - bit, 1)
    return (halved(value, 8, 0), send)


def exchange(value):
    return lax.all_to_all(value, "seq", 0, 0, tiled=True)


def exchange_members(value):
    return lax.all_to_all(
        value, "seq", 0, 0, tiled=True, axis_index_groups=hidden_groups()
    )


def flipped(value):
    for axis, bit in enumerate(reversed(position_bits())):
        value = jnp.where(upper_chip(bit), jnp.flip(value, axis + 1), value)
    return value


def to_relative(value):
    rows, width = value.shape
    count = len(position_bits())
    value = value.reshape((rows,) + (2,) * (count + 1) + (-1,))
    return flipped(value.swapaxes(count, count + 1)).reshape(rows, width)


def from_relative(value):
    rows, width = value.shape
    count = len(position_bits())
    value = flipped(value.reshape((rows,) + (2,) * (count + 1) + (-1,)))
    return value.swapaxes(count, count + 1).reshape(rows, width)


def deal_hidden(local):
    rows, hidden = local.shape
    pieces = local.reshape(rows, MEMBERS, hidden // MEMBERS).swapaxes(0, 1)
    return exchange_members(pieces).reshape(MEMBERS * rows, -1)


def widened(value):
    for bit in position_bits():
        value = jnp.concatenate([value, opposite(value, bit)], axis=0)
    return value


def narrowed(value):
    for bit in reversed(position_bits()):
        half = value.shape[0] // 2
        arrived = opposite(value[half:].astype(jnp.bfloat16), bit)
        value = (value[:half].astype(jnp.float32) + arrived.astype(jnp.float32)).astype(
            jnp.bfloat16
        )
    return value


def deal_back(values, rows):
    back = exchange_members(
        jnp.stack([value.reshape(MEMBERS, rows, -1) for value in values], axis=1)
    )
    return tuple(
        back[:, index].swapaxes(0, 1).reshape(rows, -1).astype(jnp.float32)
        for index in range(len(values))
    )


def gather_positions(rows):
    return lax.all_gather(
        rows, "seq", axis=0, tiled=True, axis_index_groups=hidden_groups()
    )


def sum_positions(partial):
    return lax.psum_scatter(
        partial, "seq", scatter_dimension=0, tiled=True, axis_index_groups=hidden_groups()
    )


def lanes(value):
    return value.reshape(-1, 128)


def everywhere(value):
    chips = lax.axis_size("seq")
    whole = exchange(jnp.broadcast_to(value[None], (chips,) + value.shape))
    return in_order(whole, swapped(whole), upper_core(), 0)


def total_heads(split, shared, gain, earlier):
    planes = plane_count()
    flat = jnp.concatenate([lanes(part) for part in split], axis=0)
    count = -(-flat.shape[0] // planes)
    flat = jnp.pad(flat, ((0, count * planes - flat.shape[0]), (0, 0)))
    flat = flat.reshape(planes, count, 128)
    mine = at_block(flat, my_plane())
    for by in range(1, planes):
        mine = mine + from_plane_before(at_block(flat, plane_before(by)), planes - by)
    both = jnp.concatenate([lanes(part) for part in shared] + [lanes(gain)], axis=0)
    keep, send = split_half(both.reshape(2, -1, 128), upper_core(), 0)
    both = keep + swapped(send)
    half = both.shape[0]
    payload = jnp.concatenate([mine, both], axis=0)
    payload = jnp.pad(payload, ((0, -payload.shape[0] % 8), (0, 0)))
    whole = everywhere(payload)
    cores, chips = whole.shape[:2]
    heads = whole[:, :, :count].reshape(cores, planes, PLANE, count, 128)
    heads = heads.swapaxes(1, 2).reshape(cores, PLANE, planes * count, 128)
    split_out = []
    start = 0
    for part in split:
        size = part.size // 128
        split_out.append(
            heads[:, :, start : start + size].reshape((cores, PLANE) + part.shape)
        )
        start += size
    rest = whole[:, :, count : count + half].swapaxes(0, 1).reshape(chips, cores * half, 128)
    shared_out = []
    start = 0
    for part in shared:
        size = part.size // 128
        shared_out.append(rest[:, start : start + size].reshape((chips,) + part.shape))
        start += size
    return (split_out, shared_out, jnp.sum(rest[:, start:], axis=0).reshape(-1), earlier)


def along_columns(parts):
    return parts.transpose(2, 0, 1, 3).reshape(parts.shape[2], -1)


def my_columns(value, axis):
    size = value.shape[axis] // PLANE
    return lax.dynamic_slice_in_dim(
        value, my_place() * size, size, axis, allow_negative_indices=False
    )


def by_place(value):
    return value.reshape(value.shape[0], PLANE, -1).swapaxes(0, 1)


def per_device(
    inputs,
    cotangent,
    attn_gain,
    query_matrix,
    key_matrix,
    value_matrix,
    output_matrix,
    query_first_factor,
    query_second_factor,
    key_first_factor,
    key_second_factor,
    value_first_factor,
    value_second_factor,
    output_first_factor,
    output_second_factor,
    query_feature,
    key_feature_layer,
    mlp_gain,
    gate_weight,
    up_weight,
    down_weight,
):
    micro, piece, width = inputs.shape
    chips = lax.axis_size("seq")
    rows = piece * lax.axis_size("tp")
    span = rows * chips
    head_width = query_feature.shape[1]
    group_size = query_feature.shape[0] // key_feature_layer.shape[0]
    rank = query_first_factor.shape[1]
    scale = 1.0 / math.sqrt(head_width)
    query_width = query_matrix.shape[1] // PLANE
    heads = query_width // head_width
    own = micro * piece
    blocks = micro * PLANE
    gain_in = attn_gain.astype(jnp.float32)
    gain_mid = mlp_gain.astype(jnp.float32)
    shrink_all = jnp.concatenate([query_first_factor, key_first_factor, value_first_factor], axis=1)
    expand_all = jnp.zeros((3 * rank, query_width + 2 * head_width), jnp.bfloat16)
    expand_all = expand_all.at[:rank, :query_width].set(my_columns(query_second_factor, 1))
    expand_all = expand_all.at[rank : 2 * rank, query_width : query_width + head_width].set(
        my_columns(key_second_factor, 1)
    )
    expand_all = expand_all.at[2 * rank :, query_width + head_width :].set(
        my_columns(value_second_factor, 1)
    )
    query_map = my_columns(query_feature, 0)
    key_map = my_columns(key_feature_layer, 0)[0]
    first_factor = my_columns(output_first_factor, 0)
    second_twice = output_second_factor * jnp.bfloat16(ADAPTER_SCALE)

    pieces = exchange_plane(
        jnp.concatenate(
            [
                by_place(query_matrix),
                by_place(key_matrix),
                by_place(value_matrix),
                by_place(output_matrix),
            ],
            axis=2,
        )
    )
    joined = query_width + 2 * head_width
    project_here = stack_planes(pieces[:, :, :joined].reshape(-1, joined))
    rows_in = inputs.astype(jnp.float32)
    scale_in = root_scale(rows_in)
    normed_input, project_here = gather_plane(
        after((rows_in * scale_in * gain_in).astype(jnp.bfloat16), pieces), project_here
    )
    cotangent_rows = cotangent.reshape(own, width)
    gate_dealt = deal_hidden(after(gate_weight, project_here))
    cotangent_all = gather_positions(after(to_relative(cotangent_rows), gate_dealt))
    up_dealt = deal_hidden(after(up_weight, gate_dealt))
    down_dealt = deal_hidden(after(down_weight, up_dealt))

    normed_flat = normed_input.reshape(blocks * rows, width)
    extended = dense_product(
        "tc,ck->tk", normed_flat, jnp.concatenate([project_here, shrink_all], axis=1)
    )
    shrunk = extended[:, joined:]
    shrunk_parts = halves(shrunk)
    expand_twice = expand_all * jnp.bfloat16(ADAPTER_SCALE)
    projected = extended[:, :joined] + dense_product(
        "tr,rk->tk", shrunk_parts, jnp.concatenate([expand_twice, expand_twice], axis=0)
    )
    positions = (
        jnp.arange(micro, dtype=jnp.int32)[:, None] * span
        + my_plane() * (PLANE * rows)
        + jnp.arange(PLANE * rows, dtype=jnp.int32)[None, :]
    )
    cosine_table, sine_table = rotary_tables(positions.reshape(-1), head_width)
    cosine_table = cosine_table.reshape(blocks, rows, -1)
    sine_table = sine_table.reshape(blocks, rows, -1)
    projected = projected.reshape(blocks, rows, joined)
    query_rows = apply_rotation(
        projected[..., :query_width].reshape(blocks, rows, heads, head_width),
        cosine_table[:, :, None],
        sine_table[:, :, None],
    ).astype(jnp.bfloat16)
    key_rows = apply_rotation(
        projected[..., query_width : query_width + head_width], cosine_table, sine_table
    ).astype(jnp.bfloat16)
    value_rows = projected[..., query_width + head_width :].astype(jnp.bfloat16)
    key_plus, key_minus = both_softmax(dense_product("ntd,de->nte", key_rows, key_map))
    key_features = jnp.concatenate([key_plus, key_minus], axis=-1).astype(jnp.bfloat16)
    carried = jnp.concatenate([key_rows, value_rows, key_features], axis=-1).reshape(
        micro, PLANE, rows, -1
    )
    arrived = from_block_before(carried[:, -1, rows - WIN :])
    window = windows(arrived, carried).reshape(blocks, WIN + rows, -1)
    keys_window = window[..., :head_width]
    values_window = window[..., head_width : 2 * head_width]
    features_window = window[..., 2 * head_width :]
    usable = jnp.logical_or(jnp.arange(blocks) > 0, my_plane() > 0)
    ones = jnp.ones((blocks, rows, 1), jnp.bfloat16)
    values_one = jnp.concatenate([value_rows, ones], axis=-1)
    states = dense_product("nbd,nbf->ndf", values_one, key_features)
    states = states.reshape((micro, PLANE) + states.shape[1:])
    outer = outer_sums(jnp.sum(states, axis=1), False)
    tails = window.reshape(micro, PLANE, WIN + rows, -1)[:, :, :WIN]
    tails_one = jnp.concatenate(
        [tails[..., head_width : 2 * head_width], jnp.ones((micro, PLANE, WIN, 1), jnp.bfloat16)],
        axis=-1,
    )
    prior = -dense_product("mpbd,mpbf->mpdf", tails_one, tails[..., 2 * head_width :])
    running = outer
    sums = []
    for place in range(PLANE):
        sums.append(running)
        running = running + states[:, place]
    prior = prior + jnp.stack(sums, axis=1)
    prior = halves(prior.reshape((blocks,) + prior.shape[2:]), 1)
    output_here = stack_planes(
        after(pieces[:, :, joined:].reshape(-1, query_width), prior)
    )
    gate_mine = widened(after(gate_dealt, prior))
    query_plus, query_minus = both_softmax(
        dense_product("nthd,hde->nthe", query_rows, query_map)
    )
    query_features = jnp.concatenate([query_plus, query_minus], axis=-1).astype(jnp.bfloat16)
    query_pos = lax.broadcasted_iota(jnp.int32, (rows, rows + WIN), 0)
    key_pos = lax.broadcasted_iota(jnp.int32, (rows, rows + WIN), 1)
    open_keys = jnp.logical_or(key_pos[None] >= WIN, usable[:, None, None])
    linear_mask = jnp.logical_and((key_pos <= query_pos)[None], open_keys)[:, :, None]
    window_mask = jnp.logical_and(
        jnp.logical_and(key_pos > query_pos, key_pos <= query_pos + WIN)[None], open_keys
    )[:, :, None]
    scores = dense_product("nthd,nbd->nthb", query_rows, keys_window) * scale
    similar = dense_product("nthf,nbf->nthb", query_features, features_window)
    exponent = jnp.where(window_mask, jnp.exp(scores), 0.0)
    weights_all = exponent + jnp.where(linear_mask, similar, 0.0)
    prior_rows = dense_product("nthf,nkf->nthk", query_features, prior)
    prior_rows = folded(prior_rows)
    divisor = jnp.sum(weights_all, axis=-1, keepdims=True) + prior_rows[..., head_width:]
    inverse = 1.0 / divisor
    ratio = weights_all * inverse
    shares = ratio.astype(jnp.bfloat16)
    prior_out = prior_rows[..., :head_width] * inverse
    mixed = (
        (dense_product("nthb,nbd->nthd", shares, values_window) + prior_out)
        .astype(jnp.bfloat16)
        .reshape(blocks * rows, query_width)
    )
    mixed, gate_mine, up_dealt, down_dealt = lax.optimization_barrier(
        (mixed, gate_mine, up_dealt, down_dealt)
    )
    up_mine = widened(after(up_dealt, gate_mine))
    low_rank = dense_product("tc,cr->tr", mixed, first_factor)
    low_parts = halves(low_rank)
    mixed_low = jnp.concatenate([mixed, low_parts], axis=1)
    branch = dense_product(
        "ta,wa->tw",
        mixed_low,
        jnp.concatenate([output_here, second_twice.T, second_twice.T], axis=1),
    )
    middle = (rows_in + sum_plane(sum_cores(branch.reshape(micro, PLANE, rows, width)))).reshape(own, width)
    scale_mid = root_scale(middle)
    middle, up_mine, cotangent_all = lax.optimization_barrier((middle, up_mine, cotangent_all))
    down_mine = widened(after(down_dealt, up_mine))
    project_ff = jnp.concatenate(
        [gate_mine, up_mine, swapped(gate_mine), swapped(up_mine)], axis=1
    )
    part = gate_mine.shape[1]

    normed_own = to_relative((middle * scale_mid * gain_mid).astype(jnp.bfloat16))
    step = own // CHUNKS
    down_here = jnp.concatenate([down_mine, swapped(down_mine)], axis=1)
    active_back = dense_product("td,df->tf", cotangent_all, down_here)
    active_back = active_back.reshape(MEMBERS, CHUNKS, step, -1)
    gathered, backs, actives, returned, firsts = [], [], [], [], []
    for chunk in range(CHUNKS):
        flip = chunk % 2 == 1
        mine = normed_own[chunk * step : (chunk + 1) * step]
        if chunk >= 2:
            mine = after(mine, gathered[chunk - 2])
        whole = gather_chips(mine, flip).reshape(MEMBERS * step, width)
        gathered.append(whole)
        both = dense_product("tc,cf->tf", whole, project_ff)
        gate = jnp.concatenate([both[:, :part], both[:, 2 * part : 3 * part]], axis=1)
        upper = jnp.concatenate([both[:, part : 2 * part], both[:, 3 * part :]], axis=1)
        logistic = jax.nn.sigmoid(gate)
        active = (gate * logistic * upper).astype(jnp.bfloat16)
        back = active_back[:, chunk].reshape(MEMBERS * step, -1)
        gate_back = (back * upper * logistic * (1.0 + gate * (1.0 - logistic))).astype(
            jnp.bfloat16
        )
        upper_back = (back * gate * logistic).astype(jnp.bfloat16)
        both_back = jnp.concatenate(
            [gate_back[:, :part], upper_back[:, :part], gate_back[:, part:], upper_back[:, part:]],
            axis=1,
        )
        partial = dense_product("tf,cf->tc", both_back, project_ff)
        summed, first = scatter_chips(partial.reshape(MEMBERS, step, width), flip)
        returned.append(summed)
        firsts.append(first)
        backs.append(both_back)
        actives.append(active.reshape(MEMBERS, step, -1))
    normed_all = jnp.concatenate(gathered)
    early = [after(item, firsts[-1]) for item in backs]
    active_all = jnp.stack(actives, axis=1).reshape(MEMBERS * own, -1)
    backs_all = jnp.concatenate(early)
    sends = (
        dense_product("tc,tf->cf", normed_all, backs_all[:, 2 * part :]).astype(jnp.bfloat16),
        dense_product("td,tf->df", cotangent_all, active_all[:, part:]).astype(jnp.bfloat16),
    )
    keeps = (
        dense_product("tc,tf->cf", normed_all, backs_all[:, : 2 * part]),
        dense_product("td,tf->df", cotangent_all, active_all[:, :part]),
    )
    sums = [
        (keep + swapped(send).astype(jnp.float32)).astype(jnp.bfloat16)
        for keep, send in zip(keeps, sends)
    ]
    mid_norm_back, both_sum, down_sum = lax.optimization_barrier(
        (jnp.concatenate(returned), sums[0], sums[1])
    )
    gate_part = narrowed(both_sum[:, :part])
    mid_norm_back = from_relative(mid_norm_back)
    mlp_gain_delta = jnp.sum(mid_norm_back * middle * scale_mid, axis=0)
    middle_back = cotangent_rows.astype(jnp.float32) + norm_back(
        mid_norm_back, middle, scale_mid, gain_mid
    )
    (branch_back,) = gather_plane(middle_back.astype(jnp.bfloat16).reshape(micro, piece, width))
    branch_back = branch_back.reshape(blocks * rows, width)
    extended_back = dense_product(
        "td,dk->tk", branch_back, jnp.concatenate([output_here, second_twice.T], axis=1)
    )
    lifted = extended_back[:, query_width:]
    lifted_parts = halves(lifted)
    first_pair = jnp.concatenate([first_factor, first_factor], axis=1)
    mixed_back = extended_back[:, :query_width] + dense_product(
        "tr,cr->tc", lifted_parts, first_pair
    )
    out_full = dense_product("td,tc->dc", branch_back, mixed_low)
    out_delta, output_second_delta = return_heads(
        jnp.concatenate(
            [out_full[:, :query_width], ADAPTER_SCALE * folded(out_full[:, query_width:])], axis=1
        ),
        query_width,
    )
    out_shrink_delta = folded(dense_product("tc,tr->cr", mixed, lifted_parts))
    heads_back = mixed_back.astype(jnp.bfloat16).reshape(blocks, rows, heads, head_width)
    shares_back = dense_product("nthd,nbd->nthb", heads_back, values_window)
    values_window_back = dense_product("nthb,nthd->nbd", shares, heads_back)
    heads_exact = heads_back.astype(jnp.float32)
    divisor_back = (
        -(
            jnp.sum(shares_back * ratio, axis=-1, keepdims=True)
            + jnp.sum(heads_exact * prior_out, axis=-1, keepdims=True)
        )
        * inverse
    )
    scaled_back = jnp.concatenate([heads_exact * inverse, divisor_back], axis=-1).astype(
        jnp.bfloat16
    )
    states_back = dense_product("nthk,nthf->nkf", scaled_back, query_features)
    states_back = states_back.reshape((micro, PLANE) + states_back.shape[1:])
    outer = outer_sums(jnp.sum(states_back, axis=1), True)
    next_first = from_block_behind(states_back[:, 0].astype(jnp.bfloat16)).astype(jnp.float32)
    running = outer
    sums = [None] * PLANE
    for place in reversed(range(PLANE)):
        behind = states_back[:, place + 1] if place + 1 < PLANE else next_first
        sums[place] = jnp.stack([running, running - behind], axis=1)
        running = running + states_back[:, place]
    later = jnp.stack(sums, axis=1)
    later = halves(later.reshape((2 * blocks,) + later.shape[3:]), 1)
    up_part = narrowed(after(both_sum[:, part:], gate_part))
    later, up_part = lax.optimization_barrier((later, up_part))
    down_rows = sum_positions(
        after(
            dense_product("tf,df->td", active_all, down_here).astype(jnp.bfloat16), branch_back
        )
    )
    project_low = jnp.concatenate(
        [after(project_here, states_back), shrink_all, shrink_all], axis=1
    )
    weights_back = shares_back * inverse + divisor_back
    scores_back = jnp.where(window_mask, weights_back * exponent, 0.0).astype(jnp.bfloat16)
    similar_back = jnp.where(linear_mask, weights_back, 0.0).astype(jnp.bfloat16)
    size = head_width + 1
    prior_state = prior[:, :head_width]
    prior_rest = prior[:, size : size + head_width]
    prior_norm = prior[:, head_width].astype(jnp.float32) + prior[:, size + head_width].astype(
        jnp.float32
    )
    query_features_back = (
        (
            dense_product("nthd,ndf->nthf", heads_back, prior_state)
            + dense_product("nthd,ndf->nthf", heads_back, prior_rest)
        )
        * inverse
        + divisor_back * prior_norm[:, None, None, :]
        + dense_product("nthb,nbf->nthf", similar_back, features_window)
    )
    features_window_back = dense_product("nthb,nthf->nbf", similar_back, query_features)
    queries_back = dense_product("nthb,nbd->nthd", scores_back, keys_window) * scale
    keys_window_back = dense_product("nthb,nthd->nbd", scores_back, query_rows) * scale
    halved_one = values_one.reshape(2 * blocks, rows // 2, head_width + 1)
    features_lead_back = dense_product(
        "nbk,nkf->nbf", jnp.concatenate([halved_one, halved_one], axis=-1), later
    ).reshape(blocks, rows, -1)
    values_lead_back = dense_product(
        "nbf,nkf->nbk", key_features.reshape(2 * blocks, rows // 2, -1), later
    )
    values_lead_back = folded(values_lead_back)[..., :head_width].reshape(blocks, rows, -1)
    window_back = jnp.concatenate(
        [keys_window_back, values_window_back, features_window_back], axis=-1
    ).reshape(micro, PLANE, WIN + rows, -1)
    arriving = from_block_behind(window_back[:, 0, :WIN].astype(jnp.bfloat16))
    following = jnp.concatenate(
        [window_back[:, 1:, :WIN], arriving[:, None].astype(jnp.float32)], axis=1
    )
    carried_back = jnp.concatenate(
        [window_back[:, :, WIN:rows], window_back[:, :, rows:] + following], axis=2
    ).reshape(blocks, rows, -1)
    keys_back = carried_back[..., :head_width]
    values_back = carried_back[..., head_width : 2 * head_width] + values_lead_back
    down_part = narrowed(after(down_sum, up_part))
    carried_back, down_part, down_rows = lax.optimization_barrier(
        (carried_back, down_part, down_rows)
    )
    key_logits_back = both_softmax_back(
        key_plus, key_minus, carried_back[..., 2 * head_width :] + features_lead_back
    ).astype(jnp.bfloat16)
    query_logits_back = both_softmax_back(query_plus, query_minus, query_features_back).astype(
        jnp.bfloat16
    )
    key_feature_delta = dense_product("ntd,nte->de", key_rows, key_logits_back)
    query_feature_delta = dense_product("nthd,nthe->hde", query_rows, query_logits_back)
    keys_back = keys_back + dense_product("nte,de->ntd", key_logits_back, key_map)
    queries_back = queries_back + dense_product("nthe,hde->nthd", query_logits_back, query_map)
    projected_back = jnp.concatenate(
        [
            apply_rotation(queries_back, cosine_table[:, :, None], -sine_table[:, :, None])
            .astype(jnp.bfloat16)
            .reshape(blocks * rows, query_width),
            apply_rotation(keys_back, cosine_table, -sine_table)
            .astype(jnp.bfloat16)
            .reshape(blocks * rows, head_width),
            values_back.astype(jnp.bfloat16).reshape(blocks * rows, head_width),
        ],
        axis=-1,
    )
    projected_back, out_delta = lax.optimization_barrier((projected_back, out_delta))
    gate_delta, up_delta, down_delta = deal_back((gate_part, up_part, down_part), width // chips)
    lift_all = dense_product("tk,rk->tr", projected_back, expand_twice)
    back_low = jnp.concatenate([projected_back, halves(lift_all)], axis=1)
    normed_back = dense_product("tk,ck->tc", back_low, project_low)
    normed_back, gate_delta, up_delta, down_delta = lax.optimization_barrier(
        (normed_back, gate_delta, up_delta, down_delta)
    )
    normed_pair = sum_cores(normed_back.reshape(micro, PLANE, rows, width))
    project_full = after(dense_product("tc,tk->ck", normed_flat, back_low), normed_pair)
    project_delta, shrink_delta = return_heads(
        jnp.concatenate([project_full[:, :joined], folded(project_full[:, joined:])], axis=1),
        joined,
    )
    expand_delta = dense_product("tr,tk->rk", shrunk_parts, projected_back)
    expand_delta = ADAPTER_SCALE * (expand_delta[: 3 * rank] + expand_delta[3 * rank :])
    in_norm_back = sum_plane(normed_pair)
    down_rows, middle_late, in_norm_back = lax.optimization_barrier(
        (down_rows, middle, in_norm_back)
    )
    results = middle_late + from_relative(down_rows).astype(jnp.float32)
    attn_gain_delta = jnp.sum(in_norm_back * rows_in * scale_in, axis=(0, 1))
    inputs_back = middle_back.reshape(micro, piece, width) + norm_back(
        in_norm_back, rows_in, scale_in, gain_in
    )
    split, shared, gain_totals, (gate_delta, up_delta, down_delta) = total_heads(
        (
            expand_delta[:rank, :query_width],
            expand_delta[rank : 2 * rank, query_width : query_width + head_width],
            expand_delta[2 * rank :, query_width + head_width :],
            out_shrink_delta,
            query_feature_delta,
            key_feature_delta,
        ),
        (shrink_delta, output_second_delta),
        jnp.concatenate([attn_gain_delta, mlp_gain_delta]),
        (gate_delta, up_delta, down_delta),
    )
    shrink_total = shared[0].swapaxes(1, 2).reshape(width, 3 * rank)
    return (
        results.astype(jnp.bfloat16).reshape(micro, piece, width),
        inputs_back,
        gain_totals[:width],
        project_delta[:, :, :query_width].reshape(-1, PLANE * query_width),
        project_delta[:, :, query_width : query_width + head_width].reshape(
            -1, PLANE * head_width
        ),
        project_delta[:, :, query_width + head_width :].reshape(-1, PLANE * head_width),
        out_delta.reshape(-1, PLANE * query_width),
        shrink_total[:, :rank],
        along_columns(split[0]),
        shrink_total[:, rank : 2 * rank],
        along_columns(split[1]),
        shrink_total[:, 2 * rank :],
        along_columns(split[2]),
        split[3].reshape(-1, rank),
        shared[1].swapaxes(0, 1).reshape(rank, width),
        split[4].reshape(-1, head_width, head_width),
        split[5].reshape(-1, head_width, head_width),
        gain_totals[width:],
        gate_delta,
        up_delta,
        down_delta,
    )


def solution(mesh):
    return jax.shard_map(
        per_device,
        mesh=mesh,
        in_specs=(
            P(None, ("seq", "tp"), None),
            P(None, ("seq", "tp"), None),
            P(),
            P("seq", "tp"),
            P("seq", "tp"),
            P("seq", "tp"),
            P("seq", "tp"),
            P(),
            P(None, "tp"),
            P(),
            P(None, "tp"),
            P(),
            P(None, "tp"),
            P("tp", None),
            P(),
            P("tp", None, None),
            P("tp", None, None),
            P(),
            P("seq", "tp"),
            P("seq", "tp"),
            P("seq", "tp"),
        ),
        out_specs=(
            P(None, ("seq", "tp"), None),
            P(None, ("seq", "tp"), None),
            P(),
            P("seq", "tp"),
            P("seq", "tp"),
            P("seq", "tp"),
            P("seq", "tp"),
            P(),
            P(),
            P(),
            P(),
            P(),
            P(),
            P(),
            P(),
            P(),
            P(),
            P(),
            P("seq", "tp"),
            P("seq", "tp"),
            P("seq", "tp"),
        ),
        check_vma=False,
    )
```

```python
import math

import jax
import jax.numpy as jnp
from jax import lax
from jax.sharding import PartitionSpec as P

WIN = 64


EPS = 1e-05
ADAPTER_SCALE = 2.0
ROPE_BASE = 500000.0

PLANE = 4
CHUNKS = 2
MEMBERS = 8


def dense_product(form, left, right):
    return jnp.einsum(form, left, right, preferred_element_type=jnp.float32)


def halves(value, axis=-1):
    high = lax.reduce_precision(value, 8, 7)
    return jnp.concatenate(
        [high.astype(jnp.bfloat16), (value - high).astype(jnp.bfloat16)], axis=axis
    )


def folded(value):
    size = value.shape[-1] // 2
    return value[..., :size] + value[..., size:]


def root_scale(value_rows):
    return lax.rsqrt(jnp.mean(value_rows * value_rows, axis=-1, keepdims=True) + EPS)


def norm_back(grad_normed, value_rows, scale, gain):
    gained = grad_normed * gain
    inner = jnp.mean(gained * value_rows, axis=-1, keepdims=True)
    return scale * gained - value_rows * (scale * scale * scale) * inner


def rotary_tables(positions, width):
    half = width // 2
    inverse = ROPE_BASE ** (-(jnp.arange(half, dtype=jnp.float32) * (2.0 / width)))
    angles = positions.astype(jnp.float32)[:, None] * inverse[None, :]
    return (jnp.cos(angles), jnp.sin(angles))


def apply_rotation(value_rows, cosine_table, sine_table):
    half = value_rows.shape[-1] // 2
    first = value_rows[..., :half]
    second = value_rows[..., half:]
    return jnp.concatenate(
        [first * cosine_table - second * sine_table, second * cosine_table + first * sine_table],
        axis=-1,
    )


def both_softmax(logits):
    return (jax.nn.softmax(logits, axis=-1), jax.nn.softmax(-logits, axis=-1))


def both_softmax_back(plus, minus, grads):
    width = plus.shape[-1]
    grad_plus = grads[..., :width]
    grad_minus = grads[..., width:]
    return plus * (grad_plus - jnp.sum(grad_plus * plus, axis=-1, keepdims=True)) - minus * (
        grad_minus - jnp.sum(grad_minus * minus, axis=-1, keepdims=True)
    )


def after(value, *earlier):
    return lax.optimization_barrier((value,) + earlier)[0]


def plane_count():
    return lax.axis_size("seq") // PLANE


def my_plane():
    return lax.div(lax.axis_index("seq"), jnp.int32(PLANE))


def my_place():
    return lax.rem(lax.axis_index("seq"), jnp.int32(PLANE))


def plane_before(by):
    planes = plane_count()
    return lax.rem(my_plane() + jnp.int32(planes - by), jnp.int32(planes))


def at_block(blocks, index):
    return lax.dynamic_index_in_dim(blocks, index, 0, False, allow_negative_indices=False)


def swapped(value):
    return lax.ppermute(value, "tp", [(0, 1), (1, 0)])


def swapped_parts(value):
    return jnp.concatenate(
        [swapped(value[:, part : part + 1]) for part in range(0, PLANE, 1)], axis=1
    )


def opposite(value, bit):
    return lax.ppermute(value, "seq", [(i, i ^ bit) for i in range(lax.axis_size("seq"))])


def from_plane_before(value, by):
    size = lax.axis_size("seq")
    return lax.ppermute(value, "seq", [(i, (i + by * PLANE) % size) for i in range(size)])


def in_order(mine, other, upper, axis):
    return jnp.stack([jnp.where(upper, other, mine), jnp.where(upper, mine, other)], axis=axis)


def split_half(value, upper, axis):
    index = upper.astype(jnp.int32)
    return (
        lax.dynamic_index_in_dim(value, index, axis, False, allow_negative_indices=False),
        lax.dynamic_index_in_dim(value, 1 - index, axis, False, allow_negative_indices=False),
    )


def upper_bit(bit):
    return (my_place() & bit) > 0


def upper_core():
    return lax.axis_index("tp") > 0


def gather_plane(own, *others):
    micro, piece, width = own.shape
    parts = []
    for part in range(micro):
        value = own[part]
        if part % 2 == 0:
            value = in_order(value, opposite(value, 1), upper_bit(1), 0)
            value = in_order(value, opposite(value, 2), upper_bit(2), 0)
        else:
            value = in_order(value, opposite(value, 2), upper_bit(2), 0)
            value = in_order(value, opposite(value, 1), upper_bit(1), 1)
        parts.append(value.reshape(PLANE, piece, width))
    rows, *others = lax.optimization_barrier((jnp.stack(parts),) + others)
    rows = in_order(rows, swapped_parts(rows), upper_core(), 2)
    return (rows.reshape(micro, PLANE, 2 * piece, width), *others)


def sum_cores(partial):
    micro, places, rows, width = partial.shape
    keep, send = split_half(
        partial.reshape(micro, places, 2, rows // 2, width), upper_core(), 2
    )
    return keep + swapped_parts(send)


def sum_plane(summed):
    micro, places, rows, width = summed.shape
    summed = summed.reshape(micro, 2, 2, rows, width)
    parts = []
    for part in range(micro):
        value = summed[part]
        for bit, axis in ((1, 1), (2, 0)) if part % 2 == 0 else ((2, 0), (1, 0)):
            keep, send = split_half(value, upper_bit(bit), axis)
            value = keep + opposite(send.astype(jnp.bfloat16), bit).astype(jnp.float32)
        parts.append(value)
    return jnp.stack(parts)


def place_groups():
    chips = lax.axis_size("seq")
    return [list(range(first, first + PLANE)) for first in range(0, chips, PLANE)]


def exchange_plane(pieces):
    return lax.all_to_all(
        pieces, "seq", 0, 0, tiled=True, axis_index_groups=place_groups()
    )


def stack_planes(value):
    planes = plane_count()
    whole = jnp.zeros((planes,) + value.shape, value.dtype)
    for by in range(planes):
        piece = from_plane_before(value, by) if by else value
        whole = lax.dynamic_update_slice_in_dim(
            whole, piece[None], plane_before(by), 0, allow_negative_indices=False
        )
    return whole.reshape((-1,) + value.shape[1:])


def return_heads(delta, columns):
    planes = plane_count()
    blocks = delta.astype(jnp.bfloat16).reshape(planes, -1, delta.shape[1])
    total = at_block(blocks, my_plane()).astype(jnp.float32)
    for by in range(1, planes):
        send = at_block(blocks, plane_before(by))
        total = total + from_plane_before(send, planes - by).astype(jnp.float32)
    pieces = exchange_plane(
        total.astype(jnp.bfloat16).reshape(PLANE, -1, delta.shape[1])
    )
    pieces = pieces.astype(jnp.float32)
    return (pieces[:, :, :columns].swapaxes(0, 1), jnp.sum(pieces[:, :, columns:], axis=0).T)


def outer_sums(total, later):
    micro = total.shape[0]
    planes = plane_count()
    total = total.astype(jnp.bfloat16)
    pieces = jnp.stack([total] + [from_plane_before(total, by) for by in range(1, planes)])
    source = lax.rem(my_plane() + planes - jnp.arange(planes), jnp.int32(planes))
    part = jnp.arange(micro)
    if later:
        beside = source[:, None, None] > my_plane()
        beyond = part[None, :, None] > part[None, None, :]
    else:
        beside = source[:, None, None] < my_plane()
        beyond = part[None, :, None] < part[None, None, :]
    same = part[None, :, None] == part[None, None, :]
    chosen = jnp.logical_or(beyond, jnp.logical_and(same, beside)).astype(jnp.bfloat16)
    return dense_product("kab,karl->brl", chosen, pieces)


def from_block_before(last):
    arrived = from_plane_before(last, 1)
    wrapped = jnp.concatenate([jnp.zeros_like(arrived[:1]), arrived[:-1]], axis=0)
    return jnp.where(my_plane() == 0, wrapped, arrived)


def from_block_behind(first):
    planes = plane_count()
    arrived = from_plane_before(first, planes - 1)
    wrapped = jnp.concatenate([arrived[1:], jnp.zeros_like(arrived[:1])], axis=0)
    return jnp.where(my_plane() == planes - 1, wrapped, arrived)


def windows(arrived, blocks):
    rows = blocks.shape[2]
    tails = jnp.concatenate([arrived[:, None], blocks[:, :-1, rows - WIN :]], axis=1)
    return jnp.concatenate([tails, blocks], axis=2)


def upper_chip(bit):
    return (lax.axis_index("seq") & bit) > 0


def position_bits():
    chips = lax.axis_size("seq")
    return [bit for bit in (4, 16, 32, 64, 128, 256) if bit < chips]


def hidden_groups():
    groups = {}
    for chip in range(lax.axis_size("seq")):
        groups.setdefault(chip & ~11, []).append(chip)
    return list(groups.values())


def gather_chips(value, flip):
    blocks = in_order(value, opposite(value, 8), upper_chip(8), 0)
    if flip:
        blocks = in_order(blocks, opposite(blocks, 1), upper_chip(1), 1)
        blocks = in_order(blocks, opposite(blocks, 2), upper_chip(2), 1)
    else:
        blocks = in_order(blocks, opposite(blocks, 2), upper_chip(2), 1)
        blocks = in_order(blocks, opposite(blocks, 1), upper_chip(1), 2)
    return blocks.reshape((MEMBERS,) + value.shape)


def halved(value, bit, axis):
    keep, send = split_half(value, upper_chip(bit), axis)
    return keep.astype(jnp.float32) + opposite(send.astype(jnp.bfloat16), bit).astype(jnp.float32)


def scatter_chips(partial, flip):
    value = partial.reshape((2, 2, 2) + partial.shape[1:])
    bit, axis = (2, 1) if flip else (1, 2)
    keep, send = split_half(value, upper_chip(bit), axis)
    send = send.astype(jnp.bfloat16)
    value = keep.astype(jnp.float32) + opposite(send, bit).astype(jnp.float32)
    value = halved(value, 3 - bit, 1)
    return (halved(value, 8, 0), send)


def exchange(value):
    return lax.all_to_all(value, "seq", 0, 0, tiled=True)


def exchange_members(value):
    return lax.all_to_all(
        value, "seq", 0, 0, tiled=True, axis_index_groups=hidden_groups()
    )


def flipped(value):
    for axis, bit in enumerate(reversed(position_bits())):
        value = jnp.where(upper_chip(bit), jnp.flip(value, axis + 1), value)
    return value


def to_relative(value):
    rows, width = value.shape
    count = len(position_bits())
    value = value.reshape((rows,) + (2,) * (count + 1) + (-1,))
    return flipped(value.swapaxes(count, count + 1)).reshape(rows, width)


def from_relative(value):
    rows, width = value.shape
    count = len(position_bits())
    value = flipped(value.reshape((rows,) + (2,) * (count + 1) + (-1,)))
    return value.swapaxes(count, count + 1).reshape(rows, width)


def deal_hidden(local):
    rows, hidden = local.shape
    pieces = local.reshape(rows, MEMBERS, hidden // MEMBERS).swapaxes(0, 1)
    return exchange_members(pieces).reshape(MEMBERS * rows, -1)


def widened(value):
    for bit in position_bits():
        value = jnp.concatenate([value, opposite(value, bit)], axis=0)
    return value


def narrowed(value):
    for bit in reversed(position_bits()):
        half = value.shape[0] // 2
        arrived = opposite(value[half:].astype(jnp.bfloat16), bit)
        value = (value[:half].astype(jnp.float32) + arrived.astype(jnp.float32)).astype(
            jnp.bfloat16
        )
    return value


def deal_back(values, rows):
    back = exchange_members(
        jnp.stack([value.reshape(MEMBERS, rows, -1) for value in values], axis=1)
    )
    return tuple(
        back[:, index].swapaxes(0, 1).reshape(rows, -1).astype(jnp.float32)
        for index in range(len(values))
    )


def gather_positions(rows):
    return lax.all_gather(
        rows, "seq", axis=0, tiled=True, axis_index_groups=hidden_groups()
    )


def sum_positions(partial):
    return lax.psum_scatter(
        partial, "seq", scatter_dimension=0, tiled=True, axis_index_groups=hidden_groups()
    )


def lanes(value):
    return value.reshape(-1, 128)


def everywhere(value):
    chips = lax.axis_size("seq")
    whole = exchange(jnp.broadcast_to(value[None], (chips,) + value.shape))
    return in_order(whole, swapped(whole), upper_core(), 0)


def total_heads(split, shared, gain, earlier):
    planes = plane_count()
    flat = jnp.concatenate([lanes(part) for part in split], axis=0)
    count = -(-flat.shape[0] // planes)
    flat = jnp.pad(flat, ((0, count * planes - flat.shape[0]), (0, 0)))
    flat = flat.reshape(planes, count, 128)
    mine = at_block(flat, my_plane())
    for by in range(1, planes):
        mine = mine + from_plane_before(at_block(flat, plane_before(by)), planes - by)
    both = jnp.concatenate([lanes(part) for part in shared] + [lanes(gain)], axis=0)
    keep, send = split_half(both.reshape(2, -1, 128), upper_core(), 0)
    both = keep + swapped(send)
    half = both.shape[0]
    payload = jnp.concatenate([mine, both], axis=0)
    payload = jnp.pad(payload, ((0, -payload.shape[0] % 8), (0, 0)))
    whole = everywhere(payload)
    cores, chips = whole.shape[:2]
    heads = whole[:, :, :count].reshape(cores, planes, PLANE, count, 128)
    heads = heads.swapaxes(1, 2).reshape(cores, PLANE, planes * count, 128)
    split_out = []
    start = 0
    for part in split:
        size = part.size // 128
        split_out.append(
            heads[:, :, start : start + size].reshape((cores, PLANE) + part.shape)
        )
        start += size
    rest = whole[:, :, count : count + half].swapaxes(0, 1).reshape(chips, cores * half, 128)
    shared_out = []
    start = 0
    for part in shared:
        size = part.size // 128
        shared_out.append(rest[:, start : start + size].reshape((chips,) + part.shape))
        start += size
    return (split_out, shared_out, jnp.sum(rest[:, start:], axis=0).reshape(-1), earlier)


def along_columns(parts):
    return parts.transpose(2, 0, 1, 3).reshape(parts.shape[2], -1)


def my_columns(value, axis):
    size = value.shape[axis] // PLANE
    return lax.dynamic_slice_in_dim(
        value, my_place() * size, size, axis, allow_negative_indices=False
    )


def by_place(value):
    return value.reshape(value.shape[0], PLANE, -1).swapaxes(0, 1)


def per_device(
    inputs,
    cotangent,
    attn_gain,
    query_matrix,
    key_matrix,
    value_matrix,
    output_matrix,
    query_first_factor,
    query_second_factor,
    key_first_factor,
    key_second_factor,
    value_first_factor,
    value_second_factor,
    output_first_factor,
    output_second_factor,
    query_feature,
    key_feature_layer,
    mlp_gain,
    gate_weight,
    up_weight,
    down_weight,
):
    micro, piece, width = inputs.shape
    chips = lax.axis_size("seq")
    rows = piece * lax.axis_size("tp")
    span = rows * chips
    head_width = query_feature.shape[1]
    group_size = query_feature.shape[0] // key_feature_layer.shape[0]
    rank = query_first_factor.shape[1]
    scale = 1.0 / math.sqrt(head_width)
    query_width = query_matrix.shape[1] // PLANE
    heads = query_width // head_width
    own = micro * piece
    blocks = micro * PLANE
    gain_in = attn_gain.astype(jnp.float32)
    gain_mid = mlp_gain.astype(jnp.float32)
    shrink_all = jnp.concatenate([query_first_factor, key_first_factor, value_first_factor], axis=1)
    expand_all = jnp.zeros((3 * rank, query_width + 2 * head_width), jnp.bfloat16)
    expand_all = expand_all.at[:rank, :query_width].set(my_columns(query_second_factor, 1))
    expand_all = expand_all.at[rank : 2 * rank, query_width : query_width + head_width].set(
        my_columns(key_second_factor, 1)
    )
    expand_all = expand_all.at[2 * rank :, query_width + head_width :].set(
        my_columns(value_second_factor, 1)
    )
    query_map = my_columns(query_feature, 0)
    key_map = my_columns(key_feature_layer, 0)[0]
    first_factor = my_columns(output_first_factor, 0)
    second_twice = output_second_factor * jnp.bfloat16(ADAPTER_SCALE)

    pieces = exchange_plane(
        jnp.concatenate(
            [
                by_place(query_matrix),
                by_place(key_matrix),
                by_place(value_matrix),
                by_place(output_matrix),
            ],
            axis=2,
        )
    )
    joined = query_width + 2 * head_width
    project_here = stack_planes(pieces[:, :, :joined].reshape(-1, joined))
    rows_in = inputs.astype(jnp.float32)
    scale_in = root_scale(rows_in)
    normed_input, project_here = gather_plane(
        after((rows_in * scale_in * gain_in).astype(jnp.bfloat16), pieces), project_here
    )
    cotangent_rows = cotangent.reshape(own, width)
    gate_dealt = deal_hidden(after(gate_weight, project_here))
    cotangent_all = gather_positions(after(to_relative(cotangent_rows), gate_dealt))
    up_dealt = deal_hidden(after(up_weight, gate_dealt))
    down_dealt = deal_hidden(after(down_weight, up_dealt))

    normed_flat = normed_input.reshape(blocks * rows, width)
    extended = dense_product(
        "tc,ck->tk", normed_flat, jnp.concatenate([project_here, shrink_all], axis=1)
    )
    shrunk = extended[:, joined:]
    shrunk_parts = halves(shrunk)
    expand_twice = expand_all * jnp.bfloat16(ADAPTER_SCALE)
    projected = extended[:, :joined] + dense_product(
        "tr,rk->tk", shrunk_parts, jnp.concatenate([expand_twice, expand_twice], axis=0)
    )
    positions = (
        jnp.arange(micro, dtype=jnp.int32)[:, None] * span
        + my_plane() * (PLANE * rows)
        + jnp.arange(PLANE * rows, dtype=jnp.int32)[None, :]
    )
    cosine_table, sine_table = rotary_tables(positions.reshape(-1), head_width)
    cosine_table = cosine_table.reshape(blocks, rows, -1)
    sine_table = sine_table.reshape(blocks, rows, -1)
    projected = projected.reshape(blocks, rows, joined)
    query_rows = apply_rotation(
        projected[..., :query_width].reshape(blocks, rows, heads, head_width),
        cosine_table[:, :, None],
        sine_table[:, :, None],
    ).astype(jnp.bfloat16)
    key_rows = apply_rotation(
        projected[..., query_width : query_width + head_width], cosine_table, sine_table
    ).astype(jnp.bfloat16)
    value_rows = projected[..., query_width + head_width :].astype(jnp.bfloat16)
    key_plus, key_minus = both_softmax(dense_product("ntd,de->nte", key_rows, key_map))
    key_features = jnp.concatenate([key_plus, key_minus], axis=-1).astype(jnp.bfloat16)
    carried = jnp.concatenate([key_rows, value_rows, key_features], axis=-1).reshape(
        micro, PLANE, rows, -1
    )
    arrived = from_block_before(carried[:, -1, rows - WIN :])
    window = windows(arrived, carried).reshape(blocks, WIN + rows, -1)
    keys_window = window[..., :head_width]
    values_window = window[..., head_width : 2 * head_width]
    features_window = window[..., 2 * head_width :]
    usable = jnp.logical_or(jnp.arange(blocks) > 0, my_plane() > 0)
    ones = jnp.ones((blocks, rows, 1), jnp.bfloat16)
    values_one = jnp.concatenate([value_rows, ones], axis=-1)
    states = dense_product("nbd,nbf->ndf", values_one, key_features)
    states = states.reshape((micro, PLANE) + states.shape[1:])
    outer = outer_sums(jnp.sum(states, axis=1), False)
    tails = window.reshape(micro, PLANE, WIN + rows, -1)[:, :, :WIN]
    tails_one = jnp.concatenate(
        [tails[..., head_width : 2 * head_width], jnp.ones((micro, PLANE, WIN, 1), jnp.bfloat16)],
        axis=-1,
    )
    prior = -dense_product("mpbd,mpbf->mpdf", tails_one, tails[..., 2 * head_width :])
    running = outer
    sums = []
    for place in range(PLANE):
        sums.append(running)
        running = running + states[:, place]
    prior = prior + jnp.stack(sums, axis=1)
    prior = halves(prior.reshape((blocks,) + prior.shape[2:]), 1)
    output_here = stack_planes(
        after(pieces[:, :, joined:].reshape(-1, query_width), prior)
    )
    gate_mine = widened(after(gate_dealt, prior))
    query_plus, query_minus = both_softmax(
        dense_product("nthd,hde->nthe", query_rows, query_map)
    )
    query_features = jnp.concatenate([query_plus, query_minus], axis=-1).astype(jnp.bfloat16)
    query_pos = lax.broadcasted_iota(jnp.int32, (rows, rows + WIN), 0)
    key_pos = lax.broadcasted_iota(jnp.int32, (rows, rows + WIN), 1)
    open_keys = jnp.logical_or(key_pos[None] >= WIN, usable[:, None, None])
    linear_mask = jnp.logical_and((key_pos <= query_pos)[None], open_keys)[:, :, None]
    window_mask = jnp.logical_and(
        jnp.logical_and(key_pos > query_pos, key_pos <= query_pos + WIN)[None], open_keys
    )[:, :, None]
    scores = dense_product("nthd,nbd->nthb", query_rows, keys_window) * scale
    similar = dense_product("nthf,nbf->nthb", query_features, features_window)
    exponent = jnp.where(window_mask, jnp.exp(scores), 0.0)
    weights_all = exponent + jnp.where(linear_mask, similar, 0.0)
    prior_rows = dense_product("nthf,nkf->nthk", query_features, prior)
    prior_rows = folded(prior_rows)
    divisor = jnp.sum(weights_all, axis=-1, keepdims=True) + prior_rows[..., head_width:]
    inverse = 1.0 / divisor
    ratio = weights_all * inverse
    shares = ratio.astype(jnp.bfloat16)
    prior_out = prior_rows[..., :head_width] * inverse
    mixed = (
        (dense_product("nthb,nbd->nthd", shares, values_window) + prior_out)
        .astype(jnp.bfloat16)
        .reshape(blocks * rows, query_width)
    )
    mixed, gate_mine, up_dealt, down_dealt = lax.optimization_barrier(
        (mixed, gate_mine, up_dealt, down_dealt)
    )
    up_mine = widened(after(up_dealt, gate_mine))
    low_rank = dense_product("tc,cr->tr", mixed, first_factor)
    low_parts = halves(low_rank)
    mixed_low = jnp.concatenate([mixed, low_parts], axis=1)
    branch = dense_product(
        "ta,wa->tw",
        mixed_low,
        jnp.concatenate([output_here, second_twice.T, second_twice.T], axis=1),
    )
    middle = (rows_in + sum_plane(sum_cores(branch.reshape(micro, PLANE, rows, width)))).reshape(own, width)
    scale_mid = root_scale(middle)
    middle, up_mine, cotangent_all = lax.optimization_barrier((middle, up_mine, cotangent_all))
    down_mine = widened(after(down_dealt, up_mine))
    project_ff = jnp.concatenate(
        [gate_mine, up_mine, swapped(gate_mine), swapped(up_mine)], axis=1
    )
    part = gate_mine.shape[1]

    normed_own = to_relative((middle * scale_mid * gain_mid).astype(jnp.bfloat16))
    step = own // CHUNKS
    down_here = jnp.concatenate([down_mine, swapped(down_mine)], axis=1)
    active_back = dense_product("td,df->tf", cotangent_all, down_here)
    active_back = active_back.reshape(MEMBERS, CHUNKS, step, -1)
    gathered, backs, actives, returned, firsts = [], [], [], [], []
    for chunk in range(CHUNKS):
        flip = chunk % 2 == 1
        mine = normed_own[chunk * step : (chunk + 1) * step]
        if chunk >= 2:
            mine = after(mine, gathered[chunk - 2])
        whole = gather_chips(mine, flip).reshape(MEMBERS * step, width)
        gathered.append(whole)
        both = dense_product("tc,cf->tf", whole, project_ff)
        gate = jnp.concatenate([both[:, :part], both[:, 2 * part : 3 * part]], axis=1)
        upper = jnp.concatenate([both[:, part : 2 * part], both[:, 3 * part :]], axis=1)
        logistic = jax.nn.sigmoid(gate)
        active = (gate * logistic * upper).astype(jnp.bfloat16)
        back = active_back[:, chunk].reshape(MEMBERS * step, -1)
        gate_back = (back * upper * logistic * (1.0 + gate * (1.0 - logistic))).astype(
            jnp.bfloat16
        )
        upper_back = (back * gate * logistic).astype(jnp.bfloat16)
        both_back = jnp.concatenate(
            [gate_back[:, :part], upper_back[:, :part], gate_back[:, part:], upper_back[:, part:]],
            axis=1,
        )
        partial = dense_product("tf,cf->tc", both_back, project_ff)
        summed, first = scatter_chips(partial.reshape(MEMBERS, step, width), flip)
        returned.append(summed)
        firsts.append(first)
        backs.append(both_back)
        actives.append(active.reshape(MEMBERS, step, -1))
    normed_all = jnp.concatenate(gathered)
    early = [after(item, firsts[-1]) for item in backs]
    active_all = jnp.stack(actives, axis=1).reshape(MEMBERS * own, -1)
    backs_all = jnp.concatenate(early)
    sends = (
        dense_product("tc,tf->cf", normed_all, backs_all[:, 2 * part :]).astype(jnp.bfloat16),
        dense_product("td,tf->df", cotangent_all, active_all[:, part:]).astype(jnp.bfloat16),
    )
    keeps = (
        dense_product("tc,tf->cf", normed_all, backs_all[:, : 2 * part]),
        dense_product("td,tf->df", cotangent_all, active_all[:, :part]),
    )
    sums = [
        (keep + swapped(send).astype(jnp.float32)).astype(jnp.bfloat16)
        for keep, send in zip(keeps, sends)
    ]
    mid_norm_back, both_sum, down_sum = lax.optimization_barrier(
        (jnp.concatenate(returned), sums[0], sums[1])
    )
    gate_part = narrowed(both_sum[:, :part])
    mid_norm_back = from_relative(mid_norm_back)
    mlp_gain_delta = jnp.sum(mid_norm_back * middle * scale_mid, axis=0)
    middle_back = cotangent_rows.astype(jnp.float32) + norm_back(
        mid_norm_back, middle, scale_mid, gain_mid
    )
    (branch_back,) = gather_plane(middle_back.astype(jnp.bfloat16).reshape(micro, piece, width))
    branch_back = branch_back.reshape(blocks * rows, width)
    extended_back = dense_product(
        "td,dk->tk", branch_back, jnp.concatenate([output_here, second_twice.T], axis=1)
    )
    lifted = extended_back[:, query_width:]
    lifted_parts = halves(lifted)
    first_pair = jnp.concatenate([first_factor, first_factor], axis=1)
    mixed_back = extended_back[:, :query_width] + dense_product(
        "tr,cr->tc", lifted_parts, first_pair
    )
    out_full = dense_product("td,tc->dc", branch_back, mixed_low)
    out_delta, output_second_delta = return_heads(
        jnp.concatenate(
            [out_full[:, :query_width], ADAPTER_SCALE * folded(out_full[:, query_width:])], axis=1
        ),
        query_width,
    )
    out_shrink_delta = folded(dense_product("tc,tr->cr", mixed, lifted_parts))
    heads_back = mixed_back.astype(jnp.bfloat16).reshape(blocks, rows, heads, head_width)
    shares_back = dense_product("nthd,nbd->nthb", heads_back, values_window)
    values_window_back = dense_product("nthb,nthd->nbd", shares, heads_back)
    heads_exact = heads_back.astype(jnp.float32)
    divisor_back = (
        -(
            jnp.sum(shares_back * ratio, axis=-1, keepdims=True)
            + jnp.sum(heads_exact * prior_out, axis=-1, keepdims=True)
        )
        * inverse
    )
    scaled_back = jnp.concatenate([heads_exact * inverse, divisor_back], axis=-1).astype(
        jnp.bfloat16
    )
    states_back = dense_product("nthk,nthf->nkf", scaled_back, query_features)
    states_back = states_back.reshape((micro, PLANE) + states_back.shape[1:])
    outer = outer_sums(jnp.sum(states_back, axis=1), True)
    next_first = from_block_behind(states_back[:, 0].astype(jnp.bfloat16)).astype(jnp.float32)
    running = outer
    sums = [None] * PLANE
    for place in reversed(range(PLANE)):
        behind = states_back[:, place + 1] if place + 1 < PLANE else next_first
        sums[place] = jnp.stack([running, running - behind], axis=1)
        running = running + states_back[:, place]
    later = jnp.stack(sums, axis=1)
    later = halves(later.reshape((2 * blocks,) + later.shape[3:]), 1)
    up_part = narrowed(after(both_sum[:, part:], gate_part))
    later, up_part = lax.optimization_barrier((later, up_part))
    down_rows = sum_positions(
        after(
            dense_product("tf,df->td", active_all, down_here).astype(jnp.bfloat16), branch_back
        )
    )
    project_low = jnp.concatenate(
        [after(project_here, states_back), shrink_all, shrink_all], axis=1
    )
    weights_back = shares_back * inverse + divisor_back
    scores_back = jnp.where(window_mask, weights_back * exponent, 0.0).astype(jnp.bfloat16)
    similar_back = jnp.where(linear_mask, weights_back, 0.0).astype(jnp.bfloat16)
    size = head_width + 1
    prior_state = prior[:, :head_width]
    prior_rest = prior[:, size : size + head_width]
    prior_norm = prior[:, head_width].astype(jnp.float32) + prior[:, size + head_width].astype(
        jnp.float32
    )
    query_features_back = (
        (
            dense_product("nthd,ndf->nthf", heads_back, prior_state)
            + dense_product("nthd,ndf->nthf", heads_back, prior_rest)
        )
        * inverse
        + divisor_back * prior_norm[:, None, None, :]
        + dense_product("nthb,nbf->nthf", similar_back, features_window)
    )
    features_window_back = dense_product("nthb,nthf->nbf", similar_back, query_features)
    queries_back = dense_product("nthb,nbd->nthd", scores_back, keys_window) * scale
    keys_window_back = dense_product("nthb,nthd->nbd", scores_back, query_rows) * scale
    halved_one = values_one.reshape(2 * blocks, rows // 2, head_width + 1)
    features_lead_back = dense_product(
        "nbk,nkf->nbf", jnp.concatenate([halved_one, halved_one], axis=-1), later
    ).reshape(blocks, rows, -1)
    values_lead_back = dense_product(
        "nbf,nkf->nbk", key_features.reshape(2 * blocks, rows // 2, -1), later
    )
    values_lead_back = folded(values_lead_back)[..., :head_width].reshape(blocks, rows, -1)
    window_back = jnp.concatenate(
        [keys_window_back, values_window_back, features_window_back], axis=-1
    ).reshape(micro, PLANE, WIN + rows, -1)
    arriving = from_block_behind(window_back[:, 0, :WIN].astype(jnp.bfloat16))
    following = jnp.concatenate(
        [window_back[:, 1:, :WIN], arriving[:, None].astype(jnp.float32)], axis=1
    )
    carried_back = jnp.concatenate(
        [window_back[:, :, WIN:rows], window_back[:, :, rows:] + following], axis=2
    ).reshape(blocks, rows, -1)
    keys_back = carried_back[..., :head_width]
    values_back = carried_back[..., head_width : 2 * head_width] + values_lead_back
    down_part = narrowed(after(down_sum, up_part))
    carried_back, down_part, down_rows = lax.optimization_barrier(
        (carried_back, down_part, down_rows)
    )
    key_logits_back = both_softmax_back(
        key_plus, key_minus, carried_back[..., 2 * head_width :] + features_lead_back
    ).astype(jnp.bfloat16)
    query_logits_back = both_softmax_back(query_plus, query_minus, query_features_back).astype(
        jnp.bfloat16
    )
    key_feature_delta = dense_product("ntd,nte->de", key_rows, key_logits_back)
    query_feature_delta = dense_product("nthd,nthe->hde", query_rows, query_logits_back)
    keys_back = keys_back + dense_product("nte,de->ntd", key_logits_back, key_map)
    queries_back = queries_back + dense_product("nthe,hde->nthd", query_logits_back, query_map)
    projected_back = jnp.concatenate(
        [
            apply_rotation(queries_back, cosine_table[:, :, None], -sine_table[:, :, None])
            .astype(jnp.bfloat16)
            .reshape(blocks * rows, query_width),
            apply_rotation(keys_back, cosine_table, -sine_table)
            .astype(jnp.bfloat16)
            .reshape(blocks * rows, head_width),
            values_back.astype(jnp.bfloat16).reshape(blocks * rows, head_width),
        ],
        axis=-1,
    )
    projected_back, out_delta = lax.optimization_barrier((projected_back, out_delta))
    gate_delta, up_delta, down_delta = deal_back((gate_part, up_part, down_part), width // chips)
    lift_all = dense_product("tk,rk->tr", projected_back, expand_twice)
    back_low = jnp.concatenate([projected_back, halves(lift_all)], axis=1)
    normed_back = dense_product("tk,ck->tc", back_low, project_low)
    normed_back, gate_delta, up_delta, down_delta = lax.optimization_barrier(
        (normed_back, gate_delta, up_delta, down_delta)
    )
    normed_pair = sum_cores(normed_back.reshape(micro, PLANE, rows, width))
    project_full = after(dense_product("tc,tk->ck", normed_flat, back_low), normed_pair)
    project_delta, shrink_delta = return_heads(
        jnp.concatenate([project_full[:, :joined], folded(project_full[:, joined:])], axis=1),
        joined,
    )
    expand_delta = dense_product("tr,tk->rk", shrunk_parts, projected_back)
    expand_delta = ADAPTER_SCALE * (expand_delta[: 3 * rank] + expand_delta[3 * rank :])
    in_norm_back = sum_plane(normed_pair)
    down_rows, middle_late, in_norm_back = lax.optimization_barrier(
        (down_rows, middle, in_norm_back)
    )
    results = middle_late + from_relative(down_rows).astype(jnp.float32)
    attn_gain_delta = jnp.sum(in_norm_back * rows_in * scale_in, axis=(0, 1))
    inputs_back = middle_back.reshape(micro, piece, width) + norm_back(
        in_norm_back, rows_in, scale_in, gain_in
    )
    split, shared, gain_totals, (gate_delta, up_delta, down_delta) = total_heads(
        (
            expand_delta[:rank, :query_width],
            expand_delta[rank : 2 * rank, query_width : query_width + head_width],
            expand_delta[2 * rank :, query_width + head_width :],
            out_shrink_delta,
            query_feature_delta,
            key_feature_delta,
        ),
        (shrink_delta, output_second_delta),
        jnp.concatenate([attn_gain_delta, mlp_gain_delta]),
        (gate_delta, up_delta, down_delta),
    )
    shrink_total = shared[0].swapaxes(1, 2).reshape(width, 3 * rank)
    return (
        results.astype(jnp.bfloat16).reshape(micro, piece, width),
        inputs_back,
        gain_totals[:width],
        project_delta[:, :, :query_width].reshape(-1, PLANE * query_width),
        project_delta[:, :, query_width : query_width + head_width].reshape(
            -1, PLANE * head_width
        ),
        project_delta[:, :, query_width + head_width :].reshape(-1, PLANE * head_width),
        out_delta.reshape(-1, PLANE * query_width),
        shrink_total[:, :rank],
        along_columns(split[0]),
        shrink_total[:, rank : 2 * rank],
        along_columns(split[1]),
        shrink_total[:, 2 * rank :],
        along_columns(split[2]),
        split[3].reshape(-1, rank),
        shared[1].swapaxes(0, 1).reshape(rank, width),
        split[4].reshape(-1, head_width, head_width),
        split[5].reshape(-1, head_width, head_width),
        gain_totals[width:],
        gate_delta,
        up_delta,
        down_delta,
    )


def solution(mesh):
    return jax.shard_map(
        per_device,
        mesh=mesh,
        in_specs=(
            P(None, ("seq", "tp"), None),
            P(None, ("seq", "tp"), None),
            P(),
            P("seq", "tp"),
            P("seq", "tp"),
            P("seq", "tp"),
            P("seq", "tp"),
            P(),
            P(None, "tp"),
            P(),
            P(None, "tp"),
            P(),
            P(None, "tp"),
            P("tp", None),
            P(),
            P("tp", None, None),
            P("tp", None, None),
            P(),
            P("seq", "tp"),
            P("seq", "tp"),
            P("seq", "tp"),
        ),
        out_specs=(
            P(None, ("seq", "tp"), None),
            P(None, ("seq", "tp"), None),
            P(),
            P("seq", "tp"),
            P("seq", "tp"),
            P("seq", "tp"),
            P("seq", "tp"),
            P(),
            P(),
            P(),
            P(),
            P(),
            P(),
            P(),
            P(),
            P(),
            P(),
            P(),
            P("seq", "tp"),
            P("seq", "tp"),
            P("seq", "tp"),
        ),
        check_vma=False,
    )
```

```python
import math

import jax
import jax.numpy as jnp
from jax import lax
from jax.sharding import PartitionSpec as P

WIN = 64


EPS = 1e-05
ADAPTER_SCALE = 2.0
ROPE_BASE = 500000.0

PLANE = 4
CHUNKS = 2
MEMBERS = 8


def dense_product(form, left, right):
    return jnp.einsum(form, left, right, preferred_element_type=jnp.float32)


def halves(value, axis=-1):
    high = lax.reduce_precision(value, 8, 7)
    return jnp.concatenate(
        [high.astype(jnp.bfloat16), (value - high).astype(jnp.bfloat16)], axis=axis
    )


def folded(value):
    size = value.shape[-1] // 2
    return value[..., :size] + value[..., size:]


def root_scale(value_rows):
    return lax.rsqrt(jnp.mean(value_rows * value_rows, axis=-1, keepdims=True) + EPS)


def norm_back(grad_normed, value_rows, scale, gain):
    gained = grad_normed * gain
    inner = jnp.mean(gained * value_rows, axis=-1, keepdims=True)
    return scale * gained - value_rows * (scale * scale * scale) * inner


def rotary_tables(positions, width):
    half = width // 2
    inverse = ROPE_BASE ** (-(jnp.arange(half, dtype=jnp.float32) * (2.0 / width)))
    angles = positions.astype(jnp.float32)[:, None] * inverse[None, :]
    return (jnp.cos(angles), jnp.sin(angles))


def apply_rotation(value_rows, cosine_table, sine_table):
    half = value_rows.shape[-1] // 2
    first = value_rows[..., :half]
    second = value_rows[..., half:]
    return jnp.concatenate(
        [first * cosine_table - second * sine_table, second * cosine_table + first * sine_table],
        axis=-1,
    )


def both_softmax(logits):
    return (jax.nn.softmax(logits, axis=-1), jax.nn.softmax(-logits, axis=-1))


def both_softmax_back(plus, minus, grads):
    width = plus.shape[-1]
    grad_plus = grads[..., :width]
    grad_minus = grads[..., width:]
    return plus * (grad_plus - jnp.sum(grad_plus * plus, axis=-1, keepdims=True)) - minus * (
        grad_minus - jnp.sum(grad_minus * minus, axis=-1, keepdims=True)
    )


def after(value, *earlier):
    return lax.optimization_barrier((value,) + earlier)[0]


def plane_count():
    return lax.axis_size("seq") // PLANE


def my_plane():
    return lax.div(lax.axis_index("seq"), jnp.int32(PLANE))


def my_place():
    return lax.rem(lax.axis_index("seq"), jnp.int32(PLANE))


def plane_before(by):
    planes = plane_count()
    return lax.rem(my_plane() + jnp.int32(planes - by), jnp.int32(planes))


def at_block(blocks, index):
    return lax.dynamic_index_in_dim(blocks, index, 0, False, allow_negative_indices=False)


def swapped(value):
    return lax.ppermute(value, "tp", [(0, 1), (1, 0)])


def swapped_parts(value):
    return jnp.concatenate(
        [swapped(value[:, part : part + 1]) for part in range(0, PLANE, 1)], axis=1
    )


def opposite(value, bit):
    return lax.ppermute(value, "seq", [(i, i ^ bit) for i in range(lax.axis_size("seq"))])


def from_plane_before(value, by):
    size = lax.axis_size("seq")
    return lax.ppermute(value, "seq", [(i, (i + by * PLANE) % size) for i in range(size)])


def in_order(mine, other, upper, axis):
    return jnp.stack([jnp.where(upper, other, mine), jnp.where(upper, mine, other)], axis=axis)


def split_half(value, upper, axis):
    index = upper.astype(jnp.int32)
    return (
        lax.dynamic_index_in_dim(value, index, axis, False, allow_negative_indices=False),
        lax.dynamic_index_in_dim(value, 1 - index, axis, False, allow_negative_indices=False),
    )


def upper_bit(bit):
    return (my_place() & bit) > 0


def upper_core():
    return lax.axis_index("tp") > 0


def gather_plane(own, *others):
    micro, piece, width = own.shape
    parts = []
    for part in range(micro):
        value = own[part]
        if part % 2 == 0:
            value = in_order(value, opposite(value, 1), upper_bit(1), 0)
            value = in_order(value, opposite(value, 2), upper_bit(2), 0)
        else:
            value = in_order(value, opposite(value, 2), upper_bit(2), 0)
            value = in_order(value, opposite(value, 1), upper_bit(1), 1)
        parts.append(value.reshape(PLANE, piece, width))
    rows, *others = lax.optimization_barrier((jnp.stack(parts),) + others)
    rows = in_order(rows, swapped_parts(rows), upper_core(), 2)
    return (rows.reshape(micro, PLANE, 2 * piece, width), *others)


def sum_cores(partial):
    micro, places, rows, width = partial.shape
    keep, send = split_half(
        partial.reshape(micro, places, 2, rows // 2, width), upper_core(), 2
    )
    return keep + swapped_parts(send.astype(jnp.bfloat16)).astype(jnp.float32)


def sum_plane(summed):
    micro, places, rows, width = summed.shape
    summed = summed.reshape(micro, 2, 2, rows, width)
    parts = []
    for part in range(micro):
        value = summed[part]
        for bit, axis in ((1, 1), (2, 0)) if part % 2 == 0 else ((2, 0), (1, 0)):
            keep, send = split_half(value, upper_bit(bit), axis)
            value = keep + opposite(send.astype(jnp.bfloat16), bit).astype(jnp.float32)
        parts.append(value)
    return jnp.stack(parts)


def place_groups():
    chips = lax.axis_size("seq")
    return [list(range(first, first + PLANE)) for first in range(0, chips, PLANE)]


def exchange_plane(pieces):
    return lax.all_to_all(
        pieces, "seq", 0, 0, tiled=True, axis_index_groups=place_groups()
    )


def stack_planes(value):
    planes = plane_count()
    whole = jnp.zeros((planes,) + value.shape, value.dtype)
    for by in range(planes):
        piece = from_plane_before(value, by) if by else value
        whole = lax.dynamic_update_slice_in_dim(
            whole, piece[None], plane_before(by), 0, allow_negative_indices=False
        )
    return whole.reshape((-1,) + value.shape[1:])


def return_heads(delta, columns):
    planes = plane_count()
    blocks = delta.astype(jnp.bfloat16).reshape(planes, -1, delta.shape[1])
    total = at_block(blocks, my_plane()).astype(jnp.float32)
    for by in range(1, planes):
        send = at_block(blocks, plane_before(by))
        total = total + from_plane_before(send, planes - by).astype(jnp.float32)
    pieces = exchange_plane(
        total.astype(jnp.bfloat16).reshape(PLANE, -1, delta.shape[1])
    )
    pieces = pieces.astype(jnp.float32)
    return (pieces[:, :, :columns].swapaxes(0, 1), jnp.sum(pieces[:, :, columns:], axis=0).T)


def outer_sums(total, later):
    micro = total.shape[0]
    planes = plane_count()
    total = total.astype(jnp.bfloat16)
    pieces = jnp.stack([total] + [from_plane_before(total, by) for by in range(1, planes)])
    source = lax.rem(my_plane() + planes - jnp.arange(planes), jnp.int32(planes))
    part = jnp.arange(micro)
    if later:
        beside = source[:, None, None] > my_plane()
        beyond = part[None, :, None] > part[None, None, :]
    else:
        beside = source[:, None, None] < my_plane()
        beyond = part[None, :, None] < part[None, None, :]
    same = part[None, :, None] == part[None, None, :]
    chosen = jnp.logical_or(beyond, jnp.logical_and(same, beside)).astype(jnp.bfloat16)
    return dense_product("kab,karl->brl", chosen, pieces)


def from_block_before(last):
    arrived = from_plane_before(last, 1)
    wrapped = jnp.concatenate([jnp.zeros_like(arrived[:1]), arrived[:-1]], axis=0)
    return jnp.where(my_plane() == 0, wrapped, arrived)


def from_block_behind(first):
    planes = plane_count()
    arrived = from_plane_before(first, planes - 1)
    wrapped = jnp.concatenate([arrived[1:], jnp.zeros_like(arrived[:1])], axis=0)
    return jnp.where(my_plane() == planes - 1, wrapped, arrived)


def windows(arrived, blocks):
    rows = blocks.shape[2]
    tails = jnp.concatenate([arrived[:, None], blocks[:, :-1, rows - WIN :]], axis=1)
    return jnp.concatenate([tails, blocks], axis=2)


def upper_chip(bit):
    return (lax.axis_index("seq") & bit) > 0


def position_bits():
    chips = lax.axis_size("seq")
    return [bit for bit in (4, 16, 32, 64, 128, 256) if bit < chips]


def hidden_groups():
    groups = {}
    for chip in range(lax.axis_size("seq")):
        groups.setdefault(chip & ~11, []).append(chip)
    return list(groups.values())


def gather_chips(value, flip):
    blocks = in_order(value, opposite(value, 8), upper_chip(8), 0)
    if flip:
        blocks = in_order(blocks, opposite(blocks, 1), upper_chip(1), 1)
        blocks = in_order(blocks, opposite(blocks, 2), upper_chip(2), 1)
    else:
        blocks = in_order(blocks, opposite(blocks, 2), upper_chip(2), 1)
        blocks = in_order(blocks, opposite(blocks, 1), upper_chip(1), 2)
    return blocks.reshape((MEMBERS,) + value.shape)


def halved(value, bit, axis):
    keep, send = split_half(value, upper_chip(bit), axis)
    return keep.astype(jnp.float32) + opposite(send.astype(jnp.bfloat16), bit).astype(jnp.float32)


def scatter_chips(partial, flip):
    value = partial.reshape((2, 2, 2) + partial.shape[1:])
    bit, axis = (2, 1) if flip else (1, 2)
    keep, send = split_half(value, upper_chip(bit), axis)
    send = send.astype(jnp.bfloat16)
    value = keep.astype(jnp.float32) + opposite(send, bit).astype(jnp.float32)
    value = halved(value, 3 - bit, 1)
    return (halved(value, 8, 0), send)


def exchange(value):
    return lax.all_to_all(value, "seq", 0, 0, tiled=True)


def exchange_members(value):
    return lax.all_to_all(
        value, "seq", 0, 0, tiled=True, axis_index_groups=hidden_groups()
    )


def flipped(value):
    for axis, bit in enumerate(reversed(position_bits())):
        value = jnp.where(upper_chip(bit), jnp.flip(value, axis + 1), value)
    return value


def to_relative(value):
    rows, width = value.shape
    count = len(position_bits())
    value = value.reshape((rows,) + (2,) * (count + 1) + (-1,))
    return flipped(value.swapaxes(count, count + 1)).reshape(rows, width)


def from_relative(value):
    rows, width = value.shape
    count = len(position_bits())
    value = flipped(value.reshape((rows,) + (2,) * (count + 1) + (-1,)))
    return value.swapaxes(count, count + 1).reshape(rows, width)


def deal_hidden(local):
    rows, hidden = local.shape
    pieces = local.reshape(rows, MEMBERS, hidden // MEMBERS).swapaxes(0, 1)
    return exchange_members(pieces).reshape(MEMBERS * rows, -1)


def widened(value):
    for bit in position_bits():
        value = jnp.concatenate([value, opposite(value, bit)], axis=0)
    return value


def narrowed(value):
    for bit in reversed(position_bits()):
        half = value.shape[0] // 2
        arrived = opposite(value[half:].astype(jnp.bfloat16), bit)
        value = (value[:half].astype(jnp.float32) + arrived.astype(jnp.float32)).astype(
            jnp.bfloat16
        )
    return value


def deal_back(values, rows):
    back = exchange_members(
        jnp.stack([value.reshape(MEMBERS, rows, -1) for value in values], axis=1)
    )
    return tuple(
        back[:, index].swapaxes(0, 1).reshape(rows, -1).astype(jnp.float32)
        for index in range(len(values))
    )


def gather_positions(rows):
    return lax.all_gather(
        rows, "seq", axis=0, tiled=True, axis_index_groups=hidden_groups()
    )


def sum_positions(partial):
    return lax.psum_scatter(
        partial, "seq", scatter_dimension=0, tiled=True, axis_index_groups=hidden_groups()
    )


def lanes(value):
    return value.reshape(-1, 128)


def everywhere(value):
    chips = lax.axis_size("seq")
    whole = exchange(jnp.broadcast_to(value[None], (chips,) + value.shape))
    return in_order(whole, swapped(whole), upper_core(), 0)


def total_heads(split, shared, gain, earlier):
    planes = plane_count()
    flat = jnp.concatenate([lanes(part) for part in split], axis=0)
    count = -(-flat.shape[0] // planes)
    flat = jnp.pad(flat, ((0, count * planes - flat.shape[0]), (0, 0)))
    flat = flat.reshape(planes, count, 128)
    mine = at_block(flat, my_plane())
    for by in range(1, planes):
        mine = mine + from_plane_before(at_block(flat, plane_before(by)), planes - by)
    both = jnp.concatenate([lanes(part) for part in shared] + [lanes(gain)], axis=0)
    keep, send = split_half(both.reshape(2, -1, 128), upper_core(), 0)
    both = keep + swapped(send)
    half = both.shape[0]
    payload = jnp.concatenate([mine, both], axis=0)
    payload = jnp.pad(payload, ((0, -payload.shape[0] % 8), (0, 0)))
    whole = everywhere(payload)
    cores, chips = whole.shape[:2]
    heads = whole[:, :, :count].reshape(cores, planes, PLANE, count, 128)
    heads = heads.swapaxes(1, 2).reshape(cores, PLANE, planes * count, 128)
    split_out = []
    start = 0
    for part in split:
        size = part.size // 128
        split_out.append(
            heads[:, :, start : start + size].reshape((cores, PLANE) + part.shape)
        )
        start += size
    rest = whole[:, :, count : count + half].swapaxes(0, 1).reshape(chips, cores * half, 128)
    shared_out = []
    start = 0
    for part in shared:
        size = part.size // 128
        shared_out.append(rest[:, start : start + size].reshape((chips,) + part.shape))
        start += size
    return (split_out, shared_out, jnp.sum(rest[:, start:], axis=0).reshape(-1), earlier)


def along_columns(parts):
    return parts.transpose(2, 0, 1, 3).reshape(parts.shape[2], -1)


def my_columns(value, axis):
    size = value.shape[axis] // PLANE
    return lax.dynamic_slice_in_dim(
        value, my_place() * size, size, axis, allow_negative_indices=False
    )


def by_place(value):
    return value.reshape(value.shape[0], PLANE, -1).swapaxes(0, 1)


def per_device(
    inputs,
    cotangent,
    attn_gain,
    query_matrix,
    key_matrix,
    value_matrix,
    output_matrix,
    query_first_factor,
    query_second_factor,
    key_first_factor,
    key_second_factor,
    value_first_factor,
    value_second_factor,
    output_first_factor,
    output_second_factor,
    query_feature,
    key_feature_layer,
    mlp_gain,
    gate_weight,
    up_weight,
    down_weight,
):
    micro, piece, width = inputs.shape
    chips = lax.axis_size("seq")
    rows = piece * lax.axis_size("tp")
    span = rows * chips
    head_width = query_feature.shape[1]
    group_size = query_feature.shape[0] // key_feature_layer.shape[0]
    rank = query_first_factor.shape[1]
    scale = 1.0 / math.sqrt(head_width)
    query_width = query_matrix.shape[1] // PLANE
    heads = query_width // head_width
    own = micro * piece
    blocks = micro * PLANE
    gain_in = attn_gain.astype(jnp.float32)
    gain_mid = mlp_gain.astype(jnp.float32)
    shrink_all = jnp.concatenate([query_first_factor, key_first_factor, value_first_factor], axis=1)
    expand_all = jnp.zeros((3 * rank, query_width + 2 * head_width), jnp.bfloat16)
    expand_all = expand_all.at[:rank, :query_width].set(my_columns(query_second_factor, 1))
    expand_all = expand_all.at[rank : 2 * rank, query_width : query_width + head_width].set(
        my_columns(key_second_factor, 1)
    )
    expand_all = expand_all.at[2 * rank :, query_width + head_width :].set(
        my_columns(value_second_factor, 1)
    )
    query_map = my_columns(query_feature, 0)
    key_map = my_columns(key_feature_layer, 0)[0]
    first_factor = my_columns(output_first_factor, 0)
    second_twice = output_second_factor * jnp.bfloat16(ADAPTER_SCALE)

    pieces = exchange_plane(
        jnp.concatenate(
            [
                by_place(query_matrix),
                by_place(key_matrix),
                by_place(value_matrix),
                by_place(output_matrix),
            ],
            axis=2,
        )
    )
    joined = query_width + 2 * head_width
    project_here = stack_planes(pieces[:, :, :joined].reshape(-1, joined))
    rows_in = inputs.astype(jnp.float32)
    scale_in = root_scale(rows_in)
    normed_input, project_here = gather_plane(
        after((rows_in * scale_in * gain_in).astype(jnp.bfloat16), pieces), project_here
    )
    cotangent_rows = cotangent.reshape(own, width)
    gate_dealt = deal_hidden(after(gate_weight, project_here))
    cotangent_all = gather_positions(after(to_relative(cotangent_rows), gate_dealt))
    up_dealt = deal_hidden(after(up_weight, gate_dealt))
    down_dealt = deal_hidden(after(down_weight, up_dealt))

    normed_flat = normed_input.reshape(blocks * rows, width)
    extended = dense_product(
        "tc,ck->tk", normed_flat, jnp.concatenate([project_here, shrink_all], axis=1)
    )
    shrunk = extended[:, joined:]
    shrunk_parts = halves(shrunk)
    expand_twice = expand_all * jnp.bfloat16(ADAPTER_SCALE)
    projected = extended[:, :joined] + dense_product(
        "tr,rk->tk", shrunk_parts, jnp.concatenate([expand_twice, expand_twice], axis=0)
    )
    positions = (
        jnp.arange(micro, dtype=jnp.int32)[:, None] * span
        + my_plane() * (PLANE * rows)
        + jnp.arange(PLANE * rows, dtype=jnp.int32)[None, :]
    )
    cosine_table, sine_table = rotary_tables(positions.reshape(-1), head_width)
    cosine_table = cosine_table.reshape(blocks, rows, -1)
    sine_table = sine_table.reshape(blocks, rows, -1)
    projected = projected.reshape(blocks, rows, joined)
    query_rows = apply_rotation(
        projected[..., :query_width].reshape(blocks, rows, heads, head_width),
        cosine_table[:, :, None],
        sine_table[:, :, None],
    ).astype(jnp.bfloat16)
    key_rows = apply_rotation(
        projected[..., query_width : query_width + head_width], cosine_table, sine_table
    ).astype(jnp.bfloat16)
    value_rows = projected[..., query_width + head_width :].astype(jnp.bfloat16)
    key_plus, key_minus = both_softmax(dense_product("ntd,de->nte", key_rows, key_map))
    key_features = jnp.concatenate([key_plus, key_minus], axis=-1).astype(jnp.bfloat16)
    carried = jnp.concatenate([key_rows, value_rows, key_features], axis=-1).reshape(
        micro, PLANE, rows, -1
    )
    arrived = from_block_before(carried[:, -1, rows - WIN :])
    window = windows(arrived, carried).reshape(blocks, WIN + rows, -1)
    keys_window = window[..., :head_width]
    values_window = window[..., head_width : 2 * head_width]
    features_window = window[..., 2 * head_width :]
    usable = jnp.logical_or(jnp.arange(blocks) > 0, my_plane() > 0)
    ones = jnp.ones((blocks, rows, 1), jnp.bfloat16)
    values_one = jnp.concatenate([value_rows, ones], axis=-1)
    states = dense_product("nbd,nbf->ndf", values_one, key_features)
    states = states.reshape((micro, PLANE) + states.shape[1:])
    outer = outer_sums(jnp.sum(states, axis=1), False)
    tails = window.reshape(micro, PLANE, WIN + rows, -1)[:, :, :WIN]
    tails_one = jnp.concatenate(
        [tails[..., head_width : 2 * head_width], jnp.ones((micro, PLANE, WIN, 1), jnp.bfloat16)],
        axis=-1,
    )
    prior = -dense_product("mpbd,mpbf->mpdf", tails_one, tails[..., 2 * head_width :])
    running = outer
    sums = []
    for place in range(PLANE):
        sums.append(running)
        running = running + states[:, place]
    prior = prior + jnp.stack(sums, axis=1)
    prior = halves(prior.reshape((blocks,) + prior.shape[2:]), 1)
    output_here = stack_planes(
        after(pieces[:, :, joined:].reshape(-1, query_width), prior)
    )
    gate_mine = widened(after(gate_dealt, prior))
    query_plus, query_minus = both_softmax(
        dense_product("nthd,hde->nthe", query_rows, query_map)
    )
    query_features = jnp.concatenate([query_plus, query_minus], axis=-1).astype(jnp.bfloat16)
    query_pos = lax.broadcasted_iota(jnp.int32, (rows, rows + WIN), 0)
    key_pos = lax.broadcasted_iota(jnp.int32, (rows, rows + WIN), 1)
    open_keys = jnp.logical_or(key_pos[None] >= WIN, usable[:, None, None])
    linear_mask = jnp.logical_and((key_pos <= query_pos)[None], open_keys)[:, :, None]
    window_mask = jnp.logical_and(
        jnp.logical_and(key_pos > query_pos, key_pos <= query_pos + WIN)[None], open_keys
    )[:, :, None]
    scores = dense_product("nthd,nbd->nthb", query_rows, keys_window) * scale
    similar = dense_product("nthf,nbf->nthb", query_features, features_window)
    exponent = jnp.where(window_mask, jnp.exp(scores), 0.0)
    weights_all = exponent + jnp.where(linear_mask, similar, 0.0)
    prior_rows = dense_product("nthf,nkf->nthk", query_features, prior)
    prior_rows = folded(prior_rows)
    divisor = jnp.sum(weights_all, axis=-1, keepdims=True) + prior_rows[..., head_width:]
    inverse = 1.0 / divisor
    ratio = weights_all * inverse
    shares = ratio.astype(jnp.bfloat16)
    prior_out = prior_rows[..., :head_width] * inverse
    mixed = (
        (dense_product("nthb,nbd->nthd", shares, values_window) + prior_out)
        .astype(jnp.bfloat16)
        .reshape(blocks * rows, query_width)
    )
    mixed, gate_mine, up_dealt, down_dealt = lax.optimization_barrier(
        (mixed, gate_mine, up_dealt, down_dealt)
    )
    up_mine = widened(after(up_dealt, gate_mine))
    low_rank = dense_product("tc,cr->tr", mixed, first_factor)
    low_parts = halves(low_rank)
    mixed_low = jnp.concatenate([mixed, low_parts], axis=1)
    branch = dense_product(
        "ta,wa->tw",
        mixed_low,
        jnp.concatenate([output_here, second_twice.T, second_twice.T], axis=1),
    )
    middle = (rows_in + sum_plane(sum_cores(branch.reshape(micro, PLANE, rows, width)))).reshape(own, width)
    scale_mid = root_scale(middle)
    middle, up_mine, cotangent_all = lax.optimization_barrier((middle, up_mine, cotangent_all))
    down_mine = widened(after(down_dealt, up_mine))
    project_ff = jnp.concatenate(
        [gate_mine, up_mine, swapped(gate_mine), swapped(up_mine)], axis=1
    )
    part = gate_mine.shape[1]

    normed_own = to_relative((middle * scale_mid * gain_mid).astype(jnp.bfloat16))
    step = own // CHUNKS
    down_here = jnp.concatenate([down_mine, swapped(down_mine)], axis=1)
    active_back = dense_product("td,df->tf", cotangent_all, down_here)
    active_back = active_back.reshape(MEMBERS, CHUNKS, step, -1)
    gathered, backs, actives, returned, firsts = [], [], [], [], []
    for chunk in range(CHUNKS):
        flip = chunk % 2 == 1
        mine = normed_own[chunk * step : (chunk + 1) * step]
        if chunk >= 2:
            mine = after(mine, gathered[chunk - 2])
        whole = gather_chips(mine, flip).reshape(MEMBERS * step, width)
        gathered.append(whole)
        both = dense_product("tc,cf->tf", whole, project_ff)
        gate = jnp.concatenate([both[:, :part], both[:, 2 * part : 3 * part]], axis=1)
        upper = jnp.concatenate([both[:, part : 2 * part], both[:, 3 * part :]], axis=1)
        logistic = jax.nn.sigmoid(gate)
        active = (gate * logistic * upper).astype(jnp.bfloat16)
        back = active_back[:, chunk].reshape(MEMBERS * step, -1)
        gate_back = (back * upper * logistic * (1.0 + gate * (1.0 - logistic))).astype(
            jnp.bfloat16
        )
        upper_back = (back * gate * logistic).astype(jnp.bfloat16)
        both_back = jnp.concatenate(
            [gate_back[:, :part], upper_back[:, :part], gate_back[:, part:], upper_back[:, part:]],
            axis=1,
        )
        partial = dense_product("tf,cf->tc", both_back, project_ff)
        summed, first = scatter_chips(partial.reshape(MEMBERS, step, width), flip)
        returned.append(summed)
        firsts.append(first)
        backs.append(both_back)
        actives.append(active.reshape(MEMBERS, step, -1))
    normed_all = jnp.concatenate(gathered)
    early = [after(item, firsts[-1]) for item in backs]
    active_all = jnp.stack(actives, axis=1).reshape(MEMBERS * own, -1)
    backs_all = jnp.concatenate(early)
    sends = (
        dense_product("tc,tf->cf", normed_all, backs_all[:, 2 * part :]).astype(jnp.bfloat16),
        dense_product("td,tf->df", cotangent_all, active_all[:, part:]).astype(jnp.bfloat16),
    )
    keeps = (
        dense_product("tc,tf->cf", normed_all, backs_all[:, : 2 * part]),
        dense_product("td,tf->df", cotangent_all, active_all[:, :part]),
    )
    sums = [
        (keep + swapped(send).astype(jnp.float32)).astype(jnp.bfloat16)
        for keep, send in zip(keeps, sends)
    ]
    mid_norm_back, both_sum, down_sum = lax.optimization_barrier(
        (jnp.concatenate(returned), sums[0], sums[1])
    )
    gate_part = narrowed(both_sum[:, :part])
    mid_norm_back = from_relative(mid_norm_back)
    mlp_gain_delta = jnp.sum(mid_norm_back * middle * scale_mid, axis=0)
    middle_back = cotangent_rows.astype(jnp.float32) + norm_back(
        mid_norm_back, middle, scale_mid, gain_mid
    )
    (branch_back,) = gather_plane(middle_back.astype(jnp.bfloat16).reshape(micro, piece, width))
    branch_back = branch_back.reshape(blocks * rows, width)
    extended_back = dense_product(
        "td,dk->tk", branch_back, jnp.concatenate([output_here, second_twice.T], axis=1)
    )
    lifted = extended_back[:, query_width:]
    lifted_parts = halves(lifted)
    first_pair = jnp.concatenate([first_factor, first_factor], axis=1)
    mixed_back = extended_back[:, :query_width] + dense_product(
        "tr,cr->tc", lifted_parts, first_pair
    )
    out_full = dense_product("td,tc->dc", branch_back, mixed_low)
    out_delta, output_second_delta = return_heads(
        jnp.concatenate(
            [out_full[:, :query_width], ADAPTER_SCALE * folded(out_full[:, query_width:])], axis=1
        ),
        query_width,
    )
    out_shrink_delta = folded(dense_product("tc,tr->cr", mixed, lifted_parts))
    heads_back = mixed_back.astype(jnp.bfloat16).reshape(blocks, rows, heads, head_width)
    shares_back = dense_product("nthd,nbd->nthb", heads_back, values_window)
    values_window_back = dense_product("nthb,nthd->nbd", shares, heads_back)
    heads_exact = heads_back.astype(jnp.float32)
    divisor_back = (
        -(
            jnp.sum(shares_back * ratio, axis=-1, keepdims=True)
            + jnp.sum(heads_exact * prior_out, axis=-1, keepdims=True)
        )
        * inverse
    )
    scaled_back = jnp.concatenate([heads_exact * inverse, divisor_back], axis=-1).astype(
        jnp.bfloat16
    )
    states_back = dense_product("nthk,nthf->nkf", scaled_back, query_features)
    states_back = states_back.reshape((micro, PLANE) + states_back.shape[1:])
    outer = outer_sums(jnp.sum(states_back, axis=1), True)
    next_first = from_block_behind(states_back[:, 0].astype(jnp.bfloat16)).astype(jnp.float32)
    running = outer
    sums = [None] * PLANE
    for place in reversed(range(PLANE)):
        behind = states_back[:, place + 1] if place + 1 < PLANE else next_first
        sums[place] = jnp.stack([running, running - behind], axis=1)
        running = running + states_back[:, place]
    later = jnp.stack(sums, axis=1)
    later = halves(later.reshape((2 * blocks,) + later.shape[3:]), 1)
    up_part = narrowed(after(both_sum[:, part:], gate_part))
    later, up_part = lax.optimization_barrier((later, up_part))
    down_rows = sum_positions(
        after(
            dense_product("tf,df->td", active_all, down_here).astype(jnp.bfloat16), branch_back
        )
    )
    project_low = jnp.concatenate(
        [after(project_here, states_back), shrink_all, shrink_all], axis=1
    )
    weights_back = shares_back * inverse + divisor_back
    scores_back = jnp.where(window_mask, weights_back * exponent, 0.0).astype(jnp.bfloat16)
    similar_back = jnp.where(linear_mask, weights_back, 0.0).astype(jnp.bfloat16)
    size = head_width + 1
    prior_state = prior[:, :head_width]
    prior_rest = prior[:, size : size + head_width]
    prior_norm = prior[:, head_width].astype(jnp.float32) + prior[:, size + head_width].astype(
        jnp.float32
    )
    query_features_back = (
        (
            dense_product("nthd,ndf->nthf", heads_back, prior_state)
            + dense_product("nthd,ndf->nthf", heads_back, prior_rest)
        )
        * inverse
        + divisor_back * prior_norm[:, None, None, :]
        + dense_product("nthb,nbf->nthf", similar_back, features_window)
    )
    features_window_back = dense_product("nthb,nthf->nbf", similar_back, query_features)
    queries_back = dense_product("nthb,nbd->nthd", scores_back, keys_window) * scale
    keys_window_back = dense_product("nthb,nthd->nbd", scores_back, query_rows) * scale
    halved_one = values_one.reshape(2 * blocks, rows // 2, head_width + 1)
    features_lead_back = dense_product(
        "nbk,nkf->nbf", jnp.concatenate([halved_one, halved_one], axis=-1), later
    ).reshape(blocks, rows, -1)
    values_lead_back = dense_product(
        "nbf,nkf->nbk", key_features.reshape(2 * blocks, rows // 2, -1), later
    )
    values_lead_back = folded(values_lead_back)[..., :head_width].reshape(blocks, rows, -1)
    window_back = jnp.concatenate(
        [keys_window_back, values_window_back, features_window_back], axis=-1
    ).reshape(micro, PLANE, WIN + rows, -1)
    arriving = from_block_behind(window_back[:, 0, :WIN].astype(jnp.bfloat16))
    following = jnp.concatenate(
        [window_back[:, 1:, :WIN], arriving[:, None].astype(jnp.float32)], axis=1
    )
    carried_back = jnp.concatenate(
        [window_back[:, :, WIN:rows], window_back[:, :, rows:] + following], axis=2
    ).reshape(blocks, rows, -1)
    keys_back = carried_back[..., :head_width]
    values_back = carried_back[..., head_width : 2 * head_width] + values_lead_back
    down_part = narrowed(after(down_sum, up_part))
    carried_back, down_part, down_rows = lax.optimization_barrier(
        (carried_back, down_part, down_rows)
    )
    key_logits_back = both_softmax_back(
        key_plus, key_minus, carried_back[..., 2 * head_width :] + features_lead_back
    ).astype(jnp.bfloat16)
    query_logits_back = both_softmax_back(query_plus, query_minus, query_features_back).astype(
        jnp.bfloat16
    )
    key_feature_delta = dense_product("ntd,nte->de", key_rows, key_logits_back)
    query_feature_delta = dense_product("nthd,nthe->hde", query_rows, query_logits_back)
    keys_back = keys_back + dense_product("nte,de->ntd", key_logits_back, key_map)
    queries_back = queries_back + dense_product("nthe,hde->nthd", query_logits_back, query_map)
    projected_back = jnp.concatenate(
        [
            apply_rotation(queries_back, cosine_table[:, :, None], -sine_table[:, :, None])
            .astype(jnp.bfloat16)
            .reshape(blocks * rows, query_width),
            apply_rotation(keys_back, cosine_table, -sine_table)
            .astype(jnp.bfloat16)
            .reshape(blocks * rows, head_width),
            values_back.astype(jnp.bfloat16).reshape(blocks * rows, head_width),
        ],
        axis=-1,
    )
    projected_back, out_delta = lax.optimization_barrier((projected_back, out_delta))
    gate_delta, up_delta, down_delta = deal_back((gate_part, up_part, down_part), width // chips)
    lift_all = dense_product("tk,rk->tr", projected_back, expand_twice)
    back_low = jnp.concatenate([projected_back, halves(lift_all)], axis=1)
    normed_back = dense_product("tk,ck->tc", back_low, project_low)
    normed_back, gate_delta, up_delta, down_delta = lax.optimization_barrier(
        (normed_back, gate_delta, up_delta, down_delta)
    )
    normed_pair = sum_cores(normed_back.reshape(micro, PLANE, rows, width))
    project_full = after(dense_product("tc,tk->ck", normed_flat, back_low), normed_pair)
    project_delta, shrink_delta = return_heads(
        jnp.concatenate([project_full[:, :joined], folded(project_full[:, joined:])], axis=1),
        joined,
    )
    expand_delta = dense_product("tr,tk->rk", shrunk_parts, projected_back)
    expand_delta = ADAPTER_SCALE * (expand_delta[: 3 * rank] + expand_delta[3 * rank :])
    in_norm_back = sum_plane(normed_pair)
    down_rows, middle_late, in_norm_back = lax.optimization_barrier(
        (down_rows, middle, in_norm_back)
    )
    results = middle_late + from_relative(down_rows).astype(jnp.float32)
    attn_gain_delta = jnp.sum(in_norm_back * rows_in * scale_in, axis=(0, 1))
    inputs_back = middle_back.reshape(micro, piece, width) + norm_back(
        in_norm_back, rows_in, scale_in, gain_in
    )
    split, shared, gain_totals, (gate_delta, up_delta, down_delta) = total_heads(
        (
            expand_delta[:rank, :query_width],
            expand_delta[rank : 2 * rank, query_width : query_width + head_width],
            expand_delta[2 * rank :, query_width + head_width :],
            out_shrink_delta,
            query_feature_delta,
            key_feature_delta,
        ),
        (shrink_delta, output_second_delta),
        jnp.concatenate([attn_gain_delta, mlp_gain_delta]),
        (gate_delta, up_delta, down_delta),
    )
    shrink_total = shared[0].swapaxes(1, 2).reshape(width, 3 * rank)
    return (
        results.astype(jnp.bfloat16).reshape(micro, piece, width),
        inputs_back,
        gain_totals[:width],
        project_delta[:, :, :query_width].reshape(-1, PLANE * query_width),
        project_delta[:, :, query_width : query_width + head_width].reshape(
            -1, PLANE * head_width
        ),
        project_delta[:, :, query_width + head_width :].reshape(-1, PLANE * head_width),
        out_delta.reshape(-1, PLANE * query_width),
        shrink_total[:, :rank],
        along_columns(split[0]),
        shrink_total[:, rank : 2 * rank],
        along_columns(split[1]),
        shrink_total[:, 2 * rank :],
        along_columns(split[2]),
        split[3].reshape(-1, rank),
        shared[1].swapaxes(0, 1).reshape(rank, width),
        split[4].reshape(-1, head_width, head_width),
        split[5].reshape(-1, head_width, head_width),
        gain_totals[width:],
        gate_delta,
        up_delta,
        down_delta,
    )


def solution(mesh):
    return jax.shard_map(
        per_device,
        mesh=mesh,
        in_specs=(
            P(None, ("seq", "tp"), None),
            P(None, ("seq", "tp"), None),
            P(),
            P("seq", "tp"),
            P("seq", "tp"),
            P("seq", "tp"),
            P("seq", "tp"),
            P(),
            P(None, "tp"),
            P(),
            P(None, "tp"),
            P(),
            P(None, "tp"),
            P("tp", None),
            P(),
            P("tp", None, None),
            P("tp", None, None),
            P(),
            P("seq", "tp"),
            P("seq", "tp"),
            P("seq", "tp"),
        ),
        out_specs=(
            P(None, ("seq", "tp"), None),
            P(None, ("seq", "tp"), None),
            P(),
            P("seq", "tp"),
            P("seq", "tp"),
            P("seq", "tp"),
            P("seq", "tp"),
            P(),
            P(),
            P(),
            P(),
            P(),
            P(),
            P(),
            P(),
            P(),
            P(),
            P(),
            P("seq", "tp"),
            P("seq", "tp"),
            P("seq", "tp"),
        ),
        check_vma=False,
    )
```
